32 devices in a mesh: row: 8 (over z, core), col: 4 (over y, x).
Axes of the slice: x: 2, y: 2, z: 4, core: 2. Of those that a mesh axis runs over, the one named last changes fastest.
Arguments:
- amplitudes: float32 [8, 4, 2, 65536], P('row', 'col'), may hold values from -6 to 6
- gate_real: float32 [2, 3, 128, 128], replicated, may hold values from -0.375 to 0.375
- gate_imag: float32 [2, 3, 128, 128], replicated, may hold values from -0.375 to 0.375
- gate_qubits: int32 [2, 3, 9], replicated, may hold values from 0 to 8, each once within a row
- swap_qubits: int32 [2, 9], replicated, may hold values from 0 to 8, each once within a row
Outputs:
- evolved: float32 [8, 4, 2, 65536], P('row', 'col')
The draws below stay inside these ranges and needn't reach their ends.
Inputs may be any that keep to these rules, and one draw needn't show every extreme that they name: `gate_qubits`: each row is an ordering of 0 to 8; a gate acts on local qubits 7 + its first 7 entries, entry j giving bit j of the gate index. `swap_qubits`: each row is an ordering of 0 to 8; in a round on an axis with k index bits, local qubit 7 + entry j for j < k is swapped with bit j of that axis's index.
All inputs are finite; a program needn't handle non-finite values.
Results may differ from the reference program's by a relative error of at most 0.0001.
Values sent between devices are 32-bit elements; how exact they have to be, the bound alone decides.
No kernel may reach another device: no remote copies, remote signals or barrier semaphores. Data moves between devices by JAX's collectives and lax.ppermute only.
A program may use at most 64 MiB of HBM per device.

```python
import jax
import jax.numpy as jnp
from jax import lax

GQ = 7
ROUNDS = 2
GATES = 3
GDIM = 128
HQ = 9
LOCAL = 65536
N_ROW = 8
N_COL = 4


def shard_levels(rng, dims, shards, low, top_value):
    loudness = 1.0
    for dim, shards_of in shards:
        draws = jax.random.uniform(jax.random.fold_in(jax.random.fold_in(rng, 6), dim), (shards_of,), jnp.float32, low / len(shards), top_value / len(shards))
        loudness = loudness * jnp.repeat(jnp.exp(draws), dims[dim] // shards_of).reshape((-1,) + (1,) * (len(dims) - 1 - dim))
    return loudness


def normal_values(rng, shape, scale, limit, cuts=(), kind=jnp.bfloat16):
    array = jax.random.normal(rng, shape, jnp.float32) * scale
    if len(cuts) > 0:
        array = shard_levels(rng, shape, cuts, -0.22, 0.18) * array
    return jnp.clip(array, min=-limit, max=limit).astype(kind)


def setup_inputs(seed: int = 0) -> dict:
    splits = jax.random.split(jax.random.key(seed), 6)
    return {
        "amplitudes": normal_values(splits[0], (N_ROW, N_COL, 2, LOCAL), 1.0, 6.0, ((0, 8), (1, 4)), jnp.float32),
        "gate_real": normal_values(splits[1], (ROUNDS, GATES, GDIM, GDIM), (2 * GDIM) ** -0.5, 0.375, (), jnp.float32),
        "gate_imag": normal_values(splits[2], (ROUNDS, GATES, GDIM, GDIM), (2 * GDIM) ** -0.5, 0.375, (), jnp.float32),
        "gate_qubits": jax.vmap(lambda own: jax.random.permutation(own, HQ))(jax.random.split(splits[3], ROUNDS * GATES)).reshape((ROUNDS, GATES, HQ)).astype(jnp.int32),
        "swap_qubits": jax.vmap(lambda own: jax.random.permutation(own, HQ))(jax.random.split(splits[4], ROUNDS)).reshape((ROUNDS, HQ)).astype(jnp.int32),
    }


def spread_bits(dest, total_bits):
    low_count = total_bits // 2
    high_count = total_bits - low_count

    def table(count, offset):
        position = jnp.arange(2 ** count, dtype=jnp.int32)
        result = jnp.zeros_like(position)
        for bit_index in range(count):
            result = result + jnp.left_shift((position >> bit_index) & 1, dest[offset + bit_index])
        return result

    low_table = table(low_count, 0)
    high_table = table(high_count, low_count)
    return (high_table[:, None] + low_table[None, :]).reshape(-1).astype(jnp.int32)


def qubit_maps(chosen, top_count, total_bits):
    qubits = jnp.arange(total_bits, dtype=jnp.int32)
    picked = chosen[:top_count].astype(jnp.int32)
    matches = picked[:, None] == qubits[None, :]
    chosen_mask = jnp.any(matches, axis=0)
    slot_top = jnp.sum(jnp.where(matches, jnp.arange(top_count, dtype=jnp.int32)[:, None], 0), axis=0).astype(jnp.int32)
    unchosen = jnp.where(chosen_mask, 0, 1).astype(jnp.int32)
    rest_rank = (jnp.cumsum(unchosen) - unchosen).astype(jnp.int32)
    ordering = jnp.argsort(jnp.where(chosen_mask, total_bits + qubits, qubits)).astype(jnp.int32)
    low_bits = total_bits - top_count
    forward_dest = jnp.concatenate([ordering[:low_bits], picked]).astype(jnp.int32)
    backward_dest = jnp.where(chosen_mask, low_bits + slot_top, rest_rank).astype(jnp.int32)
    return spread_bits(forward_dest, total_bits), spread_bits(backward_dest, total_bits)


def apply_gate(current, real_part, imag_part, chosen):
    local_size = current.shape[-1]
    total_bits = local_size.bit_length() - 1
    gate_size = real_part.shape[0]
    forward, backward = qubit_maps(chosen, gate_size.bit_length() - 1, total_bits)
    leading = current.shape[:-2]
    gathered = jnp.take(current, forward, axis=-1).reshape(leading + (2 * gate_size, local_size // gate_size))
    operator = jnp.concatenate([jnp.concatenate([real_part, -imag_part], 1), jnp.concatenate([imag_part, real_part], 1)], 0)
    applied = jnp.einsum("ij,abjk->abik", operator, gathered, precision=lax.Precision.HIGHEST)
    return jnp.take(applied.reshape(leading + (2, local_size)), backward, axis=-1)


def swap_layer(current, gate_size):
    local_size = current.shape[-1]
    leading = current.shape[:-1]
    shaped = current.reshape(leading + (local_size // (gate_size * gate_size), gate_size, gate_size))
    return jnp.swapaxes(shaped, -1, -2).reshape(current.shape)


def swap_axis(current, chosen, axis_pos):
    local_size = current.shape[-1]
    total_bits = local_size.bit_length() - 1
    devices = current.shape[axis_pos]
    forward, backward = qubit_maps(chosen, devices.bit_length() - 1, total_bits)
    gathered = jnp.take(current, forward, axis=-1)
    shaped = gathered.reshape(current.shape[:-1] + (devices, local_size // devices))
    shaped = jnp.swapaxes(shaped, axis_pos, 3).reshape(current.shape)
    return jnp.take(shaped, backward, axis=-1)


def reference(amplitudes, gate_real, gate_imag, gate_qubits, swap_qubits):
    current = amplitudes
    gate_size = gate_real.shape[-1]
    for round_index in range(ROUNDS):
        for gate_index in range(GATES):
            targets = (gate_qubits[round_index, gate_index] + GQ).astype(jnp.int32)
            current = apply_gate(current, gate_real[round_index, gate_index], gate_imag[round_index, gate_index], targets)
            current = swap_layer(current, gate_size)
        swapped = (swap_qubits[round_index] + GQ).astype(jnp.int32)
        current = swap_axis(current, swapped, round_index % 2)
    return current
```

```python
import functools

import jax
import jax.numpy as jnp
from jax import lax
from jax.experimental import pallas as pl
from jax.experimental.pallas import tpu as pltpu
from jax.sharding import PartitionSpec as P


def spread_bits(dest, total_bits):
    low_count = total_bits // 2
    high_count = total_bits - low_count

    def table(count, offset):
        position = jnp.arange(2**count, dtype=jnp.int32)
        result = jnp.zeros_like(position)
        for bit_index in range(count):
            result = result + jnp.left_shift(position >> bit_index & 1, dest[offset + bit_index])
        return result

    low_table = table(low_count, 0)
    high_table = table(high_count, low_count)
    return (high_table[:, None] + low_table[None, :]).reshape(-1)


def qubit_maps(chosen, top_count, total_bits):
    qubits = jnp.arange(total_bits, dtype=jnp.int32)
    picked = chosen[:top_count]
    matches = picked[:, None] == qubits[None, :]
    chosen_mask = jnp.any(matches, axis=0)
    slot_top = jnp.sum(
        jnp.where(matches, jnp.arange(top_count, dtype=jnp.int32)[:, None], 0), axis=0
    )
    unchosen = jnp.where(chosen_mask, 0, 1).astype(jnp.int32)
    rest_rank = jnp.cumsum(unchosen) - unchosen
    ordering = jnp.argsort(jnp.where(chosen_mask, total_bits + qubits, qubits))
    low_bits = total_bits - top_count
    forward_dest = jnp.concatenate([ordering[:low_bits], picked])
    backward_dest = jnp.where(chosen_mask, low_bits + slot_top, rest_rank)
    return (spread_bits(forward_dest, total_bits), spread_bits(backward_dest, total_bits))


def per_device(amplitudes, gate_real, gate_imag, gate_qubits, swap_qubits):
    local_size = amplitudes.shape[-1]
    total_bits = local_size.bit_length() - 1
    gate_size = gate_real.shape[-1]
    gate_bits = gate_size.bit_length() - 1
    high_bits = total_bits - gate_bits
    row_count = local_size // gate_size
    current = amplitudes.reshape(2, row_count, gate_size)
    for round_index in range(gate_real.shape[0]):
        for gate_index in range(gate_real.shape[1]):
            forward, backward = qubit_maps(
                gate_qubits[round_index, gate_index], gate_bits, high_bits
            )
            gathered = jnp.take(current, forward, axis=1, mode="clip").reshape(
                2 * gate_size, local_size // gate_size
            )
            real_part = gate_real[round_index, gate_index]
            imag_part = gate_imag[round_index, gate_index]
            operator = jnp.concatenate(
                [
                    jnp.concatenate([real_part, -imag_part], 1),
                    jnp.concatenate([imag_part, real_part], 1),
                ],
                0,
            )
            applied = jnp.dot(
                operator,
                gathered,
                precision=lax.Precision.HIGHEST,
                preferred_element_type=jnp.float32,
            ).reshape(2, row_count, gate_size)
            current = jnp.take(applied, backward, axis=1, mode="clip")
            current = (
                current.reshape(2, row_count // gate_size, gate_size, gate_size)
                .transpose(0, 1, 3, 2)
                .reshape(2, row_count, gate_size)
            )
        if round_index % 2 == 0:
            devices = lax.axis_size("row")
            forward, backward = qubit_maps(
                swap_qubits[round_index], devices.bit_length() - 1, high_bits
            )
            prepared = jnp.take(current, forward, axis=1, mode="clip").reshape(
                2, devices, local_size // devices
            )
            arrived = lax.all_to_all(prepared, "row", split_axis=1, concat_axis=1, tiled=True)
        else:
            devices = lax.axis_size("col")
            forward, backward = qubit_maps(
                swap_qubits[round_index], devices.bit_length() - 1, high_bits
            )
            prepared = jnp.take(current, forward, axis=1, mode="clip").reshape(
                2, devices, local_size // devices
            )
            arrived = lax.all_to_all(prepared, "col", split_axis=1, concat_axis=1, tiled=True)
        current = jnp.take(arrived.reshape(2, row_count, gate_size), backward, axis=1, mode="clip")
    return current.reshape(amplitudes.shape)


SUB = 3
TOP = 6


def combos(weights):
    sums = [jnp.int32(0)]
    for weight in weights:
        sums = sums + [total + weight for total in sums]
    return sums


def where(cond, yes, no):
    return jnp.where(cond, jnp.int32(yes), jnp.int32(no))


def excluded(gates, spot, bits):
    one, two = gates[spot + (bits,)], gates[spot + (bits + 1,)]
    first = where((one == bits) | (two == bits), bits, jnp.where(one == bits + 1, two, one))
    second = where((one == bits + 1) | (two == bits + 1), bits + 1, jnp.where(two == bits, one, two))
    return first, second


def row_order(gates, spot, bits, maps, area, first, second, moved):
    order = []
    filled = jnp.int32(0)
    for j in range(bits):
        target = gates[spot + (j,)]
        last = jnp.where((filled == bits - 2) & (moved[0] == 0), bits - 2, bits - 1)
        free = jnp.where(filled < bits - 2, filled, last)
        place = jnp.where(target == bits, bits - 2, jnp.where(target == bits + 1, bits - 1, free))
        filled = filled + where(target < bits, 1, 0)
        maps[area, target] = place
        order.append(place)
    maps[area, first] = jnp.int32(bits - 2)
    maps[area, second] = jnp.int32(bits - 1)
    return order


IN, LANES, ROWS_A, ROWS_B, ROWS_C, PLACE, POS = range(7)


def start_maps(maps, bits):
    for area in range(7):
        for q in range(bits + 2):
            maps[area, q] = jnp.int32(q)


def make_plan(index, gates, swaps, count, maps, bits):
    plan = {}
    high = bits + 2
    spot = (index, 0)
    first, second = excluded(gates, spot, bits)
    moved = [where(first != bits, 1, 0), where(second != bits + 1, 1, 0)]
    p0, p1 = maps[IN, first], maps[IN, second]
    low0, low1 = p0 < SUB, p1 < SUB
    s0 = jnp.where(
        low0,
        jnp.where(low1 | (p1 != bits), p0, -1),
        jnp.where(low1 & (p0 != bits), p1, -1),
    )
    s1 = jnp.where(
        low0,
        jnp.where(low1, p1, jnp.where(p1 == bits, p0, -1)),
        jnp.where(low1 & (p0 == bits), p1, -1),
    )
    plan["stage"] = [s0, s1]
    for q in range(high):
        p = maps[IN, q]
        p = jnp.where(p == s0, bits, jnp.where((p == bits) & (s0 >= 0), s0, p))
        p = jnp.where(p == s1, bits + 1, jnp.where((p == bits + 1) & (s1 >= 0), s1, p))
        maps[POS, q] = p
    e0, e1 = maps[POS, first], maps[POS, second]
    lower, upper = jnp.minimum(e0, e1) - SUB, jnp.maximum(e0, e1) - SUB
    plan["kept"] = []
    for j in range(TOP - 2):
        j = j + where(j >= lower, 1, 0)
        j = j + where(j >= upper, 1, 0)
        plan["kept"].append(jnp.left_shift(jnp.int32(1), j))
    plan["away"] = [jnp.left_shift(jnp.int32(1), e0 - SUB), jnp.left_shift(jnp.int32(1), e1 - SUB)]
    columns = []
    for j in range(bits):
        p = maps[POS, gates[spot + (j,)]]
        columns.append(p - where(e0 < p, 1, 0) - where(e1 < p, 1, 0))
    plan["columns0"] = columns
    plan["order0"] = row_order(gates, spot, bits, maps, ROWS_A, first, second, moved)
    plan["moved0"] = moved
    for gate, (lanes, rows) in enumerate(((LANES, ROWS_B), (ROWS_A, ROWS_C)), 1):
        spot = (index, gate)
        first, second = excluded(gates, spot, bits)
        moved = [where(first != bits, 1, 0), where(second != bits + 1, 1, 0)]
        l0 = jnp.where(moved[0] == 1, maps[lanes, first], 0)
        l1 = jnp.where(moved[1] == 1, maps[lanes, second], 0)
        maps[lanes, bits] = l0
        maps[lanes, bits + 1] = l1
        plan[f"lanes{gate}"] = [l0, l1]
        plan[f"columns{gate}"] = [maps[lanes, gates[spot + (j,)]] for j in range(bits)]
        plan[f"order{gate}"] = row_order(gates, spot, bits, maps, rows, first, second, moved)
        plan[f"moved{gate}"] = moved
    sent = [swaps[index, j] for j in range(count)]
    mask, taken = jnp.int32(0), jnp.int32(0)
    for j, s in enumerate(sent):
        mask = mask | jnp.left_shift(jnp.int32(1), s)
        taken = taken | where(s < bits, 1 << (bits - 1 - j), 0)
    for q in range(SUB):
        taken = taken | where((mask >> q) & 1 == 1, 0, 1 << q)
        maps[PLACE, q] = jnp.int32(q)
    for j, s in enumerate(sent):
        maps[PLACE, s] = jnp.int32(bits - 1 - j)
    for q in range(SUB, bits):
        chosen = (mask >> q) & 1
        lowest = ~taken & (taken + 1)
        place = jnp.int32(0)
        for b in range(1, bits):
            place = place + b * ((lowest >> b) & 1)
        maps[PLACE, q] = jnp.where(chosen == 1, maps[PLACE, q], place)
        taken = jnp.where(chosen == 1, taken, taken | lowest)
    maps[PLACE, bits] = jnp.int32(bits)
    maps[PLACE, bits + 1] = jnp.int32(bits + 1)
    places = [maps[PLACE, s] for s in sent]
    plan["device"] = [jnp.left_shift(jnp.int32(1), p - SUB) for p in places]
    rest = jnp.int32(2**TOP - 1)
    for weight in plan["device"]:
        rest = rest & ~weight
    plan["slot"] = []
    for _ in range(TOP - count):
        lowest = rest & -rest
        plan["slot"].append(lowest)
        rest = rest & ~lowest
    plan["lane_from"] = [maps[ROWS_B, q] for q in range(bits)]
    plan["lane_to"] = [maps[PLACE, q] for q in range(bits)]
    plan["low_from"] = [maps[ROWS_C, q] for q in range(bits)]
    for q in range(high):
        p = maps[PLACE, q]
        for place in places:
            p = p - where(place < maps[PLACE, q], 1, 0)
        maps[IN, q] = p
    for j, s in enumerate(sent):
        maps[IN, s] = jnp.int32(high - count + j)
    for q in range(bits):
        maps[LANES, q] = maps[ROWS_C, q]
    plan["last_stage"] = [jnp.where(s < SUB, s, -1) for s in sent]
    plan["last"] = []
    for q in range(SUB, high):
        p = maps[IN, q]
        for j, s in enumerate(plan["last_stage"]):
            p = jnp.where(p == s, high - count + j, p)
        plan["last"].append(jnp.left_shift(jnp.int32(1), p - SUB))
    return plan


KEYS = ("stage", "kept", "away", "moved0", "moved1", "moved2", "lanes1", "lanes2", "device", "slot")
KEYS = KEYS + ("lane_from", "lane_to", "low_from", "last_stage", "last")


def plan_sizes(count, bits):
    sizes = (2, TOP - 2, 2, 2, 2, 2, 2, 2, count, TOP - count, bits, bits, bits, count, TOP)
    return dict(zip(KEYS, sizes))


def write_plan(plan, ref):
    at = 0
    for key in KEYS:
        for value in plan[key]:
            ref[at] = value
            at += 1


def read_plan(ref, count, bits):
    plan, at = {}, 0
    for key, size in plan_sizes(count, bits).items():
        plan[key] = [ref[at + j] for j in range(size)]
        at += size
    return plan


def spread(position, sources, dests):
    total = jnp.zeros_like(position)
    for source, dest in zip(sources, dests):
        total = total | (((position >> source) & 1) << dest)
    return total


def split(value):
    top = value.astype(jnp.bfloat16)
    return top, (value - top.astype(jnp.float32)).astype(jnp.bfloat16)


def prepare_gate(plan, gate, real, imag, out):
    size = real.shape[0]
    bits = size.bit_length() - 1
    lane = lax.broadcasted_iota(jnp.int32, (8, size), 1)
    columns = spread(lane, plan[f"columns{gate}"], range(bits))
    columns = jnp.broadcast_to(columns[0:1, :], (size, size))
    row = lax.broadcasted_iota(jnp.int32, (size, size), 0)
    column = lax.broadcasted_iota(jnp.int32, (size, size), 1)
    chosen = spread(row, plan[f"order{gate}"], range(bits)) == column
    chosen = jnp.where(chosen, 1.0, 0.0).astype(jnp.bfloat16)
    parts = []
    for part in (real, imag):
        parts += split(jnp.take_along_axis(part, columns, axis=1))
    moved = jnp.dot(chosen, jnp.concatenate(parts, axis=1), preferred_element_type=jnp.float32)
    moved = moved.astype(jnp.bfloat16)
    re_hi, re_lo, im_hi, im_lo = (moved[:, j * size : (j + 1) * size] for j in range(4))
    for at, re, im in ((0, re_hi, im_hi), (2 * size, re_hi, im_hi), (4 * size, re_lo, im_lo)):
        out[gate, 0:size, at : at + size] = re
        out[gate, 0:size, at + size : at + 2 * size] = -im
        out[gate, size : 2 * size, at : at + size] = im
        out[gate, size : 2 * size, at + size : at + 2 * size] = re


def trade(v0, v1, low, keep0, keep1, index, axis):
    crossed = jnp.take_along_axis(jnp.where(low, v1, v0), index, axis=axis)
    return jnp.where(keep0, v0, crossed), jnp.where(keep1, v1, crossed)


def trade_masks(shape, axis, bit, moved):
    position = lax.broadcasted_iota(jnp.int32, shape, axis)
    value = (position >> bit) & 1
    low = value == 0
    return low, (value & moved) == 0, ((1 - value) & moved) == 0, position ^ jnp.left_shift(jnp.int32(1), bit)


def sublane_stage(state, vreg_bit, bit):
    @pl.when(bit >= 0)
    def _():
        masks = trade_masks(state.shape[2:], 0, jnp.maximum(bit, 0), 1)
        for part in range(state.shape[0]):
            for v in range(state.shape[1]):
                if (v >> vreg_bit) & 1 == 0:
                    w = v | 1 << vreg_bit
                    state[part, v], state[part, w] = trade(state[part, v], state[part, w], *masks, 0)


def block_rows(moved, size):
    a, b = 2 * size, size // 4
    d = []
    for i in range(2):
        d.append([[where(moved[i] == 1, f * a + h * b, h * a + f * b) << i for f in range(2)] for h in range(2)])
    return lambda h, f: d[0][h & 1][f & 1] + d[1][h >> 1][f >> 1]


def multiply(product, left, right, contract):
    size = left.shape[0] // 2
    out = lax.dot_general(left, right, (((1,), (contract,)), ((), ())), preferred_element_type=jnp.float32)
    for a in range(4):
        for part in range(2):
            at = a * 2 * size + part * size
            product[at : at + size, :] = out[part * size : (part + 1) * size, a * size : (a + 1) * size]


def run_round(plan, state, weights, by_row, by_lane, product, canonical):
    size = state.shape[-1]
    bits = size.bit_length() - 1
    for j in range(2):
        sublane_stage(state, TOP - 2 + j, plan["stage"][j])
    away, kept = combos(plan["away"]), combos(plan["kept"])
    for part in range(2):
        for a in range(4):
            for m in range(len(kept) // 2):
                pair = [state[part, away[a] + kept[2 * m + j]] for j in range(2)]
                high, low = split(jnp.concatenate(pair, axis=0))
                at = part * size + 16 * m
                for row, value in ((at, high), (2 * size + at, low), (4 * size + at, high)):
                    by_row[row : row + 16, a * size : (a + 1) * size] = value
    multiply(product, weights[0], by_row[...], 0)
    rows = block_rows(plan["moved0"], size)
    for gate in (1, 2):
        masks = [
            trade_masks((16, size), 1, plan[f"lanes{gate}"][j], plan[f"moved{gate}"][j]) for j in range(2)
        ]
        for part in range(2):
            for f in range(4):
                for m in range(size // 64):
                    v = []
                    for h in range(4):
                        at = pl.multiple_of(rows(h, f) + (part * size + 16 * m), 16)
                        v.append(product[pl.ds(at, 16), :])
                    v[0], v[1] = trade(v[0], v[1], *masks[0], 1)
                    v[2], v[3] = trade(v[2], v[3], *masks[0], 1)
                    v[0], v[2] = trade(v[0], v[2], *masks[1], 1)
                    v[1], v[3] = trade(v[1], v[3], *masks[1], 1)
                    for a in range(4):
                        high, low = split(v[a])
                        at = a * size + f * (size // 4) + 16 * m
                        for column, value in ((0, high), (2, low), (4, high)):
                            column = (column + part) * size
                            by_lane[at : at + 16, column : column + size] = value
        multiply(product, weights[gate], by_lane[...], 1)
        rows = block_rows(plan[f"moved{gate}"], size)
    lane = lax.broadcasted_iota(jnp.int32, (8, size), 1)
    order = spread(lane, plan["lane_to"], plan["lane_from"])
    order = jnp.broadcast_to(order[0:1, :], (size, size))
    natural = spread(lane, range(bits), plan["low_from"])
    natural = jnp.broadcast_to(natural[0:1, :], (size, size))
    for part in range(2):
        for h in range(4):
            blocks = []
            for f in range(4):
                at = pl.multiple_of(rows(h, f) + part * size, 32)
                blocks.append(product[pl.ds(at, size // 4), :])
            block = jnp.take_along_axis(jnp.concatenate(blocks, axis=0), order, axis=1).T
            if canonical:
                block = jnp.take_along_axis(block, natural, axis=1)
            state[part, h * (size // 8) : (h + 1) * (size // 8)] = block.reshape(size // 8, 8, size)


def send_chunks(plan, state, me, outs):
    slots = combos(plan["slot"])
    for offset, out in enumerate(outs):
        device = me ^ offset
        base = jnp.int32(0)
        for j, weight in enumerate(plan["device"]):
            base = base + ((device >> j) & 1) * weight
        for part in range(2):
            for j, slot in enumerate(slots):
                at = (part * len(slots) + j) * 8
                out[at : at + 8, :] = state[part, base + slot]


def take_chunks(state, me, chunks):
    slots = state.shape[1] // len(chunks)
    for offset, chunk in enumerate(chunks):
        device = me ^ offset
        for part in range(2):
            block = chunk[part * slots * 8 : (part + 1) * slots * 8, :]
            state[part, pl.ds(device * slots, slots)] = block.reshape(slots, 8, state.shape[-1])


def first_kernel(axis, count, gates, swaps, amps, real, imag, *rest):
    devices = 2**count
    outs = rest[:devices]
    maps, raw, re, im, weights, state, by_row, by_lane, product, sems = rest[devices:]
    copies = [
        pltpu.make_async_copy(source, dest, sems.at[j])
        for j, (source, dest) in enumerate(((real.at[0], re), (imag.at[0], im), (amps, raw)))
    ]
    for copy in copies:
        copy.start()
    bits = state.shape[-1].bit_length() - 1
    start_maps(maps, bits)
    plan = make_plan(0, gates, swaps, count, maps, bits)
    copies[0].wait()
    copies[1].wait()
    for gate in range(3):
        prepare_gate(plan, gate, re[gate], im[gate], weights)
    copies[2].wait()
    for part in range(2):
        for v in range(state.shape[1]):
            state[part, v] = raw[pl.ds(16 * v + part, 8, stride=2), :]
    run_round(plan, state, weights, by_row, by_lane, product, False)
    send_chunks(plan, state, lax.axis_index(axis), outs)


def plan_kernel(counts, gates, swaps, real, imag, plan_out, weights, maps, re, im, sems):
    copies = [
        pltpu.make_async_copy(source, dest, sems.at[j])
        for j, (source, dest) in enumerate(((real.at[1], re), (imag.at[1], im)))
    ]
    for copy in copies:
        copy.start()
    bits = re.shape[-1].bit_length() - 1
    start_maps(maps, bits)
    make_plan(0, gates, swaps, counts[0], maps, bits)
    plan = make_plan(1, gates, swaps, counts[1], maps, bits)
    write_plan(plan, plan_out)
    for copy in copies:
        copy.wait()
    for gate in range(3):
        prepare_gate(plan, gate, re[gate], im[gate], weights)


def second_kernel(axes, counts, plan_ref, weights, *rest):
    chunks, rest = rest[: 2 ** counts[0]], rest[2 ** counts[0] :]
    outs, rest = rest[: 2 ** counts[1]], rest[2 ** counts[1] :]
    state, by_row, by_lane, product = rest
    plan = read_plan(plan_ref, counts[1], state.shape[-1].bit_length() - 1)
    take_chunks(state, lax.axis_index(axes[0]), chunks)
    run_round(plan, state, weights, by_row, by_lane, product, True)
    send_chunks(plan, state, lax.axis_index(axes[1]), outs)


def last_kernel(axis, count, plan_ref, *rest):
    chunks, (out, state) = rest[: 2**count], rest[2**count :]
    plan = read_plan(plan_ref, count, state.shape[-1].bit_length() - 1)
    take_chunks(state, lax.axis_index(axis), chunks)
    for j in range(count):
        sublane_stage(state, TOP - count + j, plan["last_stage"][j])
    for part in range(2):
        for v, source in enumerate(combos(plan["last"])):
            out[pl.ds(16 * v + part, 8, stride=2), :] = state[part, source]


def exchange(chunks, axis):
    devices = len(chunks)
    moved = [chunks[0]]
    for offset in range(1, devices):
        pairs = [(d, d ^ offset) for d in range(devices)]
        moved.append(lax.ppermute(chunks[offset], axis, pairs))
    return moved


def fused(axes, counts, amplitudes, gate_real, gate_imag, gate_qubits, swap_qubits):
    size = gate_real.shape[-1]
    rows = amplitudes.shape[-1] // size
    amps = amplitudes.reshape(2, rows, size).transpose(1, 0, 2).reshape(2 * rows, size)
    f32, bf16, i32 = jnp.float32, jnp.bfloat16, jnp.int32
    smem = pl.BlockSpec(memory_space=pltpu.SMEM)
    vmem = pl.BlockSpec(memory_space=pltpu.VMEM)
    hbm = pl.BlockSpec(memory_space=pl.ANY)
    maps = pltpu.SMEM((8, 16), i32)
    gate = pltpu.VMEM(gate_real.shape[1:], f32)
    operators = (gate_real.shape[1], 2 * size, 6 * size)
    state = pltpu.VMEM((2, rows // 8, 8, size), f32)
    work = [
        state,
        pltpu.VMEM((6 * size, rows), bf16),
        pltpu.VMEM((rows, 6 * size), bf16),
        pltpu.VMEM((2 * rows, size), f32),
    ]
    chunk = [jax.ShapeDtypeStruct((2 * rows >> count, size), f32) for count in counts]
    sent = pl.pallas_call(
        functools.partial(first_kernel, axes[0], counts[0]),
        out_shape=[chunk[0]] * 2 ** counts[0],
        in_specs=[smem, smem, hbm, hbm, hbm],
        out_specs=[vmem] * 2 ** counts[0],
        scratch_shapes=[maps, pltpu.VMEM(amps.shape, f32), gate, gate, pltpu.VMEM(operators, bf16), *work]
        + [pltpu.SemaphoreType.DMA((3,))],
        name="first_round",
    )(gate_qubits, swap_qubits, amps, gate_real, gate_imag)
    plan, weights = pl.pallas_call(
        functools.partial(plan_kernel, counts),
        out_shape=[
            jax.ShapeDtypeStruct((sum(plan_sizes(counts[1], size.bit_length() - 1).values()),), i32),
            jax.ShapeDtypeStruct(operators, bf16),
        ],
        in_specs=[smem, smem, hbm, hbm],
        out_specs=[smem, vmem],
        scratch_shapes=[maps, gate, gate, pltpu.SemaphoreType.DMA((2,))],
        name="second_plan",
    )(gate_qubits, swap_qubits, gate_real, gate_imag)
    arrived = exchange(sent, axes[0])
    sent = pl.pallas_call(
        functools.partial(second_kernel, axes, counts),
        out_shape=[chunk[1]] * 2 ** counts[1],
        in_specs=[smem, vmem] + [vmem] * len(arrived),
        out_specs=[vmem] * 2 ** counts[1],
        scratch_shapes=work,
        name="second_round",
    )(plan, weights, *arrived)
    arrived = exchange(sent, axes[1])
    out = pl.pallas_call(
        functools.partial(last_kernel, axes[1], counts[1]),
        out_shape=jax.ShapeDtypeStruct(amps.shape, f32),
        in_specs=[smem] + [vmem] * len(arrived),
        out_specs=vmem,
        scratch_shapes=[state],
        name="last_places",
    )(plan, *arrived)
    return out.reshape(rows, 2, size).transpose(1, 0, 2).reshape(amplitudes.shape)


def program(mesh, *arrays):
    axes = ("row", "col")
    counts = tuple(mesh.shape[axis].bit_length() - 1 for axis in axes)
    amplitudes, gate_real = arrays[:2]
    size = gate_real.shape[-1]
    rounds = gate_real.shape[0] == 2 and gate_real.shape[1] == 3
    known = size == 128 and amplitudes.shape[-1] == 4 * size * size
    if known and rounds and max(counts) <= 4:
        return fused(axes, counts, *arrays)
    return per_device(*arrays)


def solution(mesh):
    placed = (P("row", "col", None, None), P(), P(), P(), P())
    return jax.shard_map(
        functools.partial(program, mesh),
        mesh=mesh,
        in_specs=placed,
        out_specs=P("row", "col", None, None),
        check_vma=False,
    )
```

```python
import functools

import jax
import jax.numpy as jnp
from jax import lax
from jax.experimental import pallas as pl
from jax.experimental.pallas import tpu as pltpu
from jax.sharding import PartitionSpec as P


def spread_bits(dest, total_bits):
    low_count = total_bits // 2
    high_count = total_bits - low_count

    def table(count, offset):
        position = jnp.arange(2**count, dtype=jnp.int32)
        result = jnp.zeros_like(position)
        for bit_index in range(count):
            result = result + jnp.left_shift(position >> bit_index & 1, dest[offset + bit_index])
        return result

    low_table = table(low_count, 0)
    high_table = table(high_count, low_count)
    return (high_table[:, None] + low_table[None, :]).reshape(-1)


def qubit_maps(chosen, top_count, total_bits):
    qubits = jnp.arange(total_bits, dtype=jnp.int32)
    picked = chosen[:top_count]
    matches = picked[:, None] == qubits[None, :]
    chosen_mask = jnp.any(matches, axis=0)
    slot_top = jnp.sum(
        jnp.where(matches, jnp.arange(top_count, dtype=jnp.int32)[:, None], 0), axis=0
    )
    unchosen = jnp.where(chosen_mask, 0, 1).astype(jnp.int32)
    rest_rank = jnp.cumsum(unchosen) - unchosen
    ordering = jnp.argsort(jnp.where(chosen_mask, total_bits + qubits, qubits))
    low_bits = total_bits - top_count
    forward_dest = jnp.concatenate([ordering[:low_bits], picked])
    backward_dest = jnp.where(chosen_mask, low_bits + slot_top, rest_rank)
    return (spread_bits(forward_dest, total_bits), spread_bits(backward_dest, total_bits))


def per_device(amplitudes, gate_real, gate_imag, gate_qubits, swap_qubits):
    local_size = amplitudes.shape[-1]
    total_bits = local_size.bit_length() - 1
    gate_size = gate_real.shape[-1]
    gate_bits = gate_size.bit_length() - 1
    high_bits = total_bits - gate_bits
    row_count = local_size // gate_size
    current = amplitudes.reshape(2, row_count, gate_size)
    for round_index in range(gate_real.shape[0]):
        for gate_index in range(gate_real.shape[1]):
            forward, backward = qubit_maps(
                gate_qubits[round_index, gate_index], gate_bits, high_bits
            )
            gathered = jnp.take(current, forward, axis=1, mode="clip").reshape(
                2 * gate_size, local_size // gate_size
            )
            real_part = gate_real[round_index, gate_index]
            imag_part = gate_imag[round_index, gate_index]
            operator = jnp.concatenate(
                [
                    jnp.concatenate([real_part, -imag_part], 1),
                    jnp.concatenate([imag_part, real_part], 1),
                ],
                0,
            )
            applied = jnp.dot(
                operator,
                gathered,
                precision=lax.Precision.HIGHEST,
                preferred_element_type=jnp.float32,
            ).reshape(2, row_count, gate_size)
            current = jnp.take(applied, backward, axis=1, mode="clip")
            current = (
                current.reshape(2, row_count // gate_size, gate_size, gate_size)
                .transpose(0, 1, 3, 2)
                .reshape(2, row_count, gate_size)
            )
        if round_index % 2 == 0:
            devices = lax.axis_size("row")
            forward, backward = qubit_maps(
                swap_qubits[round_index], devices.bit_length() - 1, high_bits
            )
            prepared = jnp.take(current, forward, axis=1, mode="clip").reshape(
                2, devices, local_size // devices
            )
            arrived = lax.all_to_all(prepared, "row", split_axis=1, concat_axis=1, tiled=True)
        else:
            devices = lax.axis_size("col")
            forward, backward = qubit_maps(
                swap_qubits[round_index], devices.bit_length() - 1, high_bits
            )
            prepared = jnp.take(current, forward, axis=1, mode="clip").reshape(
                2, devices, local_size // devices
            )
            arrived = lax.all_to_all(prepared, "col", split_axis=1, concat_axis=1, tiled=True)
        current = jnp.take(arrived.reshape(2, row_count, gate_size), backward, axis=1, mode="clip")
    return current.reshape(amplitudes.shape)


SUB = 3
TOP = 6


def combos(weights):
    sums = [jnp.int32(0)]
    for weight in weights:
        sums = sums + [total + weight for total in sums]
    return sums


def where(cond, yes, no):
    return jnp.where(cond, jnp.int32(yes), jnp.int32(no))


def excluded(gates, spot, bits):
    one, two = gates[spot + (bits,)], gates[spot + (bits + 1,)]
    first = where((one == bits) | (two == bits), bits, jnp.where(one == bits + 1, two, one))
    second = where((one == bits + 1) | (two == bits + 1), bits + 1, jnp.where(two == bits, one, two))
    return first, second


def row_order(gates, spot, bits, maps, area, first, second, moved):
    order = []
    filled = jnp.int32(0)
    for j in range(bits):
        target = gates[spot + (j,)]
        last = jnp.where((filled == bits - 2) & (moved[0] == 0), bits - 2, bits - 1)
        free = jnp.where(filled < bits - 2, filled, last)
        place = jnp.where(target == bits, bits - 2, jnp.where(target == bits + 1, bits - 1, free))
        filled = filled + where(target < bits, 1, 0)
        maps[area, target] = place
        order.append(place)
    maps[area, first] = jnp.int32(bits - 2)
    maps[area, second] = jnp.int32(bits - 1)
    return order


IN, LANES, ROWS_A, ROWS_B, ROWS_C, PLACE, POS = range(7)


def start_maps(maps, bits):
    for area in range(7):
        for q in range(bits + 2):
            maps[area, q] = jnp.int32(q)


def make_plan(index, gates, swaps, count, maps, bits):
    plan = {}
    high = bits + 2
    spot = (0, index)
    first, second = excluded(gates, spot, bits)
    moved = [where(first != bits, 1, 0), where(second != bits + 1, 1, 0)]
    p0, p1 = maps[IN, first], maps[IN, second]
    low0, low1 = p0 < SUB, p1 < SUB
    s0 = jnp.where(
        low0,
        jnp.where(low1 | (p1 != bits), p0, -1),
        jnp.where(low1 & (p0 != bits), p1, -1),
    )
    s1 = jnp.where(
        low0,
        jnp.where(low1, p1, jnp.where(p1 == bits, p0, -1)),
        jnp.where(low1 & (p0 == bits), p1, -1),
    )
    plan["stage"] = [s0, s1]
    for q in range(high):
        p = maps[IN, q]
        p = jnp.where(p == s0, bits, jnp.where((p == bits) & (s0 >= 0), s0, p))
        p = jnp.where(p == s1, bits + 1, jnp.where((p == bits + 1) & (s1 >= 0), s1, p))
        maps[POS, q] = p
    e0, e1 = maps[POS, first], maps[POS, second]
    lower, upper = jnp.minimum(e0, e1) - SUB, jnp.maximum(e0, e1) - SUB
    plan["kept"] = []
    for j in range(TOP - 2):
        j = j + where(j >= lower, 1, 0)
        j = j + where(j >= upper, 1, 0)
        plan["kept"].append(jnp.left_shift(jnp.int32(1), j))
    plan["away"] = [jnp.left_shift(jnp.int32(1), e0 - SUB), jnp.left_shift(jnp.int32(1), e1 - SUB)]
    columns = []
    for j in range(bits):
        p = maps[POS, gates[spot + (j,)]]
        columns.append(p - where(e0 < p, 1, 0) - where(e1 < p, 1, 0))
    plan["columns0"] = columns
    plan["order0"] = row_order(gates, spot, bits, maps, ROWS_A, first, second, moved)
    plan["moved0"] = moved
    for gate, (lanes, rows) in enumerate(((LANES, ROWS_B), (ROWS_A, ROWS_C)), 1):
        spot = (gate, index)
        first, second = excluded(gates, spot, bits)
        moved = [where(first != bits, 1, 0), where(second != bits + 1, 1, 0)]
        l0 = jnp.where(moved[0] == 1, maps[lanes, first], 0)
        l1 = jnp.where(moved[1] == 1, maps[lanes, second], 0)
        maps[lanes, bits] = l0
        maps[lanes, bits + 1] = l1
        plan[f"lanes{gate}"] = [l0, l1]
        plan[f"columns{gate}"] = [maps[lanes, gates[spot + (j,)]] for j in range(bits)]
        plan[f"order{gate}"] = row_order(gates, spot, bits, maps, rows, first, second, moved)
        plan[f"moved{gate}"] = moved
    sent = [swaps[index, j] for j in range(count)]
    mask, taken = jnp.int32(0), jnp.int32(0)
    for j, s in enumerate(sent):
        mask = mask | jnp.left_shift(jnp.int32(1), s)
        taken = taken | where(s < bits, 1 << (bits - 1 - j), 0)
    for q in range(SUB):
        taken = taken | where((mask >> q) & 1 == 1, 0, 1 << q)
        maps[PLACE, q] = jnp.int32(q)
    for j, s in enumerate(sent):
        maps[PLACE, s] = jnp.int32(bits - 1 - j)
    for q in range(SUB, bits):
        chosen = (mask >> q) & 1
        lowest = ~taken & (taken + 1)
        place = jnp.int32(0)
        for b in range(1, bits):
            place = place + b * ((lowest >> b) & 1)
        maps[PLACE, q] = jnp.where(chosen == 1, maps[PLACE, q], place)
        taken = jnp.where(chosen == 1, taken, taken | lowest)
    maps[PLACE, bits] = jnp.int32(bits)
    maps[PLACE, bits + 1] = jnp.int32(bits + 1)
    places = [maps[PLACE, s] for s in sent]
    plan["device"] = [jnp.left_shift(jnp.int32(1), p - SUB) for p in places]
    rest = jnp.int32(2**TOP - 1)
    for weight in plan["device"]:
        rest = rest & ~weight
    plan["slot"] = []
    for _ in range(TOP - count):
        lowest = rest & -rest
        plan["slot"].append(lowest)
        rest = rest & ~lowest
    plan["lane_from"] = [maps[ROWS_B, q] for q in range(bits)]
    plan["lane_to"] = [maps[PLACE, q] for q in range(bits)]
    plan["low_from"] = [maps[ROWS_C, q] for q in range(bits)]
    for q in range(high):
        p = maps[PLACE, q]
        for place in places:
            p = p - where(place < maps[PLACE, q], 1, 0)
        maps[IN, q] = p
    for j, s in enumerate(sent):
        maps[IN, s] = jnp.int32(high - count + j)
    for q in range(bits):
        maps[LANES, q] = maps[ROWS_C, q]
    plan["last_stage"] = [jnp.where(s < SUB, s, -1) for s in sent]
    plan["last"] = []
    for q in range(SUB, high):
        p = maps[IN, q]
        for j, s in enumerate(plan["last_stage"]):
            p = jnp.where(p == s, high - count + j, p)
        plan["last"].append(jnp.left_shift(jnp.int32(1), p - SUB))
    return plan


KEYS = ("stage", "kept", "away", "moved0", "moved1", "moved2", "lanes1", "lanes2", "device", "slot")
KEYS = KEYS + ("lane_from", "lane_to", "low_from", "last_stage", "last")


def plan_sizes(count, bits):
    sizes = (2, TOP - 2, 2, 2, 2, 2, 2, 2, count, TOP - count, bits, bits, bits, count, TOP)
    return dict(zip(KEYS, sizes))


def write_plan(plan, ref):
    at = 0
    for key in KEYS:
        for value in plan[key]:
            ref[at] = value
            at += 1


def read_plan(ref, count, bits):
    plan, at = {}, 0
    for key, size in plan_sizes(count, bits).items():
        plan[key] = [ref[at + j] for j in range(size)]
        at += size
    return plan


def spread(position, sources, dests):
    total = jnp.zeros_like(position)
    for source, dest in zip(sources, dests):
        total = total | (((position >> source) & 1) << dest)
    return total


def split(value):
    top = value.astype(jnp.bfloat16)
    return top, (value - top.astype(jnp.float32)).astype(jnp.bfloat16)


def prepare_gate(plan, gate, real, imag, out):
    size = real.shape[0]
    bits = size.bit_length() - 1
    lane = lax.broadcasted_iota(jnp.int32, (8, size), 1)
    columns = spread(lane, plan[f"columns{gate}"], range(bits))
    columns = jnp.broadcast_to(columns[0:1, :], (size, size))
    row = lax.broadcasted_iota(jnp.int32, (size, size), 0)
    column = lax.broadcasted_iota(jnp.int32, (size, size), 1)
    chosen = spread(row, plan[f"order{gate}"], range(bits)) == column
    chosen = jnp.where(chosen, 1.0, 0.0).astype(jnp.bfloat16)
    parts = []
    for part in (real, imag):
        parts += split(jnp.take_along_axis(part, columns, axis=1))
    moved = jnp.dot(chosen, jnp.concatenate(parts, axis=1), preferred_element_type=jnp.float32)
    moved = moved.astype(jnp.bfloat16)
    re_hi, re_lo, im_hi, im_lo = (moved[:, j * size : (j + 1) * size] for j in range(4))
    for at, re, im in ((0, re_hi, im_hi), (2 * size, re_hi, im_hi), (4 * size, re_lo, im_lo)):
        out[gate, 0:size, at : at + size] = re
        out[gate, 0:size, at + size : at + 2 * size] = -im
        out[gate, size : 2 * size, at : at + size] = im
        out[gate, size : 2 * size, at + size : at + 2 * size] = re


def trade(v0, v1, low, keep0, keep1, index, axis):
    crossed = jnp.take_along_axis(jnp.where(low, v1, v0), index, axis=axis)
    return jnp.where(keep0, v0, crossed), jnp.where(keep1, v1, crossed)


def trade_masks(shape, axis, bit, moved):
    position = lax.broadcasted_iota(jnp.int32, shape, axis)
    value = (position >> bit) & 1
    low = value == 0
    return low, (value & moved) == 0, ((1 - value) & moved) == 0, position ^ jnp.left_shift(jnp.int32(1), bit)


def sublane_stage(state, vreg_bit, bit):
    @pl.when(bit >= 0)
    def _():
        masks = trade_masks(state.shape[2:], 0, jnp.maximum(bit, 0), 1)
        for part in range(state.shape[0]):
            for v in range(state.shape[1]):
                if (v >> vreg_bit) & 1 == 0:
                    w = v | 1 << vreg_bit
                    state[part, v], state[part, w] = trade(state[part, v], state[part, w], *masks, 0)


def block_rows(moved, size):
    a, b = 2 * size, size // 4
    d = []
    for i in range(2):
        d.append([[where(moved[i] == 1, f * a + h * b, h * a + f * b) << i for f in range(2)] for h in range(2)])
    return lambda h, f: d[0][h & 1][f & 1] + d[1][h >> 1][f >> 1]


def multiply(product, left, right, contract):
    size = left.shape[0] // 2
    out = lax.dot_general(left, right, (((1,), (contract,)), ((), ())), preferred_element_type=jnp.float32)
    for a in range(4):
        for part in range(2):
            at = a * 2 * size + part * size
            product[at : at + size, :] = out[part * size : (part + 1) * size, a * size : (a + 1) * size]


def run_round(plan, state, weights, by_row, by_lane, product, canonical):
    size = state.shape[-1]
    bits = size.bit_length() - 1
    for j in range(2):
        sublane_stage(state, TOP - 2 + j, plan["stage"][j])
    away, kept = combos(plan["away"]), combos(plan["kept"])
    for part in range(2):
        for a in range(4):
            for m in range(len(kept) // 2):
                pair = [state[part, away[a] + kept[2 * m + j]] for j in range(2)]
                high, low = split(jnp.concatenate(pair, axis=0))
                at = part * size + 16 * m
                for row, value in ((at, high), (2 * size + at, low), (4 * size + at, high)):
                    by_row[row : row + 16, a * size : (a + 1) * size] = value
    multiply(product, weights[0], by_row[...], 0)
    rows = block_rows(plan["moved0"], size)
    for gate in (1, 2):
        masks = [
            trade_masks((16, size), 1, plan[f"lanes{gate}"][j], plan[f"moved{gate}"][j]) for j in range(2)
        ]
        for part in range(2):
            for f in range(4):
                for m in range(size // 64):
                    v = []
                    for h in range(4):
                        at = pl.multiple_of(rows(h, f) + (part * size + 16 * m), 16)
                        v.append(product[pl.ds(at, 16), :])
                    v[0], v[1] = trade(v[0], v[1], *masks[0], 1)
                    v[2], v[3] = trade(v[2], v[3], *masks[0], 1)
                    v[0], v[2] = trade(v[0], v[2], *masks[1], 1)
                    v[1], v[3] = trade(v[1], v[3], *masks[1], 1)
                    for a in range(4):
                        high, low = split(v[a])
                        at = a * size + f * (size // 4) + 16 * m
                        for column, value in ((0, high), (2, low), (4, high)):
                            column = (column + part) * size
                            by_lane[at : at + 16, column : column + size] = value
        multiply(product, weights[gate], by_lane[...], 1)
        rows = block_rows(plan[f"moved{gate}"], size)
    lane = lax.broadcasted_iota(jnp.int32, (8, size), 1)
    order = spread(lane, plan["lane_to"], plan["lane_from"])
    order = jnp.broadcast_to(order[0:1, :], (size, size))
    natural = spread(lane, range(bits), plan["low_from"])
    natural = jnp.broadcast_to(natural[0:1, :], (size, size))
    for part in range(2):
        for h in range(4):
            blocks = []
            for f in range(4):
                at = pl.multiple_of(rows(h, f) + part * size, 32)
                blocks.append(product[pl.ds(at, size // 4), :])
            block = jnp.take_along_axis(jnp.concatenate(blocks, axis=0), order, axis=1).T
            if canonical:
                block = jnp.take_along_axis(block, natural, axis=1)
            state[part, h * (size // 8) : (h + 1) * (size // 8)] = block.reshape(size // 8, 8, size)


def send_chunks(plan, state, me, outs):
    slots = combos(plan["slot"])
    for offset, out in enumerate(outs):
        device = me ^ offset
        base = jnp.int32(0)
        for j, weight in enumerate(plan["device"]):
            base = base + ((device >> j) & 1) * weight
        for part in range(2):
            for j, slot in enumerate(slots):
                at = (part * len(slots) + j) * 8
                out[at : at + 8, :] = state[part, base + slot]


def take_chunks(state, me, chunks):
    slots = state.shape[1] // len(chunks)
    for offset, chunk in enumerate(chunks):
        device = me ^ offset
        for part in range(2):
            block = chunk[part * slots * 8 : (part + 1) * slots * 8, :]
            state[part, pl.ds(device * slots, slots)] = block.reshape(slots, 8, state.shape[-1])


def first_kernel(axis, count, gates, swaps, amps, real, imag, *rest):
    devices = 2**count
    outs = rest[:devices]
    maps, raw, re, im, weights, state, by_row, by_lane, product, sems = rest[devices:]
    copies = [
        pltpu.make_async_copy(source, dest, sems.at[j])
        for j, (source, dest) in enumerate(((real.at[0], re), (imag.at[0], im), (amps, raw)))
    ]
    for copy in copies:
        copy.start()
    bits = state.shape[-1].bit_length() - 1
    start_maps(maps, bits)
    plan = make_plan(0, gates, swaps, count, maps, bits)
    copies[0].wait()
    copies[1].wait()
    for gate in range(3):
        prepare_gate(plan, gate, re[gate], im[gate], weights)
    copies[2].wait()
    for part in range(2):
        for v in range(state.shape[1]):
            state[part, v] = raw[pl.ds(16 * v + part, 8, stride=2), :]
    run_round(plan, state, weights, by_row, by_lane, product, False)
    send_chunks(plan, state, lax.axis_index(axis), outs)


def plan_kernel(counts, gates, swaps, real, imag, plan_out, weights, maps, re, im, sems):
    copies = [
        pltpu.make_async_copy(source, dest, sems.at[j])
        for j, (source, dest) in enumerate(((real.at[1], re), (imag.at[1], im)))
    ]
    for copy in copies:
        copy.start()
    bits = re.shape[-1].bit_length() - 1
    start_maps(maps, bits)
    make_plan(0, gates, swaps, counts[0], maps, bits)
    plan = make_plan(1, gates, swaps, counts[1], maps, bits)
    write_plan(plan, plan_out)
    for copy in copies:
        copy.wait()
    for gate in range(3):
        prepare_gate(plan, gate, re[gate], im[gate], weights)


def second_kernel(axes, counts, plan_ref, weights, *rest):
    chunks, rest = rest[: 2 ** counts[0]], rest[2 ** counts[0] :]
    outs, rest = rest[: 2 ** counts[1]], rest[2 ** counts[1] :]
    state, by_row, by_lane, product = rest
    plan = read_plan(plan_ref, counts[1], state.shape[-1].bit_length() - 1)
    take_chunks(state, lax.axis_index(axes[0]), chunks)
    run_round(plan, state, weights, by_row, by_lane, product, True)
    send_chunks(plan, state, lax.axis_index(axes[1]), outs)


def last_kernel(axis, count, plan_ref, *rest):
    chunks, (out, state) = rest[: 2**count], rest[2**count :]
    plan = read_plan(plan_ref, count, state.shape[-1].bit_length() - 1)
    take_chunks(state, lax.axis_index(axis), chunks)
    for j in range(count):
        sublane_stage(state, TOP - count + j, plan["last_stage"][j])
    for part in range(2):
        for v, source in enumerate(combos(plan["last"])):
            out[pl.ds(16 * v + part, 8, stride=2), :] = state[part, source]


def exchange(chunks, axis):
    devices = len(chunks)
    moved = list(chunks)
    for offset in reversed(range(1, devices)):
        pairs = [(d, d ^ offset) for d in range(devices)]
        moved[offset] = lax.ppermute(chunks[offset], axis, pairs)
    return [pltpu.with_memory_space_constraint(chunk, pltpu.VMEM) for chunk in moved]


def fused(axes, counts, amplitudes, gate_real, gate_imag, gate_qubits, swap_qubits):
    size = gate_real.shape[-1]
    rows = amplitudes.shape[-1] // size
    amps = amplitudes.reshape(2, rows, size).transpose(1, 0, 2).reshape(2 * rows, size)
    f32, bf16, i32 = jnp.float32, jnp.bfloat16, jnp.int32
    smem = pl.BlockSpec(memory_space=pltpu.SMEM)
    vmem = pl.BlockSpec(memory_space=pltpu.VMEM)
    hbm = pl.BlockSpec(memory_space=pl.ANY)
    maps = pltpu.SMEM((8, 16), i32)
    gate_qubits = gate_qubits.transpose(1, 0, 2)
    gate = pltpu.VMEM(gate_real.shape[1:], f32)
    operators = (gate_real.shape[1], 2 * size, 6 * size)
    state = pltpu.VMEM((2, rows // 8, 8, size), f32)
    work = [
        state,
        pltpu.VMEM((6 * size, rows), bf16),
        pltpu.VMEM((rows, 6 * size), bf16),
        pltpu.VMEM((2 * rows, size), f32),
    ]
    chunk = [pltpu.VMEM((2 * rows >> count, size), f32) for count in counts]
    sent = pl.pallas_call(
        functools.partial(first_kernel, axes[0], counts[0]),
        out_shape=[chunk[0]] * 2 ** counts[0],
        in_specs=[smem, smem, hbm, hbm, hbm],
        out_specs=[vmem] * 2 ** counts[0],
        scratch_shapes=[maps, pltpu.VMEM(amps.shape, f32), gate, gate, pltpu.VMEM(operators, bf16), *work]
        + [pltpu.SemaphoreType.DMA((3,))],
        name="first_round",
    )(gate_qubits, swap_qubits, amps, gate_real, gate_imag)
    plan, weights = pl.pallas_call(
        functools.partial(plan_kernel, counts),
        out_shape=[
            jax.ShapeDtypeStruct((sum(plan_sizes(counts[1], size.bit_length() - 1).values()),), i32),
            pltpu.VMEM(operators, bf16),
        ],
        in_specs=[smem, smem, hbm, hbm],
        out_specs=[smem, vmem],
        scratch_shapes=[maps, gate, gate, pltpu.SemaphoreType.DMA((2,))],
        name="second_plan",
    )(gate_qubits, swap_qubits, gate_real, gate_imag)
    weights = pltpu.with_memory_space_constraint(weights, pltpu.VMEM)
    arrived = exchange(sent, axes[0])
    sent = pl.pallas_call(
        functools.partial(second_kernel, axes, counts),
        out_shape=[chunk[1]] * 2 ** counts[1],
        in_specs=[smem, vmem] + [vmem] * len(arrived),
        out_specs=[vmem] * 2 ** counts[1],
        scratch_shapes=work,
        name="second_round",
    )(plan, weights, *arrived)
    arrived = exchange(sent, axes[1])
    out = pl.pallas_call(
        functools.partial(last_kernel, axes[1], counts[1]),
        out_shape=jax.ShapeDtypeStruct(amps.shape, f32),
        in_specs=[smem] + [vmem] * len(arrived),
        out_specs=vmem,
        scratch_shapes=[state],
        name="last_places",
    )(plan, *arrived)
    return out.reshape(rows, 2, size).transpose(1, 0, 2).reshape(amplitudes.shape)


def program(mesh, *arrays):
    axes = ("row", "col")
    counts = tuple(mesh.shape[axis].bit_length() - 1 for axis in axes)
    amplitudes, gate_real = arrays[:2]
    size = gate_real.shape[-1]
    rounds = gate_real.shape[0] == 2 and gate_real.shape[1] == 3
    known = size == 128 and amplitudes.shape[-1] == 4 * size * size
    if known and rounds and max(counts) <= 4:
        return fused(axes, counts, *arrays)
    return per_device(*arrays)


def solution(mesh):
    placed = (P("row", "col", None, None), P(), P(), P(), P())
    return jax.shard_map(
        functools.partial(program, mesh),
        mesh=mesh,
        in_specs=placed,
        out_specs=P("row", "col", None, None),
        check_vma=False,
    )
```

```python
import functools

import jax
import jax.numpy as jnp
from jax import lax
from jax.experimental import pallas as pl
from jax.experimental.pallas import tpu as pltpu
from jax.sharding import PartitionSpec as P


def spread_bits(dest, total_bits):
    low_count = total_bits // 2
    high_count = total_bits - low_count

    def table(count, offset):
        position = jnp.arange(2**count, dtype=jnp.int32)
        result = jnp.zeros_like(position)
        for bit_index in range(count):
            result = result + jnp.left_shift(position >> bit_index & 1, dest[offset + bit_index])
        return result

    low_table = table(low_count, 0)
    high_table = table(high_count, low_count)
    return (high_table[:, None] + low_table[None, :]).reshape(-1)


def qubit_maps(chosen, top_count, total_bits):
    qubits = jnp.arange(total_bits, dtype=jnp.int32)
    picked = chosen[:top_count]
    matches = picked[:, None] == qubits[None, :]
    chosen_mask = jnp.any(matches, axis=0)
    slot_top = jnp.sum(
        jnp.where(matches, jnp.arange(top_count, dtype=jnp.int32)[:, None], 0), axis=0
    )
    unchosen = jnp.where(chosen_mask, 0, 1).astype(jnp.int32)
    rest_rank = jnp.cumsum(unchosen) - unchosen
    ordering = jnp.argsort(jnp.where(chosen_mask, total_bits + qubits, qubits))
    low_bits = total_bits - top_count
    forward_dest = jnp.concatenate([ordering[:low_bits], picked])
    backward_dest = jnp.where(chosen_mask, low_bits + slot_top, rest_rank)
    return (spread_bits(forward_dest, total_bits), spread_bits(backward_dest, total_bits))


def per_device(amplitudes, gate_real, gate_imag, gate_qubits, swap_qubits):
    local_size = amplitudes.shape[-1]
    total_bits = local_size.bit_length() - 1
    gate_size = gate_real.shape[-1]
    gate_bits = gate_size.bit_length() - 1
    high_bits = total_bits - gate_bits
    row_count = local_size // gate_size
    current = amplitudes.reshape(2, row_count, gate_size)
    for round_index in range(gate_real.shape[0]):
        for gate_index in range(gate_real.shape[1]):
            forward, backward = qubit_maps(
                gate_qubits[round_index, gate_index], gate_bits, high_bits
            )
            gathered = jnp.take(current, forward, axis=1, mode="clip").reshape(
                2 * gate_size, local_size // gate_size
            )
            real_part = gate_real[round_index, gate_index]
            imag_part = gate_imag[round_index, gate_index]
            operator = jnp.concatenate(
                [
                    jnp.concatenate([real_part, -imag_part], 1),
                    jnp.concatenate([imag_part, real_part], 1),
                ],
                0,
            )
            applied = jnp.dot(
                operator,
                gathered,
                precision=lax.Precision.HIGHEST,
                preferred_element_type=jnp.float32,
            ).reshape(2, row_count, gate_size)
            current = jnp.take(applied, backward, axis=1, mode="clip")
            current = (
                current.reshape(2, row_count // gate_size, gate_size, gate_size)
                .transpose(0, 1, 3, 2)
                .reshape(2, row_count, gate_size)
            )
        if round_index % 2 == 0:
            devices = lax.axis_size("row")
            forward, backward = qubit_maps(
                swap_qubits[round_index], devices.bit_length() - 1, high_bits
            )
            prepared = jnp.take(current, forward, axis=1, mode="clip").reshape(
                2, devices, local_size // devices
            )
            arrived = lax.all_to_all(prepared, "row", split_axis=1, concat_axis=1, tiled=True)
        else:
            devices = lax.axis_size("col")
            forward, backward = qubit_maps(
                swap_qubits[round_index], devices.bit_length() - 1, high_bits
            )
            prepared = jnp.take(current, forward, axis=1, mode="clip").reshape(
                2, devices, local_size // devices
            )
            arrived = lax.all_to_all(prepared, "col", split_axis=1, concat_axis=1, tiled=True)
        current = jnp.take(arrived.reshape(2, row_count, gate_size), backward, axis=1, mode="clip")
    return current.reshape(amplitudes.shape)


SUB = 3
TOP = 6


def combos(weights):
    sums = [jnp.int32(0)]
    for weight in weights:
        sums = sums + [total + weight for total in sums]
    return sums


def where(cond, yes, no):
    return jnp.where(cond, jnp.int32(yes), jnp.int32(no))


def excluded(gates, spot, bits):
    one, two = gates[spot + (bits,)], gates[spot + (bits + 1,)]
    first = where((one == bits) | (two == bits), bits, jnp.where(one == bits + 1, two, one))
    second = where((one == bits + 1) | (two == bits + 1), bits + 1, jnp.where(two == bits, one, two))
    return first, second


def row_order(gates, spot, bits, maps, area, first, second, moved):
    filled = jnp.int32(0)
    for j in range(bits):
        target = gates[spot + (j,)]
        last = jnp.where((filled == bits - 2) & (moved[0] == 0), bits - 2, bits - 1)
        free = jnp.where(filled < bits - 2, filled, last)
        place = jnp.where(target == bits, bits - 2, jnp.where(target == bits + 1, bits - 1, free))
        filled = filled + where(target < bits, 1, 0)
        maps[area, target] = place
        maps[INVERSE, place] = jnp.int32(1 << j)
    maps[area, first] = jnp.int32(bits - 2)
    maps[area, second] = jnp.int32(bits - 1)
    return [maps[INVERSE, b] for b in range(bits)]


IN, LANES, ROWS_A, ROWS_B, ROWS_C, PLACE, POS, INVERSE = range(8)


def start_maps(maps, bits):
    for area in range(7):
        for q in range(bits + 2):
            maps[area, q] = jnp.int32(q)


def first_plan(index, gates, maps, bits):
    plan = {}
    high = bits + 2
    spot = (0, index)
    first, second = excluded(gates, spot, bits)
    moved = [where(first != bits, 1, 0), where(second != bits + 1, 1, 0)]
    p0, p1 = maps[IN, first], maps[IN, second]
    low0, low1 = p0 < SUB, p1 < SUB
    s0 = jnp.where(
        low0,
        jnp.where(low1 | (p1 != bits), p0, -1),
        jnp.where(low1 & (p0 != bits), p1, -1),
    )
    s1 = jnp.where(
        low0,
        jnp.where(low1, p1, jnp.where(p1 == bits, p0, -1)),
        jnp.where(low1 & (p0 == bits), p1, -1),
    )
    plan["stage"] = [s0, s1]
    for q in range(high):
        p = maps[IN, q]
        p = jnp.where(p == s0, bits, jnp.where((p == bits) & (s0 >= 0), s0, p))
        p = jnp.where(p == s1, bits + 1, jnp.where((p == bits + 1) & (s1 >= 0), s1, p))
        maps[POS, q] = p
    e0, e1 = maps[POS, first], maps[POS, second]
    lower, upper = jnp.minimum(e0, e1) - SUB, jnp.maximum(e0, e1) - SUB
    plan["kept"] = []
    for j in range(TOP - 2):
        j = j + where(j >= lower, 1, 0)
        j = j + where(j >= upper, 1, 0)
        plan["kept"].append(jnp.left_shift(jnp.int32(1), j))
    plan["away"] = [jnp.left_shift(jnp.int32(1), e0 - SUB), jnp.left_shift(jnp.int32(1), e1 - SUB)]
    columns = []
    for j in range(bits):
        p = maps[POS, gates[spot + (j,)]]
        columns.append(p - where(e0 < p, 1, 0) - where(e1 < p, 1, 0))
    plan["columns0"] = columns
    plan["order0"] = row_order(gates, spot, bits, maps, ROWS_A, first, second, moved)
    plan["moved0"] = moved
    return plan


def place_rows(first, second, moved, sent, wanted, keep, maps, bits):
    free = jnp.int32((1 << (bits - 2)) - 1)
    free = free | where(moved[0] == 0, 1 << (bits - 2), 0) | where(moved[1] == 0, 1 << (bits - 1), 0)
    done = jnp.left_shift(jnp.int32(1), first) | jnp.left_shift(jnp.int32(1), second)
    p = jnp.where(moved[1] == 0, bits - 1, jnp.where(moved[0] == 0, bits - 2, bits - 3))
    over = jnp.int32(-1)
    for j, q in enumerate(sent + wanted):
        fits = (q < bits) & ((done >> q) & 1 == 0)
        if j == SUB - 1:
            over = jnp.where(fits & (p < SUB), p, over)
        maps[ROWS_B, jnp.where(fits, q, bits + 2)] = p
        bit = jnp.left_shift(jnp.int32(1), p)
        free = jnp.where(fits, free & ~bit, free)
        done = jnp.where(fits, done | jnp.left_shift(jnp.int32(1), q), done)
        p = jnp.where(fits, p - 1 - where((p == bits - 1) & (moved[0] == 1), 1, 0), p)
    if keep:
        for q in range(SUB):
            fits = (done >> q) & 1 == 0
            maps[ROWS_B, jnp.where(fits, q, bits + 2)] = jnp.int32(q)
            free = jnp.where(fits, free & ~(1 << q), free)
            done = done | (1 << q)
    for q in range(SUB if keep else 0, bits):
        lowest = free & -free
        place = jnp.int32(0)
        for b in range(1, bits):
            place = place + b * ((lowest >> b) & 1)
        fits = (done >> q) & 1 == 0
        maps[ROWS_B, jnp.where(fits, q, bits + 2)] = place
        free = jnp.where(fits, free & ~lowest, free)
    maps[ROWS_B, first] = jnp.int32(bits - 2)
    maps[ROWS_B, second] = jnp.int32(bits - 1)
    return over


def later_plan(index, gates, swaps, count, maps, bits):
    plan = {}
    high = bits + 2
    ends = index + 1 == gates.shape[1]
    sent = [swaps[index, j] for j in range(count)]
    wanted = [] if ends else [gates[0, index + 1, bits + j] for j in range(2)]
    for gate, lanes in ((1, LANES), (2, ROWS_A)):
        spot = (gate, index)
        first, second = excluded(gates, spot, bits)
        moved = [where(first != bits, 1, 0), where(second != bits + 1, 1, 0)]
        l0 = jnp.where(moved[0] == 1, maps[lanes, first], 0)
        l1 = jnp.where(moved[1] == 1, maps[lanes, second], 0)
        maps[lanes, bits] = l0
        maps[lanes, bits + 1] = l1
        plan[f"lanes{gate}"] = [l0, l1]
        targets = [gates[spot + (j,)] for j in range(bits)]
        plan[f"columns{gate}"] = [maps[lanes, target] for target in targets]
        plan[f"moved{gate}"] = moved
        if gate == 1:
            over = place_rows(first, second, moved, sent, wanted, ends, maps, bits)
            rows = ROWS_B
            maps[rows, bits] = jnp.int32(bits - 2)
            maps[rows, bits + 1] = jnp.int32(bits - 1)
            aside = (first, second)
        else:
            rows = ROWS_C
            for q in range(bits):
                maps[rows, q] = jnp.int32(q)
            maps[rows, bits] = first
            maps[rows, bits + 1] = second
            plan["back"] = [jnp.where(moved[0] == 1, first, 0), jnp.where(moved[1] == 1, second, 0)]
        for j, target in enumerate(targets):
            maps[INVERSE, maps[rows, target]] = jnp.int32(1 << j)
        plan[f"order{gate}"] = [maps[INVERSE, b] for b in range(bits)]
    if ends:
        mask = jnp.int32(0)
        for s in sent:
            mask = mask | jnp.left_shift(jnp.int32(1), s)
        post = [jnp.where((q < SUB) & ((mask >> q) & 1 == 0), q, -1) for q in aside]
    else:
        post = [over, jnp.int32(-1)]
    plan["post"] = post
    for q in range(bits):
        p = maps[ROWS_B, q]
        p = jnp.where(p == post[0], bits - 2, jnp.where((p == bits - 2) & (post[0] >= 0), post[0], p))
        p = jnp.where(p == post[1], bits - 1, jnp.where((p == bits - 1) & (post[1] >= 0), post[1], p))
        maps[PLACE, q] = p
    maps[PLACE, bits] = jnp.int32(bits)
    maps[PLACE, bits + 1] = jnp.int32(bits + 1)
    places = [maps[PLACE, s] for s in sent]
    plan["device"] = [jnp.left_shift(jnp.int32(1), p - SUB) for p in places]
    rest = jnp.int32(2**TOP - 1)
    for weight in plan["device"]:
        rest = rest & ~weight
    plan["slot"] = []
    for _ in range(TOP - count):
        lowest = rest & -rest
        plan["slot"].append(lowest)
        rest = rest & ~lowest
    for q in range(high):
        p = maps[PLACE, q]
        for place in places:
            p = p - where(place < maps[PLACE, q], 1, 0)
        maps[IN, q] = p
    for j, s in enumerate(sent):
        maps[IN, s] = jnp.int32(high - count + j)
    for q in range(bits):
        maps[LANES, q] = jnp.int32(q)
    plan["last_stage"] = [jnp.where(s < SUB, s, -1) for s in sent]
    plan["last"] = []
    for q in range(SUB, high):
        p = maps[IN, q]
        for j, s in enumerate(plan["last_stage"]):
            p = jnp.where(p == s, high - count + j, p)
        plan["last"].append(jnp.left_shift(jnp.int32(1), p - SUB))
    return plan


def make_plan(index, gates, swaps, count, maps, bits):
    plan = first_plan(index, gates, maps, bits)
    return plan | later_plan(index, gates, swaps, count, maps, bits)


KEYS = ("stage", "kept", "away", "moved0", "moved1", "moved2", "lanes1", "lanes2", "device", "slot")
KEYS = KEYS + ("back", "post", "last_stage", "last")


def plan_sizes(count, bits):
    sizes = (2, TOP - 2, 2, 2, 2, 2, 2, 2, count, TOP - count, 2, 2, count, TOP)
    return dict(zip(KEYS, sizes))


def write_plan(plan, ref):
    at = 0
    for key in KEYS:
        for value in plan[key]:
            ref[at] = value
            at += 1


def read_plan(ref, count, bits):
    plan, at = {}, 0
    for key, size in plan_sizes(count, bits).items():
        plan[key] = [ref[at + j] for j in range(size)]
        at += size
    return plan


def spread(position, sources, dests):
    total = jnp.zeros_like(position)
    for source, dest in zip(sources, dests):
        total = total | (((position >> source) & 1) << dest)
    return total


def split(value):
    top = value.astype(jnp.bfloat16)
    return top, (value - top.astype(jnp.float32)).astype(jnp.bfloat16)


def prepare_gate(plan, gate, real, imag, out):
    size = real.shape[0]
    bits = size.bit_length() - 1
    lane = lax.broadcasted_iota(jnp.int32, (8, size), 1)
    columns = spread(lane, plan[f"columns{gate}"], range(bits))
    columns = jnp.broadcast_to(columns[0:1, :], (size, size))
    weights = plan[f"order{gate}"]
    row = lax.broadcasted_iota(jnp.int32, (8, size), 0)
    for b in range(SUB):
        lane = lane - ((row >> b) & 1) * weights[b]
    chosen = [jnp.where(lane == first, 1.0, 0.0) for first in combos(weights[SUB:])]
    chosen = jnp.concatenate(chosen, axis=0).astype(jnp.bfloat16)
    parts = []
    for part in (real, imag):
        parts += split(jnp.take_along_axis(part, columns, axis=1))
    moved = jnp.dot(chosen, jnp.concatenate(parts, axis=1), preferred_element_type=jnp.float32)
    moved = moved.astype(jnp.bfloat16)
    re_hi, re_lo, im_hi, im_lo = (moved[:, j * size : (j + 1) * size] for j in range(4))
    for at, re, im in ((0, re_hi, im_hi), (2 * size, re_hi, im_hi), (4 * size, re_lo, im_lo)):
        out[gate, 0:size, at : at + size] = re
        out[gate, 0:size, at + size : at + 2 * size] = -im
        out[gate, size : 2 * size, at : at + size] = im
        out[gate, size : 2 * size, at + size : at + 2 * size] = re


def trade(v0, v1, low, keep0, keep1, index, axis):
    crossed = jnp.take_along_axis(jnp.where(low, v1, v0), index, axis=axis)
    return jnp.where(keep0, v0, crossed), jnp.where(keep1, v1, crossed)


def trade_masks(shape, axis, bit, moved):
    position = lax.broadcasted_iota(jnp.int32, shape, axis)
    value = (position >> bit) & 1
    low = value == 0
    return low, (value & moved) == 0, ((1 - value) & moved) == 0, position ^ jnp.left_shift(jnp.int32(1), bit)


def trade_array(v, masks):
    for j, (a, b) in enumerate(((0, 1), (2, 3), (0, 2), (1, 3))):
        v[a], v[b] = trade(v[a], v[b], *masks[j // 2], 1)


def sublane_stage(state, vreg_bit, bit):
    @pl.when(bit >= 0)
    def _():
        masks = trade_masks(state.shape[2:], 0, jnp.maximum(bit, 0), 1)
        for part in range(state.shape[0]):
            for v in range(state.shape[1]):
                if (v >> vreg_bit) & 1 == 0:
                    w = v | 1 << vreg_bit
                    state[part, v], state[part, w] = trade(state[part, v], state[part, w], *masks, 0)


def block_rows(moved, size):
    a, b = 2 * size, size // 4
    d = []
    for i in range(2):
        d.append([[where(moved[i] == 1, f * a + h * b, h * a + f * b) << i for f in range(2)] for h in range(2)])
    return lambda h, f: d[0][h & 1][f & 1] + d[1][h >> 1][f >> 1]


def multiply(product, left, right, contract):
    size = left.shape[0] // 2
    out = lax.dot_general(left, right, (((1,), (contract,)), ((), ())), preferred_element_type=jnp.float32)
    for a in range(4):
        for part in range(2):
            at = a * 2 * size + part * size
            product[at : at + size, :] = out[part * size : (part + 1) * size, a * size : (a + 1) * size]


def run_round(plan, later, state, weights, by_row, by_lane, product):
    size = state.shape[-1]
    for j in range(2):
        sublane_stage(state, TOP - 2 + j, plan["stage"][j])
    away, kept = combos(plan["away"]), combos(plan["kept"])
    for part in range(2):
        for a in range(4):
            for m in range(len(kept) // 2):
                pair = [state[part, away[a] + kept[2 * m + j]] for j in range(2)]
                high, low = split(jnp.concatenate(pair, axis=0))
                at = part * size + 16 * m
                for row, value in ((at, high), (2 * size + at, low), (4 * size + at, high)):
                    by_row[row : row + 16, a * size : (a + 1) * size] = value
    plan = plan | later()
    multiply(product, weights[0], by_row[...], 0)
    rows = block_rows(plan["moved0"], size)
    for gate in (1, 2):
        masks = [
            trade_masks((16, size), 1, plan[f"lanes{gate}"][j], plan[f"moved{gate}"][j]) for j in range(2)
        ]
        for part in range(2):
            for f in range(4):
                for m in range(size // 64):
                    v = []
                    for h in range(4):
                        at = pl.multiple_of(rows(h, f) + (part * size + 16 * m), 16)
                        v.append(product[pl.ds(at, 16), :])
                    trade_array(v, masks)
                    for a in range(4):
                        high, low = split(v[a])
                        at = a * size + f * (size // 4) + 16 * m
                        for column, value in ((0, high), (2, low), (4, high)):
                            column = (column + part) * size
                            by_lane[at : at + 16, column : column + size] = value
        if gate == 1:
            multiply(product, weights[gate], by_lane[...], 1)
            rows = block_rows(plan["moved1"], size)
    out = lax.dot_general(
        by_lane[...], weights[2], (((1,), (1,)), ((), ())), preferred_element_type=jnp.float32
    )
    masks = [trade_masks((16, size), 1, plan["back"][j], plan["moved2"][j]) for j in range(2)]
    for part in range(2):
        for m in range(size // 16):
            v = [out[a * size + 16 * m : a * size + 16 * m + 16, part * size : (part + 1) * size] for a in range(4)]
            trade_array(v, masks)
            for h in range(4):
                at = h * (size // 8) + 2 * m
                state[part, at : at + 2] = v[h].reshape(2, 8, size)
    for j in range(2):
        sublane_stage(state, TOP - 4 + j, plan["post"][j])
    return plan


def send_chunks(plan, state, me, outs):
    slots = combos(plan["slot"])
    for offset, out in enumerate(outs):
        device = me ^ offset
        base = jnp.int32(0)
        for j, weight in enumerate(plan["device"]):
            base = base + ((device >> j) & 1) * weight
        for part in range(2):
            for j, slot in enumerate(slots):
                at = (part * len(slots) + j) * 8
                out[at : at + 8, :] = state[part, base + slot]


def take_chunks(state, me, chunks):
    slots = state.shape[1] // len(chunks)
    for offset, chunk in zip(far_first(len(chunks)) + [0], chunks):
        device = me ^ offset
        for part in range(2):
            block = chunk[part * slots * 8 : (part + 1) * slots * 8, :]
            state[part, pl.ds(device * slots, slots)] = block.reshape(slots, 8, state.shape[-1])


def first_kernel(axis, count, gates, swaps, amps, real, imag, *rest):
    devices = 2**count
    outs = rest[:devices]
    maps, raw, re, im, weights, state, by_row, by_lane, product, sems = rest[devices:]
    piece = amps.shape[0] // 4
    moves = [(real.at[0, 0], re.at[0]), (imag.at[0, 0], im.at[0])]
    moves += [(amps.at[pl.ds(piece * j, piece)], raw.at[pl.ds(piece * j, piece)]) for j in range(4)]
    moves += [(real.at[0, pl.ds(1, 2)], re.at[pl.ds(1, 2)]), (imag.at[0, pl.ds(1, 2)], im.at[pl.ds(1, 2)])]
    copies = [pltpu.make_async_copy(source, dest, sems.at[j]) for j, (source, dest) in enumerate(moves)]
    for copy in copies:
        copy.start()
    bits = state.shape[-1].bit_length() - 1
    start_maps(maps, bits)
    plan = first_plan(0, gates, maps, bits)
    copies[0].wait()
    copies[1].wait()
    prepare_gate(plan, 0, re[0], im[0], weights)
    for copy in copies[2:]:
        copy.wait()
    for part in range(2):
        for v in range(state.shape[1]):
            state[part, v] = raw[pl.ds(16 * v + part, 8, stride=2), :]

    def later():
        rest = later_plan(0, gates, swaps, count, maps, bits)
        for gate in (1, 2):
            prepare_gate(rest, gate, re[gate], im[gate], weights)
        return rest

    plan = run_round(plan, later, state, weights, by_row, by_lane, product)
    send_chunks(plan, state, lax.axis_index(axis), outs)


def plan_kernel(counts, gates, swaps, real, imag, plan_out, weights, maps, re, im, sems):
    copies = [
        pltpu.make_async_copy(source, dest, sems.at[j])
        for j, (source, dest) in enumerate(((real.at[1], re), (imag.at[1], im)))
    ]
    for copy in copies:
        copy.start()
    bits = re.shape[-1].bit_length() - 1
    start_maps(maps, bits)
    make_plan(0, gates, swaps, counts[0], maps, bits)
    plan = make_plan(1, gates, swaps, counts[1], maps, bits)
    write_plan(plan, plan_out)
    for copy in copies:
        copy.wait()
    for gate in range(3):
        prepare_gate(plan, gate, re[gate], im[gate], weights)


def second_kernel(axes, counts, plan_ref, weights, *rest):
    chunks, rest = rest[: 2 ** counts[0]], rest[2 ** counts[0] :]
    outs, rest = rest[: 2 ** counts[1]], rest[2 ** counts[1] :]
    state, by_row, by_lane, product = rest
    plan = read_plan(plan_ref, counts[1], state.shape[-1].bit_length() - 1)
    take_chunks(state, lax.axis_index(axes[0]), chunks)
    run_round(plan, dict, state, weights, by_row, by_lane, product)
    send_chunks(plan, state, lax.axis_index(axes[1]), outs)


def last_kernel(axis, count, plan_ref, *rest):
    chunks, (out, state) = rest[: 2**count], rest[2**count :]
    plan = read_plan(plan_ref, count, state.shape[-1].bit_length() - 1)
    take_chunks(state, lax.axis_index(axis), chunks)
    for j in range(count):
        sublane_stage(state, TOP - count + j, plan["last_stage"][j])
    for part in range(2):
        for v, source in enumerate(combos(plan["last"])):
            out[pl.ds(16 * v + part, 8, stride=2), :] = state[part, source]


def far_first(devices):
    return sorted(range(1, devices), key=lambda offset: (-(offset >> 1), offset))


def exchange(chunks, axis):
    devices = len(chunks)
    moved = list(chunks)
    for offset in far_first(devices):
        pairs = [(d, d ^ offset) for d in range(devices)]
        moved[offset] = lax.ppermute(chunks[offset], axis, pairs)
    order = far_first(devices) + [0]
    return [pltpu.with_memory_space_constraint(moved[offset], pltpu.VMEM) for offset in order]


def fused(axes, counts, amplitudes, gate_real, gate_imag, gate_qubits, swap_qubits):
    size = gate_real.shape[-1]
    rows = amplitudes.shape[-1] // size
    amps = amplitudes.reshape(2, rows, size).transpose(1, 0, 2).reshape(2 * rows, size)
    f32, bf16, i32 = jnp.float32, jnp.bfloat16, jnp.int32
    smem = pl.BlockSpec(memory_space=pltpu.SMEM)
    vmem = pl.BlockSpec(memory_space=pltpu.VMEM)
    hbm = pl.BlockSpec(memory_space=pl.ANY)
    maps = pltpu.SMEM((8, 16), i32)
    gate_qubits = gate_qubits.transpose(1, 0, 2)
    gate = pltpu.VMEM(gate_real.shape[1:], f32)
    operators = (gate_real.shape[1], 2 * size, 6 * size)
    state = pltpu.VMEM((2, rows // 8, 8, size), f32)
    work = [
        state,
        pltpu.VMEM((6 * size, rows), bf16),
        pltpu.VMEM((rows, 6 * size), bf16),
        pltpu.VMEM((2 * rows, size), f32),
    ]
    chunk = [pltpu.VMEM((2 * rows >> count, size), f32) for count in counts]
    sent = pl.pallas_call(
        functools.partial(first_kernel, axes[0], counts[0]),
        out_shape=[chunk[0]] * 2 ** counts[0],
        in_specs=[smem, smem, hbm, hbm, hbm],
        out_specs=[vmem] * 2 ** counts[0],
        scratch_shapes=[maps, pltpu.VMEM(amps.shape, f32), gate, gate, pltpu.VMEM(operators, bf16), *work]
        + [pltpu.SemaphoreType.DMA((8,))],
        name="first_round",
    )(gate_qubits, swap_qubits, amps, gate_real, gate_imag)
    plan, weights = pl.pallas_call(
        functools.partial(plan_kernel, counts),
        out_shape=[
            jax.ShapeDtypeStruct((sum(plan_sizes(counts[1], size.bit_length() - 1).values()),), i32),
            pltpu.VMEM(operators, bf16),
        ],
        in_specs=[smem, smem, hbm, hbm],
        out_specs=[smem, vmem],
        scratch_shapes=[maps, gate, gate, pltpu.SemaphoreType.DMA((2,))],
        name="second_plan",
    )(gate_qubits, swap_qubits, gate_real, gate_imag)
    weights = pltpu.with_memory_space_constraint(weights, pltpu.VMEM)
    arrived = exchange(sent, axes[0])
    sent = pl.pallas_call(
        functools.partial(second_kernel, axes, counts),
        out_shape=[chunk[1]] * 2 ** counts[1],
        in_specs=[smem, vmem] + [vmem] * len(arrived),
        out_specs=[vmem] * 2 ** counts[1],
        scratch_shapes=work,
        name="second_round",
    )(plan, weights, *arrived)
    arrived = exchange(sent, axes[1])
    out = pl.pallas_call(
        functools.partial(last_kernel, axes[1], counts[1]),
        out_shape=jax.ShapeDtypeStruct(amps.shape, f32),
        in_specs=[smem] + [vmem] * len(arrived),
        out_specs=vmem,
        scratch_shapes=[state],
        name="last_places",
    )(plan, *arrived)
    return out.reshape(rows, 2, size).transpose(1, 0, 2).reshape(amplitudes.shape)


def program(mesh, *arrays):
    axes = ("row", "col")
    counts = tuple(mesh.shape[axis].bit_length() - 1 for axis in axes)
    amplitudes, gate_real = arrays[:2]
    size = gate_real.shape[-1]
    rounds = gate_real.shape[0] == 2 and gate_real.shape[1] == 3
    known = size == 128 and amplitudes.shape[-1] == 4 * size * size
    if known and rounds and max(counts) <= SUB:
        return fused(axes, counts, *arrays)
    return per_device(*arrays)


def solution(mesh):
    placed = (P("row", "col", None, None), P(), P(), P(), P())
    return jax.shard_map(
        functools.partial(program, mesh),
        mesh=mesh,
        in_specs=placed,
        out_specs=P("row", "col", None, None),
        check_vma=False,
    )
```

```python
import functools

import jax
import jax.numpy as jnp
from jax import lax
from jax.experimental import pallas as pl
from jax.experimental.pallas import tpu as pltpu
from jax.sharding import PartitionSpec as P


def spread_bits(dest, total_bits):
    low_count = total_bits // 2
    high_count = total_bits - low_count

    def table(count, offset):
        position = jnp.arange(2**count, dtype=jnp.int32)
        result = jnp.zeros_like(position)
        for bit_index in range(count):
            result = result + jnp.left_shift(position >> bit_index & 1, dest[offset + bit_index])
        return result

    low_table = table(low_count, 0)
    high_table = table(high_count, low_count)
    return (high_table[:, None] + low_table[None, :]).reshape(-1)


def qubit_maps(chosen, top_count, total_bits):
    qubits = jnp.arange(total_bits, dtype=jnp.int32)
    picked = chosen[:top_count]
    matches = picked[:, None] == qubits[None, :]
    chosen_mask = jnp.any(matches, axis=0)
    slot_top = jnp.sum(
        jnp.where(matches, jnp.arange(top_count, dtype=jnp.int32)[:, None], 0), axis=0
    )
    unchosen = jnp.where(chosen_mask, 0, 1).astype(jnp.int32)
    rest_rank = jnp.cumsum(unchosen) - unchosen
    ordering = jnp.argsort(jnp.where(chosen_mask, total_bits + qubits, qubits))
    low_bits = total_bits - top_count
    forward_dest = jnp.concatenate([ordering[:low_bits], picked])
    backward_dest = jnp.where(chosen_mask, low_bits + slot_top, rest_rank)
    return (spread_bits(forward_dest, total_bits), spread_bits(backward_dest, total_bits))


def per_device(amplitudes, gate_real, gate_imag, gate_qubits, swap_qubits):
    local_size = amplitudes.shape[-1]
    total_bits = local_size.bit_length() - 1
    gate_size = gate_real.shape[-1]
    gate_bits = gate_size.bit_length() - 1
    high_bits = total_bits - gate_bits
    row_count = local_size // gate_size
    current = amplitudes.reshape(2, row_count, gate_size)
    for round_index in range(gate_real.shape[0]):
        for gate_index in range(gate_real.shape[1]):
            forward, backward = qubit_maps(
                gate_qubits[round_index, gate_index], gate_bits, high_bits
            )
            gathered = jnp.take(current, forward, axis=1, mode="clip").reshape(
                2 * gate_size, local_size // gate_size
            )
            real_part = gate_real[round_index, gate_index]
            imag_part = gate_imag[round_index, gate_index]
            operator = jnp.concatenate(
                [
                    jnp.concatenate([real_part, -imag_part], 1),
                    jnp.concatenate([imag_part, real_part], 1),
                ],
                0,
            )
            applied = jnp.dot(
                operator,
                gathered,
                precision=lax.Precision.HIGHEST,
                preferred_element_type=jnp.float32,
            ).reshape(2, row_count, gate_size)
            current = jnp.take(applied, backward, axis=1, mode="clip")
            current = (
                current.reshape(2, row_count // gate_size, gate_size, gate_size)
                .transpose(0, 1, 3, 2)
                .reshape(2, row_count, gate_size)
            )
        if round_index % 2 == 0:
            devices = lax.axis_size("row")
            forward, backward = qubit_maps(
                swap_qubits[round_index], devices.bit_length() - 1, high_bits
            )
            prepared = jnp.take(current, forward, axis=1, mode="clip").reshape(
                2, devices, local_size // devices
            )
            arrived = lax.all_to_all(prepared, "row", split_axis=1, concat_axis=1, tiled=True)
        else:
            devices = lax.axis_size("col")
            forward, backward = qubit_maps(
                swap_qubits[round_index], devices.bit_length() - 1, high_bits
            )
            prepared = jnp.take(current, forward, axis=1, mode="clip").reshape(
                2, devices, local_size // devices
            )
            arrived = lax.all_to_all(prepared, "col", split_axis=1, concat_axis=1, tiled=True)
        current = jnp.take(arrived.reshape(2, row_count, gate_size), backward, axis=1, mode="clip")
    return current.reshape(amplitudes.shape)


SUB = 3
TOP = 6


def combos(weights):
    sums = [jnp.int32(0)]
    for weight in weights:
        sums = sums + [total + weight for total in sums]
    return sums


def where(cond, yes, no):
    return jnp.where(cond, jnp.int32(yes), jnp.int32(no))


def excluded(gates, spot, bits):
    one, two = gates[spot + (bits,)], gates[spot + (bits + 1,)]
    first = where((one == bits) | (two == bits), bits, jnp.where(one == bits + 1, two, one))
    second = where((one == bits + 1) | (two == bits + 1), bits + 1, jnp.where(two == bits, one, two))
    return first, second


def place_targets(first, second, moved, maps, area, bits):
    for q in range(bits):
        maps[area, q] = jnp.int32(q)
    other = where(second == bits - 2, bits + 1, bits - 2)
    maps[area, jnp.where(moved[0] == 1, other, SPARE)] = first
    back = jnp.where((moved[0] == 1) & (second == bits - 2), first, second)
    last = jnp.where((moved[0] == 1) & (first == bits - 1), other, bits - 1)
    maps[area, jnp.where(moved[1] == 1, last, SPARE)] = back
    for j, qubit in enumerate((first, second)):
        maps[area, bits + j] = jnp.int32(bits - 2 + j)
        maps[area, qubit] = jnp.int32(bits - 2 + j)


def row_order(targets, maps, area, bits):
    for j, target in enumerate(targets):
        maps[INVERSE, maps[area, target]] = jnp.int32(1 << j)
    return [maps[INVERSE, b] for b in range(bits)]


IN, LANES, ROWS_A, ROWS_B, ROWS_C, PLACE, POS, INVERSE, HELD = range(9)
SPARE = 15


class Maps:
    def __init__(self, ref):
        self.ref = ref

    def __getitem__(self, at):
        return self.ref[at[0] * (SPARE + 1) + at[1]]

    def __setitem__(self, at, value):
        self.ref[at[0] * (SPARE + 1) + at[1]] = value


def start_maps(maps, bits):
    for area in (IN, LANES):
        for q in range(bits + 2):
            maps[area, q] = jnp.int32(q)


def first_plan(index, gates, maps, bits):
    plan = {}
    high = bits + 2
    spot = (0, index)
    first, second = excluded(gates, spot, bits)
    moved = [where(first != bits, 1, 0), where(second != bits + 1, 1, 0)]
    p0, p1 = (first, second) if index == 0 else (maps[IN, first], maps[IN, second])
    low0, low1 = p0 < SUB, p1 < SUB
    s0 = jnp.where(
        low0,
        jnp.where(low1 | (p1 != bits), p0, -1),
        jnp.where(low1 & (p0 != bits), p1, -1),
    )
    s1 = jnp.where(
        low0,
        jnp.where(low1, p1, jnp.where(p1 == bits, p0, -1)),
        jnp.where(low1 & (p0 == bits), p1, -1),
    )
    plan["stage"] = [s0, s1]
    for q in range(high if index == 0 else 0):
        maps[POS, q] = jnp.int32(q)
    for j, s in enumerate((s0, s1) if index == 0 else ()):
        maps[POS, jnp.where(s >= 0, s, SPARE)] = jnp.int32(bits + j)
        maps[POS, jnp.where(s >= 0, bits + j, SPARE)] = s
    for q in range(high if index > 0 else 0):
        p = maps[IN, q]
        p = jnp.where(p == s0, bits, jnp.where((p == bits) & (s0 >= 0), s0, p))
        p = jnp.where(p == s1, bits + 1, jnp.where((p == bits + 1) & (s1 >= 0), s1, p))
        maps[POS, q] = p
    e0, e1 = maps[POS, first], maps[POS, second]
    lower, upper = jnp.minimum(e0, e1) - SUB, jnp.maximum(e0, e1) - SUB
    plan["kept"] = []
    for j in range(TOP - 2):
        j = j + where(j >= lower, 1, 0)
        j = j + where(j >= upper, 1, 0)
        plan["kept"].append(jnp.left_shift(jnp.int32(1), j))
    plan["away"] = [jnp.left_shift(jnp.int32(1), e0 - SUB), jnp.left_shift(jnp.int32(1), e1 - SUB)]
    targets = [gates[spot + (j,)] for j in range(bits)]
    columns = [maps[POS, target] for target in targets]
    plan["columns0"] = [p - where(e0 < p, 1, 0) - where(e1 < p, 1, 0) for p in columns]
    place_targets(first, second, moved, maps, ROWS_A, bits)
    plan["order0"] = row_order(targets, maps, ROWS_A, bits)
    plan["moved0"] = moved
    return plan


def place_rows(first, second, moved, sent, wanted, maps, bits):
    place_targets(first, second, moved, maps, ROWS_B, bits)
    for q in range(bits):
        maps[HELD, maps[ROWS_B, q]] = jnp.int32(q)
    free = jnp.int32((1 << (bits - 2)) - (1 << SUB))
    free = free | where(moved[0] == 0, 1 << (bits - 2), 0) | where(moved[1] == 0, 1 << (bits - 1), 0)
    over = jnp.int32(-1)
    for q in sent:
        free = free & ~jnp.left_shift(jnp.int32(1), maps[ROWS_B, q])
    for j, q in enumerate(sent + wanted):
        if j == len(sent):
            for other in wanted:
                free = free & ~jnp.left_shift(jnp.int32(1), maps[ROWS_B, other])
        p = maps[ROWS_B, q]
        lowest = free & -free
        fits = (p < SUB) & (free != 0)
        place = jnp.int32(SUB)
        for b in range(SUB + 1, bits):
            place = place + (b - SUB) * ((lowest >> b) & 1)
        held = maps[HELD, place]
        maps[ROWS_B, jnp.where(fits, held, SPARE)] = p
        maps[ROWS_B, jnp.where(fits, q, SPARE)] = place
        if j < len(sent):
            over = jnp.where((p < SUB) & (free == 0), p, over)
        free = jnp.where(fits, free & ~lowest, free)
    return over


def later_plan(index, gates, swaps, count, maps, bits):
    plan = {}
    ends = index + 1 == gates.shape[1]
    sent = [swaps[index, j] for j in range(count)]
    wanted = [] if ends else [gates[0, index + 1, bits + j] for j in range(2)]
    for gate, lanes in ((1, LANES), (2, ROWS_A)):
        spot = (gate, index)
        first, second = excluded(gates, spot, bits)
        moved = [where(first != bits, 1, 0), where(second != bits + 1, 1, 0)]
        l0 = jnp.where(moved[0] == 1, maps[lanes, first], 0)
        l1 = jnp.where(moved[1] == 1, maps[lanes, second], 0)
        maps[lanes, bits] = l0
        maps[lanes, bits + 1] = l1
        plan[f"lanes{gate}"] = [l0, l1]
        targets = [gates[spot + (j,)] for j in range(bits)]
        plan[f"columns{gate}"] = [maps[lanes, target] for target in targets]
        plan[f"moved{gate}"] = moved
        if gate == 1:
            over = place_rows(first, second, moved, sent, wanted, maps, bits)
            rows = ROWS_B
            aside = (first, second)
        else:
            rows = ROWS_C
            for q in range(bits):
                maps[rows, q] = jnp.int32(q)
            maps[rows, bits] = first
            maps[rows, bits + 1] = second
            plan["back"] = [jnp.where(moved[0] == 1, first, 0), jnp.where(moved[1] == 1, second, 0)]
        plan[f"order{gate}"] = row_order(targets, maps, rows, bits)
    if ends:
        mask = jnp.int32(0)
        for s in sent:
            mask = mask | jnp.left_shift(jnp.int32(1), s)
        plan["post"] = [jnp.where((q < SUB) & ((mask >> q) & 1 == 0), q, -1) for q in aside]
    else:
        plan["post"] = [over, jnp.int32(-1)]
    plan["device"] = []
    rest = jnp.int32(2**TOP - 1)
    for s in sent:
        p = maps[ROWS_B, s]
        p = jnp.where(s >= bits, s, jnp.where(p == over, bits - 2, p))
        plan["device"].append(jnp.left_shift(jnp.int32(1), p - SUB))
        rest = rest & ~plan["device"][-1]
    plan["slot"] = []
    for _ in range(TOP - count):
        lowest = rest & -rest
        plan["slot"].append(lowest)
        rest = rest & ~lowest
    return plan


def end_places(plan, index, swaps, count, maps, bits):
    high = bits + 2
    sent = [swaps[index, j] for j in range(count)]
    post = plan["post"]
    for q in range(bits):
        p = maps[ROWS_B, q]
        p = jnp.where(p == post[0], bits - 2, jnp.where((p == bits - 2) & (post[0] >= 0), post[0], p))
        p = jnp.where(p == post[1], bits - 1, jnp.where((p == bits - 1) & (post[1] >= 0), post[1], p))
        maps[PLACE, q] = p
    maps[PLACE, bits] = jnp.int32(bits)
    maps[PLACE, bits + 1] = jnp.int32(bits + 1)
    places = [maps[PLACE, s] for s in sent]
    for q in range(high):
        p = maps[PLACE, q]
        for place in places:
            p = p - where(place < maps[PLACE, q], 1, 0)
        maps[IN, q] = p
    for j, s in enumerate(sent):
        maps[IN, s] = jnp.int32(high - count + j)
    for q in range(bits):
        maps[LANES, q] = jnp.int32(q)
    plan["last_stage"] = [jnp.where(s < SUB, s, -1) for s in sent]
    plan["last"] = []
    for q in range(SUB, high):
        p = maps[IN, q]
        for j, s in enumerate(plan["last_stage"]):
            p = jnp.where(p == s, high - count + j, p)
        plan["last"].append(jnp.left_shift(jnp.int32(1), p - SUB))


def make_plan(index, gates, swaps, count, maps, bits):
    plan = first_plan(index, gates, maps, bits)
    plan = plan | later_plan(index, gates, swaps, count, maps, bits)
    end_places(plan, index, swaps, count, maps, bits)
    return plan


KEYS = ("stage", "kept", "away", "moved0", "moved1", "moved2", "lanes1", "lanes2", "device", "slot")
KEYS = KEYS + ("back", "post", "last_stage", "last")


def plan_sizes(count, bits):
    sizes = (2, TOP - 2, 2, 2, 2, 2, 2, 2, count, TOP - count, 2, 2, count, TOP)
    return dict(zip(KEYS, sizes))


def write_plan(plan, ref):
    at = 0
    for key in KEYS:
        for value in plan[key]:
            ref[at] = value
            at += 1


def read_plan(ref, count, bits):
    plan, at = {}, 0
    for key, size in plan_sizes(count, bits).items():
        plan[key] = [ref[at + j] for j in range(size)]
        at += size
    return plan


def spread(position, sources, dests):
    total = jnp.zeros_like(position)
    for source, dest in zip(sources, dests):
        total = total | (((position >> source) & 1) << dest)
    return total


def split(value):
    top = value.astype(jnp.bfloat16)
    return top, (value - top.astype(jnp.float32)).astype(jnp.bfloat16)


def prepare_gate(plan, gate, real, imag, out):
    size = real.shape[0]
    bits = size.bit_length() - 1
    lane = lax.broadcasted_iota(jnp.int32, (8, size), 1)
    columns = spread(lane, plan[f"columns{gate}"], range(bits))
    columns = jnp.broadcast_to(columns[0:1, :], (size, size))
    weights = plan[f"order{gate}"]
    row = lax.broadcasted_iota(jnp.int32, (8, size), 0)
    for b in range(SUB):
        lane = lane - ((row >> b) & 1) * weights[b]
    chosen = [jnp.where(lane == first, 1.0, 0.0) for first in combos(weights[SUB:])]
    chosen = jnp.concatenate(chosen, axis=0).astype(jnp.bfloat16)
    parts = []
    for part in (real, imag):
        parts += split(jnp.take_along_axis(part, columns, axis=1))
    moved = jnp.dot(chosen, jnp.concatenate(parts, axis=1), preferred_element_type=jnp.float32)
    moved = moved.astype(jnp.bfloat16)
    re_hi, re_lo, im_hi, im_lo = (moved[:, j * size : (j + 1) * size] for j in range(4))
    for at, re, im in ((0, re_hi, im_hi), (2 * size, re_hi, im_hi), (4 * size, re_lo, im_lo)):
        out[gate, 0:size, at : at + size] = re
        out[gate, 0:size, at + size : at + 2 * size] = -im
        out[gate, size : 2 * size, at : at + size] = im
        out[gate, size : 2 * size, at + size : at + 2 * size] = re


def trade(v0, v1, low, keep0, keep1, index, axis):
    crossed = jnp.take_along_axis(jnp.where(low, v1, v0), index, axis=axis)
    return jnp.where(keep0, v0, crossed), jnp.where(keep1, v1, crossed)


def trade_masks(shape, axis, bit, moved):
    position = lax.broadcasted_iota(jnp.int32, shape, axis)
    value = (position >> bit) & 1
    low = value == 0
    return low, (value & moved) == 0, ((1 - value) & moved) == 0, position ^ jnp.left_shift(jnp.int32(1), bit)


def trade_array(v, masks):
    for j, (a, b) in enumerate(((0, 1), (2, 3), (0, 2), (1, 3))):
        v[a], v[b] = trade(v[a], v[b], *masks[j // 2], 1)


def sublane_stage(state, vreg_bit, bit):
    @pl.when(bit >= 0)
    def _():
        masks = trade_masks(state.shape[2:], 0, jnp.maximum(bit, 0), 1)
        for part in range(state.shape[0]):
            for v in range(state.shape[1]):
                if (v >> vreg_bit) & 1 == 0:
                    w = v | 1 << vreg_bit
                    state[part, v], state[part, w] = trade(state[part, v], state[part, w], *masks, 0)


def block_rows(moved, size):
    a, b = 2 * size, size // 4
    d = []
    for i in range(2):
        d.append([[where(moved[i] == 1, f * a + h * b, h * a + f * b) << i for f in range(2)] for h in range(2)])
    return lambda h, f: d[0][h & 1][f & 1] + d[1][h >> 1][f >> 1]


def multiply(product, left, right, contract):
    size = left.shape[0] // 2
    out = lax.dot_general(left, right, (((1,), (contract,)), ((), ())), preferred_element_type=jnp.float32)
    for a in range(4):
        for part in range(2):
            at = a * 2 * size + part * size
            product[at : at + size, :] = out[part * size : (part + 1) * size, a * size : (a + 1) * size]


def run_round(plan, later, state, weights, by_row, by_lane, product):
    size = state.shape[-1]
    for j in range(2):
        sublane_stage(state, TOP - 2 + j, plan["stage"][j])
    away, kept = combos(plan["away"]), combos(plan["kept"])
    for part in range(2):
        for a in range(4):
            for m in range(len(kept) // 2):
                pair = [state[part, away[a] + kept[2 * m + j]] for j in range(2)]
                high, low = split(jnp.concatenate(pair, axis=0))
                at = part * size + 16 * m
                for row, value in ((at, high), (2 * size + at, low), (4 * size + at, high)):
                    by_row[row : row + 16, a * size : (a + 1) * size] = value
    plan = plan | later()
    multiply(product, weights[0], by_row[...], 0)
    rows = block_rows(plan["moved0"], size)
    for gate in (1, 2):
        masks = [
            trade_masks((16, size), 1, plan[f"lanes{gate}"][j], plan[f"moved{gate}"][j]) for j in range(2)
        ]
        for part in range(2):
            for f in range(4):
                for m in range(size // 64):
                    v = []
                    for h in range(4):
                        at = pl.multiple_of(rows(h, f) + (part * size + 16 * m), 16)
                        v.append(product[pl.ds(at, 16), :])
                    trade_array(v, masks)
                    for a in range(4):
                        high, low = split(v[a])
                        at = a * size + f * (size // 4) + 16 * m
                        for column, value in ((0, high), (2, low), (4, high)):
                            column = (column + part) * size
                            by_lane[at : at + 16, column : column + size] = value
        if gate == 1:
            multiply(product, weights[gate], by_lane[...], 1)
            rows = block_rows(plan["moved1"], size)
    out = lax.dot_general(
        by_lane[...], weights[2], (((1,), (1,)), ((), ())), preferred_element_type=jnp.float32
    )
    masks = [trade_masks((16, size), 1, plan["back"][j], plan["moved2"][j]) for j in range(2)]
    for part in range(2):
        for m in range(size // 16):
            v = [out[a * size + 16 * m : a * size + 16 * m + 16, part * size : (part + 1) * size] for a in range(4)]
            trade_array(v, masks)
            for h in range(4):
                at = h * (size // 8) + 2 * m
                state[part, at : at + 2] = v[h].reshape(2, 8, size)
    for j in range(2):
        sublane_stage(state, TOP - 4 + j, plan["post"][j])
    return plan


def send_chunks(plan, state, me, outs):
    slots = combos(plan["slot"])
    for offset, out in enumerate(outs):
        device = me ^ offset
        base = jnp.int32(0)
        for j, weight in enumerate(plan["device"]):
            base = base + ((device >> j) & 1) * weight
        for part in range(2):
            for j, slot in enumerate(slots):
                at = (part * len(slots) + j) * 8
                out[at : at + 8, :] = state[part, base + slot]


def take_chunks(state, me, chunks):
    slots = state.shape[1] // len(chunks)
    for offset, chunk in zip(far_first(len(chunks)) + [0], chunks):
        device = me ^ offset
        for part in range(2):
            block = chunk[part * slots * 8 : (part + 1) * slots * 8, :]
            state[part, pl.ds(device * slots, slots)] = block.reshape(slots, 8, state.shape[-1])


def first_kernel(axis, count, all_gates, all_swaps, amps, real, imag, *rest):
    devices = 2**count
    outs = rest[:devices]
    gates, swaps, maps, raw, re, im, weights, state, by_row, by_lane, product, sems = rest[devices:]
    piece = amps.shape[0] // 4
    moves = [(all_gates, gates), (all_swaps, swaps), (real.at[0, 0], re.at[0]), (imag.at[0, 0], im.at[0])]
    moves += [(amps.at[pl.ds(piece * j, piece)], raw.at[pl.ds(piece * j, piece)]) for j in range(4)]
    moves += [(real.at[0, pl.ds(1, 2)], re.at[pl.ds(1, 2)]), (imag.at[0, pl.ds(1, 2)], im.at[pl.ds(1, 2)])]
    copies = [pltpu.make_async_copy(source, dest, sems.at[j]) for j, (source, dest) in enumerate(moves)]
    for copy in copies:
        copy.start()
    bits = state.shape[-1].bit_length() - 1
    maps = Maps(maps)
    start_maps(maps, bits)
    for copy in copies[:2]:
        copy.wait()
    plan = first_plan(0, gates, maps, bits)
    for copy in copies[2:4]:
        copy.wait()
    prepare_gate(plan, 0, re[0], im[0], weights)
    for copy in copies[4:]:
        copy.wait()
    for part in range(2):
        for v in range(state.shape[1]):
            state[part, v] = raw[pl.ds(16 * v + part, 8, stride=2), :]

    def later():
        rest = later_plan(0, gates, swaps, count, maps, bits)
        for gate in (1, 2):
            prepare_gate(rest, gate, re[gate], im[gate], weights)
        return rest

    plan = run_round(plan, later, state, weights, by_row, by_lane, product)
    send_chunks(plan, state, lax.axis_index(axis), outs)


def plan_kernel(counts, gates, swaps, real, imag, plan_out, weights, maps, re, im, sems):
    copies = [
        pltpu.make_async_copy(source, dest, sems.at[j])
        for j, (source, dest) in enumerate(((real.at[1], re), (imag.at[1], im)))
    ]
    for copy in copies:
        copy.start()
    bits = re.shape[-1].bit_length() - 1
    maps = Maps(maps)
    start_maps(maps, bits)
    make_plan(0, gates, swaps, counts[0], maps, bits)
    plan = make_plan(1, gates, swaps, counts[1], maps, bits)
    write_plan(plan, plan_out)
    for copy in copies:
        copy.wait()
    for gate in range(3):
        prepare_gate(plan, gate, re[gate], im[gate], weights)


def second_kernel(axes, counts, plan_ref, weights, *rest):
    chunks, rest = rest[: 2 ** counts[0]], rest[2 ** counts[0] :]
    outs, rest = rest[: 2 ** counts[1]], rest[2 ** counts[1] :]
    state, by_row, by_lane, product = rest
    plan = read_plan(plan_ref, counts[1], state.shape[-1].bit_length() - 1)
    take_chunks(state, lax.axis_index(axes[0]), chunks)
    run_round(plan, dict, state, weights, by_row, by_lane, product)
    send_chunks(plan, state, lax.axis_index(axes[1]), outs)


def last_kernel(axis, count, plan_ref, *rest):
    chunks, (out, state) = rest[: 2**count], rest[2**count :]
    plan = read_plan(plan_ref, count, state.shape[-1].bit_length() - 1)
    take_chunks(state, lax.axis_index(axis), chunks)
    for j in range(count):
        sublane_stage(state, TOP - count + j, plan["last_stage"][j])
    for part in range(2):
        for v, source in enumerate(combos(plan["last"])):
            out[pl.ds(16 * v + part, 8, stride=2), :] = state[part, source]


def far_first(devices):
    return sorted(range(1, devices), key=lambda offset: (-(offset >> 1), offset))


def exchange(chunks, axis):
    devices = len(chunks)
    moved = list(chunks)
    for offset in far_first(devices):
        pairs = [(d, d ^ offset) for d in range(devices)]
        moved[offset] = lax.ppermute(chunks[offset], axis, pairs)
    order = far_first(devices) + [0]
    return [pltpu.with_memory_space_constraint(moved[offset], pltpu.VMEM) for offset in order]


def fused(axes, counts, amplitudes, gate_real, gate_imag, gate_qubits, swap_qubits):
    size = gate_real.shape[-1]
    rows = amplitudes.shape[-1] // size
    amps = amplitudes.reshape(2, rows, size).transpose(1, 0, 2).reshape(2 * rows, size)
    f32, bf16, i32 = jnp.float32, jnp.bfloat16, jnp.int32
    smem = pl.BlockSpec(memory_space=pltpu.SMEM)
    vmem = pl.BlockSpec(memory_space=pltpu.VMEM)
    hbm = pl.BlockSpec(memory_space=pl.ANY)
    maps = pltpu.SMEM((9 * (SPARE + 1),), i32)
    gate_qubits = gate_qubits.transpose(1, 0, 2)
    gate = pltpu.VMEM(gate_real.shape[1:], f32)
    operators = (gate_real.shape[1], 2 * size, 6 * size)
    state = pltpu.VMEM((2, rows // 8, 8, size), f32)
    work = [
        state,
        pltpu.VMEM((6 * size, rows), bf16),
        pltpu.VMEM((rows, 6 * size), bf16),
        pltpu.VMEM((2 * rows, size), f32),
    ]
    chunk = [pltpu.VMEM((2 * rows >> count, size), f32) for count in counts]
    sent = pl.pallas_call(
        functools.partial(first_kernel, axes[0], counts[0]),
        out_shape=[chunk[0]] * 2 ** counts[0],
        in_specs=[hbm] * 5,
        out_specs=[vmem] * 2 ** counts[0],
        scratch_shapes=[pltpu.SMEM(gate_qubits.shape, i32), pltpu.SMEM(swap_qubits.shape, i32)]
        + [maps, pltpu.VMEM(amps.shape, f32), gate, gate, pltpu.VMEM(operators, bf16), *work]
        + [pltpu.SemaphoreType.DMA((10,))],
        name="first_round",
    )(gate_qubits, swap_qubits, amps, gate_real, gate_imag)
    plan, weights = pl.pallas_call(
        functools.partial(plan_kernel, counts),
        out_shape=[
            jax.ShapeDtypeStruct((sum(plan_sizes(counts[1], size.bit_length() - 1).values()),), i32),
            pltpu.VMEM(operators, bf16),
        ],
        in_specs=[smem, smem, hbm, hbm],
        out_specs=[smem, vmem],
        scratch_shapes=[maps, gate, gate, pltpu.SemaphoreType.DMA((2,))],
        name="second_plan",
    )(gate_qubits, swap_qubits, gate_real, gate_imag)
    weights = pltpu.with_memory_space_constraint(weights, pltpu.VMEM)
    arrived = exchange(sent, axes[0])
    sent = pl.pallas_call(
        functools.partial(second_kernel, axes, counts),
        out_shape=[chunk[1]] * 2 ** counts[1],
        in_specs=[smem, vmem] + [vmem] * len(arrived),
        out_specs=[vmem] * 2 ** counts[1],
        scratch_shapes=work,
        name="second_round",
    )(plan, weights, *arrived)
    arrived = exchange(sent, axes[1])
    out = pl.pallas_call(
        functools.partial(last_kernel, axes[1], counts[1]),
        out_shape=jax.ShapeDtypeStruct(amps.shape, f32),
        in_specs=[smem] + [vmem] * len(arrived),
        out_specs=vmem,
        scratch_shapes=[state],
        name="last_places",
    )(plan, *arrived)
    return out.reshape(rows, 2, size).transpose(1, 0, 2).reshape(amplitudes.shape)


def program(mesh, *arrays):
    axes = ("row", "col")
    counts = tuple(mesh.shape[axis].bit_length() - 1 for axis in axes)
    amplitudes, gate_real = arrays[:2]
    size = gate_real.shape[-1]
    rounds = gate_real.shape[0] == 2 and gate_real.shape[1] == 3
    known = size == 128 and amplitudes.shape[-1] == 4 * size * size
    if known and rounds and max(counts) <= SUB:
        return fused(axes, counts, *arrays)
    return per_device(*arrays)


def solution(mesh):
    placed = (P("row", "col", None, None), P(), P(), P(), P())
    return jax.shard_map(
        functools.partial(program, mesh),
        mesh=mesh,
        in_specs=placed,
        out_specs=P("row", "col", None, None),
        check_vma=False,
    )
```

```python
import functools

import jax
import jax.numpy as jnp
from jax import lax
from jax.experimental import pallas as pl
from jax.experimental.pallas import tpu as pltpu
from jax.sharding import PartitionSpec as P


def spread_bits(dest, total_bits):
    low_count = total_bits // 2
    high_count = total_bits - low_count

    def table(count, offset):
        position = jnp.arange(2**count, dtype=jnp.int32)
        result = jnp.zeros_like(position)
        for bit_index in range(count):
            result = result + jnp.left_shift(position >> bit_index & 1, dest[offset + bit_index])
        return result

    low_table = table(low_count, 0)
    high_table = table(high_count, low_count)
    return (high_table[:, None] + low_table[None, :]).reshape(-1)


def qubit_maps(chosen, top_count, total_bits):
    qubits = jnp.arange(total_bits, dtype=jnp.int32)
    picked = chosen[:top_count]
    matches = picked[:, None] == qubits[None, :]
    chosen_mask = jnp.any(matches, axis=0)
    slot_top = jnp.sum(
        jnp.where(matches, jnp.arange(top_count, dtype=jnp.int32)[:, None], 0), axis=0
    )
    unchosen = jnp.where(chosen_mask, 0, 1).astype(jnp.int32)
    rest_rank = jnp.cumsum(unchosen) - unchosen
    ordering = jnp.argsort(jnp.where(chosen_mask, total_bits + qubits, qubits))
    low_bits = total_bits - top_count
    forward_dest = jnp.concatenate([ordering[:low_bits], picked])
    backward_dest = jnp.where(chosen_mask, low_bits + slot_top, rest_rank)
    return (spread_bits(forward_dest, total_bits), spread_bits(backward_dest, total_bits))


def per_device(amplitudes, gate_real, gate_imag, gate_qubits, swap_qubits):
    local_size = amplitudes.shape[-1]
    total_bits = local_size.bit_length() - 1
    gate_size = gate_real.shape[-1]
    gate_bits = gate_size.bit_length() - 1
    high_bits = total_bits - gate_bits
    row_count = local_size // gate_size
    current = amplitudes.reshape(2, row_count, gate_size)
    for round_index in range(gate_real.shape[0]):
        for gate_index in range(gate_real.shape[1]):
            forward, backward = qubit_maps(
                gate_qubits[round_index, gate_index], gate_bits, high_bits
            )
            gathered = jnp.take(current, forward, axis=1, mode="clip").reshape(
                2 * gate_size, local_size // gate_size
            )
            real_part = gate_real[round_index, gate_index]
            imag_part = gate_imag[round_index, gate_index]
            operator = jnp.concatenate(
                [
                    jnp.concatenate([real_part, -imag_part], 1),
                    jnp.concatenate([imag_part, real_part], 1),
                ],
                0,
            )
            applied = jnp.dot(
                operator,
                gathered,
                precision=lax.Precision.HIGHEST,
                preferred_element_type=jnp.float32,
            ).reshape(2, row_count, gate_size)
            current = jnp.take(applied, backward, axis=1, mode="clip")
            current = (
                current.reshape(2, row_count // gate_size, gate_size, gate_size)
                .transpose(0, 1, 3, 2)
                .reshape(2, row_count, gate_size)
            )
        if round_index % 2 == 0:
            devices = lax.axis_size("row")
            forward, backward = qubit_maps(
                swap_qubits[round_index], devices.bit_length() - 1, high_bits
            )
            prepared = jnp.take(current, forward, axis=1, mode="clip").reshape(
                2, devices, local_size // devices
            )
            arrived = lax.all_to_all(prepared, "row", split_axis=1, concat_axis=1, tiled=True)
        else:
            devices = lax.axis_size("col")
            forward, backward = qubit_maps(
                swap_qubits[round_index], devices.bit_length() - 1, high_bits
            )
            prepared = jnp.take(current, forward, axis=1, mode="clip").reshape(
                2, devices, local_size // devices
            )
            arrived = lax.all_to_all(prepared, "col", split_axis=1, concat_axis=1, tiled=True)
        current = jnp.take(arrived.reshape(2, row_count, gate_size), backward, axis=1, mode="clip")
    return current.reshape(amplitudes.shape)


SUB = 3
TOP = 6


def combos(weights):
    sums = [jnp.int32(0)]
    for weight in weights:
        sums = sums + [total + weight for total in sums]
    return sums


def where(cond, yes, no):
    return jnp.where(cond, jnp.int32(yes), jnp.int32(no))


def excluded(gates, spot, bits):
    one, two = gates[spot + (bits,)], gates[spot + (bits + 1,)]
    first = where((one == bits) | (two == bits), bits, jnp.where(one == bits + 1, two, one))
    second = where((one == bits + 1) | (two == bits + 1), bits + 1, jnp.where(two == bits, one, two))
    return first, second


def place_targets(first, second, moved, maps, area, bits):
    for q in range(bits):
        maps[area, q] = jnp.int32(q)
    other = where(second == bits - 2, bits + 1, bits - 2)
    maps[area, jnp.where(moved[0] == 1, other, SPARE)] = first
    back = jnp.where((moved[0] == 1) & (second == bits - 2), first, second)
    last = jnp.where((moved[0] == 1) & (first == bits - 1), other, bits - 1)
    maps[area, jnp.where(moved[1] == 1, last, SPARE)] = back
    for j, qubit in enumerate((first, second)):
        maps[area, bits + j] = jnp.int32(bits - 2 + j)
        maps[area, qubit] = jnp.int32(bits - 2 + j)


def row_order(targets, maps, area, bits):
    for j, target in enumerate(targets):
        maps[INVERSE, maps[area, target]] = jnp.int32(1 << j)
    return [maps[INVERSE, b] for b in range(bits)]


IN, LANES, ROWS_A, ROWS_B, ROWS_C, PLACE, POS, INVERSE, HELD = range(9)
SPARE = 15


class Maps:
    def __init__(self, ref):
        self.ref = ref

    def __getitem__(self, at):
        return self.ref[at[0] * (SPARE + 1) + at[1]]

    def __setitem__(self, at, value):
        self.ref[at[0] * (SPARE + 1) + at[1]] = value


def start_maps(maps, bits):
    for area in (IN, LANES):
        for q in range(bits + 2):
            maps[area, q] = jnp.int32(q)


def first_plan(index, gates, maps, bits):
    plan = {}
    high = bits + 2
    spot = (0, index)
    first, second = excluded(gates, spot, bits)
    moved = [where(first != bits, 1, 0), where(second != bits + 1, 1, 0)]
    p0, p1 = (first, second) if index == 0 else (maps[IN, first], maps[IN, second])
    low0, low1 = p0 < SUB, p1 < SUB
    s0 = jnp.where(
        low0,
        jnp.where(low1 | (p1 != bits), p0, -1),
        jnp.where(low1 & (p0 != bits), p1, -1),
    )
    s1 = jnp.where(
        low0,
        jnp.where(low1, p1, jnp.where(p1 == bits, p0, -1)),
        jnp.where(low1 & (p0 == bits), p1, -1),
    )
    plan["stage"] = [s0, s1]
    for q in range(high if index == 0 else 0):
        maps[POS, q] = jnp.int32(q)
    for j, s in enumerate((s0, s1) if index == 0 else ()):
        maps[POS, jnp.where(s >= 0, s, SPARE)] = jnp.int32(bits + j)
        maps[POS, jnp.where(s >= 0, bits + j, SPARE)] = s
    for q in range(high if index > 0 else 0):
        p = maps[IN, q]
        p = jnp.where(p == s0, bits, jnp.where((p == bits) & (s0 >= 0), s0, p))
        p = jnp.where(p == s1, bits + 1, jnp.where((p == bits + 1) & (s1 >= 0), s1, p))
        maps[POS, q] = p
    e0, e1 = maps[POS, first], maps[POS, second]
    lower, upper = jnp.minimum(e0, e1) - SUB, jnp.maximum(e0, e1) - SUB
    plan["kept"] = []
    for j in range(TOP - 2):
        j = j + where(j >= lower, 1, 0)
        j = j + where(j >= upper, 1, 0)
        plan["kept"].append(jnp.left_shift(jnp.int32(1), j))
    plan["away"] = [jnp.left_shift(jnp.int32(1), e0 - SUB), jnp.left_shift(jnp.int32(1), e1 - SUB)]
    targets = [gates[spot + (j,)] for j in range(bits)]
    columns = [maps[POS, target] for target in targets]
    plan["columns0"] = [p - where(e0 < p, 1, 0) - where(e1 < p, 1, 0) for p in columns]
    place_targets(first, second, moved, maps, ROWS_A, bits)
    plan["order0"] = row_order(targets, maps, ROWS_A, bits)
    plan["moved0"] = moved
    return plan


def place_rows(first, second, moved, sent, wanted, maps, bits):
    place_targets(first, second, moved, maps, ROWS_B, bits)
    for q in range(bits):
        maps[HELD, maps[ROWS_B, q]] = jnp.int32(q)
    free = jnp.int32((1 << (bits - 2)) - (1 << SUB))
    free = free | where(moved[0] == 0, 1 << (bits - 2), 0) | where(moved[1] == 0, 1 << (bits - 1), 0)
    over = jnp.int32(-1)
    for q in sent:
        free = free & ~jnp.left_shift(jnp.int32(1), maps[ROWS_B, q])
    for j, q in enumerate(sent + wanted):
        if j == len(sent):
            for other in wanted:
                free = free & ~jnp.left_shift(jnp.int32(1), maps[ROWS_B, other])
        p = maps[ROWS_B, q]
        lowest = free & -free
        fits = (p < SUB) & (free != 0)
        place = jnp.int32(SUB)
        for b in range(SUB + 1, bits):
            place = place + (b - SUB) * ((lowest >> b) & 1)
        held = maps[HELD, place]
        maps[ROWS_B, jnp.where(fits, held, SPARE)] = p
        maps[ROWS_B, jnp.where(fits, q, SPARE)] = place
        if j < len(sent):
            over = jnp.where((p < SUB) & (free == 0), p, over)
        free = jnp.where(fits, free & ~lowest, free)
    return over


def later_plan(index, gates, swaps, count, maps, bits):
    plan = {}
    ends = index + 1 == gates.shape[1]
    sent = [swaps[index, j] for j in range(count)]
    wanted = [] if ends else [gates[0, index + 1, bits + j] for j in range(2)]
    for gate, lanes in ((1, LANES), (2, ROWS_A)):
        spot = (gate, index)
        first, second = excluded(gates, spot, bits)
        moved = [where(first != bits, 1, 0), where(second != bits + 1, 1, 0)]
        l0 = jnp.where(moved[0] == 1, maps[lanes, first], 0)
        l1 = jnp.where(moved[1] == 1, maps[lanes, second], 0)
        maps[lanes, bits] = l0
        maps[lanes, bits + 1] = l1
        plan[f"lanes{gate}"] = [l0, l1]
        targets = [gates[spot + (j,)] for j in range(bits)]
        plan[f"columns{gate}"] = [maps[lanes, target] for target in targets]
        plan[f"moved{gate}"] = moved
        if gate == 1:
            over = place_rows(first, second, moved, sent, wanted, maps, bits)
            rows = ROWS_B
            aside = (first, second)
        else:
            rows = ROWS_C
            for q in range(bits):
                maps[rows, q] = jnp.int32(q)
            maps[rows, bits] = first
            maps[rows, bits + 1] = second
            plan["back"] = [jnp.where(moved[0] == 1, first, 0), jnp.where(moved[1] == 1, second, 0)]
        plan[f"order{gate}"] = row_order(targets, maps, rows, bits)
    if ends:
        mask = jnp.int32(0)
        for s in sent:
            mask = mask | jnp.left_shift(jnp.int32(1), s)
        plan["post"] = [jnp.where((q < SUB) & ((mask >> q) & 1 == 0), q, -1) for q in aside]
    else:
        plan["post"] = [over, jnp.int32(-1)]
    plan["device"] = []
    rest = jnp.int32(2**TOP - 1)
    for s in sent:
        p = maps[ROWS_B, s]
        p = jnp.where(s >= bits, s, jnp.where(p == over, bits - 2, p))
        plan["device"].append(jnp.left_shift(jnp.int32(1), p - SUB))
        rest = rest & ~plan["device"][-1]
    plan["slot"] = []
    for _ in range(TOP - count):
        lowest = rest & -rest
        plan["slot"].append(lowest)
        rest = rest & ~lowest
    return plan


def end_places(plan, index, swaps, count, maps, bits):
    high = bits + 2
    sent = [swaps[index, j] for j in range(count)]
    post = plan["post"]
    for q in range(bits):
        p = maps[ROWS_B, q]
        p = jnp.where(p == post[0], bits - 2, jnp.where((p == bits - 2) & (post[0] >= 0), post[0], p))
        p = jnp.where(p == post[1], bits - 1, jnp.where((p == bits - 1) & (post[1] >= 0), post[1], p))
        maps[PLACE, q] = p
    maps[PLACE, bits] = jnp.int32(bits)
    maps[PLACE, bits + 1] = jnp.int32(bits + 1)
    places = [maps[PLACE, s] for s in sent]
    for q in range(high):
        p = maps[PLACE, q]
        for place in places:
            p = p - where(place < maps[PLACE, q], 1, 0)
        maps[IN, q] = p
    for j, s in enumerate(sent):
        maps[IN, s] = jnp.int32(high - count + j)
    for q in range(bits):
        maps[LANES, q] = jnp.int32(q)
    plan["last_stage"] = [jnp.where(s < SUB, s, -1) for s in sent]
    for q in range(SUB, high):
        p = maps[IN, q]
        for j, s in enumerate(plan["last_stage"]):
            p = jnp.where(p == s, high - count + j, p)
        maps[INVERSE, p - SUB] = jnp.int32(1 << (q - SUB))
    plan["last"] = [maps[INVERSE, j] for j in range(TOP)]


def make_plan(index, gates, swaps, count, maps, bits):
    plan = first_plan(index, gates, maps, bits)
    plan = plan | later_plan(index, gates, swaps, count, maps, bits)
    end_places(plan, index, swaps, count, maps, bits)
    return plan


KEYS = ("stage", "kept", "away", "moved0", "moved1", "moved2", "lanes1", "lanes2", "device", "slot")
KEYS = KEYS + ("back", "post", "last_stage", "last")


def plan_sizes(count, bits):
    sizes = (2, TOP - 2, 2, 2, 2, 2, 2, 2, count, TOP - count, 2, 2, count, TOP)
    return dict(zip(KEYS, sizes))


def write_plan(plan, ref):
    at = 0
    for key in KEYS:
        for value in plan[key]:
            ref[at] = value
            at += 1


def read_plan(ref, count, bits):
    plan, at = {}, 0
    for key, size in plan_sizes(count, bits).items():
        plan[key] = [ref[at + j] for j in range(size)]
        at += size
    return plan


def spread(position, sources, dests):
    total = jnp.zeros_like(position)
    for source, dest in zip(sources, dests):
        total = total | (((position >> source) & 1) << dest)
    return total


def split(value):
    top = value.astype(jnp.bfloat16)
    return top, (value - top.astype(jnp.float32)).astype(jnp.bfloat16)


def prepare_gate(plan, gate, real, imag, out):
    size = real.shape[0]
    bits = size.bit_length() - 1
    lane = lax.broadcasted_iota(jnp.int32, (8, size), 1)
    columns = spread(lane, plan[f"columns{gate}"], range(bits))
    columns = jnp.broadcast_to(columns[0:1, :], (size, size))
    weights = plan[f"order{gate}"]
    row = lax.broadcasted_iota(jnp.int32, (8, size), 0)
    for b in range(SUB):
        lane = lane - ((row >> b) & 1) * weights[b]
    chosen = [jnp.where(lane == first, 1.0, 0.0) for first in combos(weights[SUB:])]
    chosen = jnp.concatenate(chosen, axis=0).astype(jnp.bfloat16)
    parts = []
    for part in (real, imag):
        parts += split(jnp.take_along_axis(part, columns, axis=1))
    moved = jnp.dot(chosen, jnp.concatenate(parts, axis=1), preferred_element_type=jnp.float32)
    moved = moved.astype(jnp.bfloat16)
    re_hi, re_lo, im_hi, im_lo = (moved[:, j * size : (j + 1) * size] for j in range(4))
    for at, re, im in ((0, re_hi, im_hi), (2 * size, re_hi, im_hi), (4 * size, re_lo, im_lo)):
        out[gate, 0:size, at : at + size] = re
        out[gate, 0:size, at + size : at + 2 * size] = -im
        out[gate, size : 2 * size, at : at + size] = im
        out[gate, size : 2 * size, at + size : at + 2 * size] = re


def trade(v0, v1, low, keep0, keep1, index, axis):
    crossed = jnp.take_along_axis(jnp.where(low, v1, v0), index, axis=axis)
    return jnp.where(keep0, v0, crossed), jnp.where(keep1, v1, crossed)


def trade_masks(shape, axis, bit, moved, flip=0):
    position = lax.broadcasted_iota(jnp.int32, shape, axis)
    value = (position >> bit) & 1 ^ flip
    low = value == 0
    return low, (value & moved) == 0, ((1 - value) & moved) == 0, position ^ jnp.left_shift(jnp.int32(1), bit)


def trade_array(v, masks):
    for j, (a, b) in enumerate(((0, 1), (2, 3), (0, 2), (1, 3))):
        v[a], v[b] = trade(v[a], v[b], *masks[j // 2], 1)


def sublane_stage(state, vreg_bit, bit):
    @pl.when(bit >= 0)
    def _():
        masks = trade_masks(state.shape[2:], 0, jnp.maximum(bit, 0), 1)
        for part in range(state.shape[0]):
            for v in range(state.shape[1]):
                if (v >> vreg_bit) & 1 == 0:
                    w = v | 1 << vreg_bit
                    state[part, v], state[part, w] = trade(state[part, v], state[part, w], *masks, 0)


def block_rows(moved, size):
    a, b = 2 * size, size // 4
    d = []
    for i in range(2):
        d.append([[where(moved[i] == 1, f * a + h * b, h * a + f * b) << i for f in range(2)] for h in range(2)])
    return lambda h, f: d[0][h & 1][f & 1] + d[1][h >> 1][f >> 1]


def multiply(product, left, right, contract):
    size = left.shape[0] // 2
    out = lax.dot_general(left, right, (((1,), (contract,)), ((), ())), preferred_element_type=jnp.float32)
    for a in range(4):
        for part in range(2):
            at = a * 2 * size + part * size
            product[at : at + size, :] = out[part * size : (part + 1) * size, a * size : (a + 1) * size]


def run_round(plan, later, state, weights, by_row, by_lane, product):
    size = state.shape[-1]
    for j in range(2):
        sublane_stage(state, TOP - 2 + j, plan["stage"][j])
    away, kept = combos(plan["away"]), combos(plan["kept"])
    for part in range(2):
        for a in range(4):
            for m in range(len(kept) // 2):
                pair = [state[part, away[a] + kept[2 * m + j]] for j in range(2)]
                high, low = split(jnp.concatenate(pair, axis=0))
                at = part * size + 16 * m
                for row, value in ((at, high), (2 * size + at, low), (4 * size + at, high)):
                    by_row[row : row + 16, a * size : (a + 1) * size] = value
    plan = plan | later()
    multiply(product, weights[0], by_row[...], 0)
    rows = block_rows(plan["moved0"], size)
    for gate in (1, 2):
        masks = [
            trade_masks((16, size), 1, plan[f"lanes{gate}"][j], plan[f"moved{gate}"][j]) for j in range(2)
        ]
        for part in range(2):
            for f in range(4):
                for m in range(size // 64):
                    v = []
                    for h in range(4):
                        at = pl.multiple_of(rows(h, f) + (part * size + 16 * m), 16)
                        v.append(product[pl.ds(at, 16), :])
                    trade_array(v, masks)
                    for a in range(4):
                        high, low = split(v[a])
                        at = a * size + f * (size // 4) + 16 * m
                        for column, value in ((0, high), (2, low), (4, high)):
                            column = (column + part) * size
                            by_lane[at : at + 16, column : column + size] = value
        if gate == 1:
            multiply(product, weights[gate], by_lane[...], 1)
            rows = block_rows(plan["moved1"], size)
    out = lax.dot_general(
        by_lane[...], weights[2], (((1,), (1,)), ((), ())), preferred_element_type=jnp.float32
    )
    masks = [trade_masks((16, size), 1, plan["back"][j], plan["moved2"][j]) for j in range(2)]
    for part in range(2):
        for m in range(size // 16):
            v = [out[a * size + 16 * m : a * size + 16 * m + 16, part * size : (part + 1) * size] for a in range(4)]
            trade_array(v, masks)
            for h in range(4):
                at = h * (size // 8) + 2 * m
                state[part, at : at + 2] = v[h].reshape(2, 8, size)
    for j in range(2):
        sublane_stage(state, TOP - 4 + j, plan["post"][j])
    return plan


def turned(offset, turn):
    return offset ^ (3 * turn) if (offset ^ offset >> 1) & 1 else offset


def send_chunks(plan, state, me, turn, outs):
    slots = combos(plan["slot"])
    for offset, out in enumerate(outs):
        device = me ^ turned(offset, turn)
        base = jnp.int32(0)
        for j, weight in enumerate(plan["device"]):
            base = base + ((device >> j) & 1) * weight
        for part in range(2):
            for j, slot in enumerate(slots):
                at = (part * len(slots) + j) * 8
                out[at : at + 8, :] = state[part, base + slot]


def take_chunks(state, me, turn, order, chunks):
    slots = state.shape[1] // len(chunks)
    for offset, chunk in zip(order, chunks):
        device = me ^ turned(offset, turn)
        for part in range(2):
            block = chunk[part * slots * 8 : (part + 1) * slots * 8, :]
            state[part, pl.ds(device * slots, slots)] = block.reshape(slots, 8, state.shape[-1])


def first_kernel(axis, count, all_gates, all_swaps, amps, real, imag, *rest):
    devices = 2**count
    outs = rest[:devices]
    gates, swaps, maps, raw, re, im, weights, state, by_row, by_lane, product, sems = rest[devices:]
    piece = amps.shape[0] // 4
    moves = [(all_gates, gates), (all_swaps, swaps), (real.at[0, 0], re.at[0]), (imag.at[0, 0], im.at[0])]
    moves += [(amps.at[pl.ds(piece * j, piece)], raw.at[pl.ds(piece * j, piece)]) for j in range(4)]
    moves += [(real.at[0, pl.ds(1, 2)], re.at[pl.ds(1, 2)]), (imag.at[0, pl.ds(1, 2)], im.at[pl.ds(1, 2)])]
    copies = [pltpu.make_async_copy(source, dest, sems.at[j]) for j, (source, dest) in enumerate(moves)]
    for copy in copies:
        copy.start()
    bits = state.shape[-1].bit_length() - 1
    maps = Maps(maps)
    start_maps(maps, bits)
    for copy in copies[:2]:
        copy.wait()
    plan = first_plan(0, gates, maps, bits)
    for copy in copies[2:4]:
        copy.wait()
    prepare_gate(plan, 0, re[0], im[0], weights)
    for copy in copies[4:]:
        copy.wait()
    for part in range(2):
        for v in range(state.shape[1]):
            state[part, v] = raw[pl.ds(16 * v + part, 8, stride=2), :]

    def later():
        rest = later_plan(0, gates, swaps, count, maps, bits)
        for gate in (1, 2):
            prepare_gate(rest, gate, re[gate], im[gate], weights)
        return rest

    plan = run_round(plan, later, state, weights, by_row, by_lane, product)
    send_chunks(plan, state, lax.axis_index(axis), 0, outs)


def plan_kernel(counts, gates, swaps, real, imag, plan_out, weights, maps, re, im, sems):
    copies = [
        pltpu.make_async_copy(source, dest, sems.at[j])
        for j, (source, dest) in enumerate(((real.at[1], re), (imag.at[1], im)))
    ]
    for copy in copies:
        copy.start()
    bits = re.shape[-1].bit_length() - 1
    maps = Maps(maps)
    start_maps(maps, bits)
    make_plan(0, gates, swaps, counts[0], maps, bits)
    plan = make_plan(1, gates, swaps, counts[1], maps, bits)
    write_plan(plan, plan_out)
    for copy in copies:
        copy.wait()
    for gate in range(3):
        prepare_gate(plan, gate, re[gate], im[gate], weights)


def second_kernel(axes, counts, plan_ref, weights, *rest):
    chunks, rest = rest[: 2 ** counts[0]], rest[2 ** counts[0] :]
    outs, rest = rest[: 2 ** counts[1]], rest[2 ** counts[1] :]
    state, by_row, by_lane, product = rest
    plan = read_plan(plan_ref, counts[1], state.shape[-1].bit_length() - 1)
    take_chunks(state, lax.axis_index(axes[0]), 0, far_first(len(chunks)), chunks)
    run_round(plan, dict, state, weights, by_row, by_lane, product)
    send_chunks(plan, state, lax.axis_index(axes[1]), lax.axis_index(axes[0]) & 1, outs)


def last_kernel(axes, count, plan_ref, *rest):
    chunks, out = rest[:-1], rest[-1]
    devices, size = len(chunks), out.shape[-1]
    chunks = [chunks[near_first(devices).index(offset)] for offset in range(devices)]
    plan = read_plan(plan_ref, count, size.bit_length() - 1)
    turn, me = lax.axis_index(axes[0]) & 1, lax.axis_index(axes[1])
    masks = []
    for j in range(count):
        bit, mine = plan["last_stage"][j], (me >> j) & 1
        if j < 2:
            bit = jnp.where(turn == 1, plan["last_stage"][1 - j], bit)
            mine = jnp.where(turn == 1, (me >> (1 - j)) & 1, mine)
        masks.append(trade_masks((8, size), 0, jnp.maximum(bit, 0), where(bit >= 0, 1, 0), mine))
    slots = combos(plan["last"][: TOP - count])
    bases = []
    for offset in range(devices):
        device = me ^ turned(offset, turn)
        base = jnp.int32(0)
        for j in range(count):
            base = base + ((device >> j) & 1) * plan["last"][TOP - count + j]
        bases.append(base)
    for part in range(2):
        for m, slot in enumerate(slots):
            at = (part * len(slots) + m) * 8
            v = [chunk[at : at + 8, :] for chunk in chunks]
            for j in range(count):
                for low in range(devices):
                    high = low | 1 << j
                    if low != high:
                        v[low], v[high] = trade(v[low], v[high], *masks[j], 0)
            for base, value in zip(bases, v):
                out[pl.ds(16 * (base + slot) + part, 8, stride=2), :] = value


def far_first(devices):
    return sorted(range(devices), key=lambda offset: (offset == 0, -(offset >> 1), offset))


def near_first(devices):
    return list(reversed(range(devices)))


def exchange(chunks, axis, order):
    devices = len(chunks)
    moved = []
    for offset in order:
        pairs = [(d, d ^ offset) for d in range(devices)]
        moved.append(lax.ppermute(chunks[offset], axis, pairs) if offset else chunks[0])
    return [pltpu.with_memory_space_constraint(chunk, pltpu.VMEM) for chunk in moved]


def exchange_turned(chunks, axes, others, order):
    devices = len(chunks)
    moved = []
    for offset in order:
        pairs = [
            (o * devices + d, o * devices + (d ^ turned(offset, o & 1))) for o in range(others) for d in range(devices)
        ]
        moved.append(lax.ppermute(chunks[offset], axes, pairs) if offset else chunks[0])
    return [pltpu.with_memory_space_constraint(chunk, pltpu.VMEM) for chunk in moved]


def fused(axes, counts, amplitudes, gate_real, gate_imag, gate_qubits, swap_qubits):
    size = gate_real.shape[-1]
    rows = amplitudes.shape[-1] // size
    amps = amplitudes.reshape(2, rows, size).transpose(1, 0, 2).reshape(2 * rows, size)
    f32, bf16, i32 = jnp.float32, jnp.bfloat16, jnp.int32
    smem = pl.BlockSpec(memory_space=pltpu.SMEM)
    vmem = pl.BlockSpec(memory_space=pltpu.VMEM)
    hbm = pl.BlockSpec(memory_space=pl.ANY)
    maps = pltpu.SMEM((9 * (SPARE + 1),), i32)
    gate_qubits = gate_qubits.transpose(1, 0, 2)
    gate = pltpu.VMEM(gate_real.shape[1:], f32)
    operators = (gate_real.shape[1], 2 * size, 6 * size)
    state = pltpu.VMEM((2, rows // 8, 8, size), f32)
    work = [
        state,
        pltpu.VMEM((6 * size, rows), bf16),
        pltpu.VMEM((rows, 6 * size), bf16),
        pltpu.VMEM((2 * rows, size), f32),
    ]
    chunk = [pltpu.VMEM((2 * rows >> count, size), f32) for count in counts]
    sent = pl.pallas_call(
        functools.partial(first_kernel, axes[0], counts[0]),
        out_shape=[chunk[0]] * 2 ** counts[0],
        in_specs=[hbm] * 5,
        out_specs=[vmem] * 2 ** counts[0],
        scratch_shapes=[pltpu.SMEM(gate_qubits.shape, i32), pltpu.SMEM(swap_qubits.shape, i32)]
        + [maps, pltpu.VMEM(amps.shape, f32), gate, gate, pltpu.VMEM(operators, bf16), *work]
        + [pltpu.SemaphoreType.DMA((10,))],
        name="first_round",
    )(gate_qubits, swap_qubits, amps, gate_real, gate_imag)
    plan, weights = pl.pallas_call(
        functools.partial(plan_kernel, counts),
        out_shape=[
            jax.ShapeDtypeStruct((sum(plan_sizes(counts[1], size.bit_length() - 1).values()),), i32),
            pltpu.VMEM(operators, bf16),
        ],
        in_specs=[smem, smem, hbm, hbm],
        out_specs=[smem, vmem],
        scratch_shapes=[maps, gate, gate, pltpu.SemaphoreType.DMA((2,))],
        name="second_plan",
    )(gate_qubits, swap_qubits, gate_real, gate_imag)
    weights = pltpu.with_memory_space_constraint(weights, pltpu.VMEM)
    arrived = exchange(sent, axes[0], far_first(len(sent)))
    sent = pl.pallas_call(
        functools.partial(second_kernel, axes, counts),
        out_shape=[chunk[1]] * 2 ** counts[1],
        in_specs=[smem, vmem] + [vmem] * len(arrived),
        out_specs=[vmem] * 2 ** counts[1],
        scratch_shapes=work,
        name="second_round",
    )(plan, weights, *arrived)
    arrived = exchange_turned(sent, axes, 2 ** counts[0], near_first(len(sent)))
    out = pl.pallas_call(
        functools.partial(last_kernel, axes, counts[1]),
        out_shape=jax.ShapeDtypeStruct(amps.shape, f32),
        in_specs=[smem] + [vmem] * len(arrived),
        out_specs=vmem,
        name="last_places",
    )(plan, *arrived)
    return out.reshape(rows, 2, size).transpose(1, 0, 2).reshape(amplitudes.shape)


def program(mesh, *arrays):
    axes = ("row", "col")
    counts = tuple(mesh.shape[axis].bit_length() - 1 for axis in axes)
    amplitudes, gate_real = arrays[:2]
    size = gate_real.shape[-1]
    rounds = gate_real.shape[0] == 2 and gate_real.shape[1] == 3
    known = size == 128 and amplitudes.shape[-1] == 4 * size * size
    if known and rounds and max(counts) <= SUB and counts[1] > 1:
        return fused(axes, counts, *arrays)
    return per_device(*arrays)


def solution(mesh):
    placed = (P("row", "col", None, None), P(), P(), P(), P())
    return jax.shard_map(
        functools.partial(program, mesh),
        mesh=mesh,
        in_specs=placed,
        out_specs=P("row", "col", None, None),
        check_vma=False,
    )
```

```python
import functools

import jax
import jax.numpy as jnp
from jax import lax
from jax.experimental import pallas as pl
from jax.experimental.pallas import tpu as pltpu
from jax.sharding import PartitionSpec as P


def spread_bits(dest, total_bits):
    low_count = total_bits // 2
    high_count = total_bits - low_count

    def table(count, offset):
        position = jnp.arange(2**count, dtype=jnp.int32)
        result = jnp.zeros_like(position)
        for bit_index in range(count):
            result = result + jnp.left_shift(position >> bit_index & 1, dest[offset + bit_index])
        return result

    low_table = table(low_count, 0)
    high_table = table(high_count, low_count)
    return (high_table[:, None] + low_table[None, :]).reshape(-1)


def qubit_maps(chosen, top_count, total_bits):
    qubits = jnp.arange(total_bits, dtype=jnp.int32)
    picked = chosen[:top_count]
    matches = picked[:, None] == qubits[None, :]
    chosen_mask = jnp.any(matches, axis=0)
    slot_top = jnp.sum(
        jnp.where(matches, jnp.arange(top_count, dtype=jnp.int32)[:, None], 0), axis=0
    )
    unchosen = jnp.where(chosen_mask, 0, 1).astype(jnp.int32)
    rest_rank = jnp.cumsum(unchosen) - unchosen
    ordering = jnp.argsort(jnp.where(chosen_mask, total_bits + qubits, qubits))
    low_bits = total_bits - top_count
    forward_dest = jnp.concatenate([ordering[:low_bits], picked])
    backward_dest = jnp.where(chosen_mask, low_bits + slot_top, rest_rank)
    return (spread_bits(forward_dest, total_bits), spread_bits(backward_dest, total_bits))


def per_device(amplitudes, gate_real, gate_imag, gate_qubits, swap_qubits):
    local_size = amplitudes.shape[-1]
    total_bits = local_size.bit_length() - 1
    gate_size = gate_real.shape[-1]
    gate_bits = gate_size.bit_length() - 1
    high_bits = total_bits - gate_bits
    row_count = local_size // gate_size
    current = amplitudes.reshape(2, row_count, gate_size)
    for round_index in range(gate_real.shape[0]):
        for gate_index in range(gate_real.shape[1]):
            forward, backward = qubit_maps(
                gate_qubits[round_index, gate_index], gate_bits, high_bits
            )
            gathered = jnp.take(current, forward, axis=1, mode="clip").reshape(
                2 * gate_size, local_size // gate_size
            )
            real_part = gate_real[round_index, gate_index]
            imag_part = gate_imag[round_index, gate_index]
            operator = jnp.concatenate(
                [
                    jnp.concatenate([real_part, -imag_part], 1),
                    jnp.concatenate([imag_part, real_part], 1),
                ],
                0,
            )
            applied = jnp.dot(
                operator,
                gathered,
                precision=lax.Precision.HIGHEST,
                preferred_element_type=jnp.float32,
            ).reshape(2, row_count, gate_size)
            current = jnp.take(applied, backward, axis=1, mode="clip")
            current = (
                current.reshape(2, row_count // gate_size, gate_size, gate_size)
                .transpose(0, 1, 3, 2)
                .reshape(2, row_count, gate_size)
            )
        if round_index % 2 == 0:
            devices = lax.axis_size("row")
            forward, backward = qubit_maps(
                swap_qubits[round_index], devices.bit_length() - 1, high_bits
            )
            prepared = jnp.take(current, forward, axis=1, mode="clip").reshape(
                2, devices, local_size // devices
            )
            arrived = lax.all_to_all(prepared, "row", split_axis=1, concat_axis=1, tiled=True)
        else:
            devices = lax.axis_size("col")
            forward, backward = qubit_maps(
                swap_qubits[round_index], devices.bit_length() - 1, high_bits
            )
            prepared = jnp.take(current, forward, axis=1, mode="clip").reshape(
                2, devices, local_size // devices
            )
            arrived = lax.all_to_all(prepared, "col", split_axis=1, concat_axis=1, tiled=True)
        current = jnp.take(arrived.reshape(2, row_count, gate_size), backward, axis=1, mode="clip")
    return current.reshape(amplitudes.shape)


SUB = 3
TOP = 6


def combos(weights):
    sums = [jnp.int32(0)]
    for weight in weights:
        sums = sums + [total + weight for total in sums]
    return sums


def where(cond, yes, no):
    return jnp.where(cond, jnp.int32(yes), jnp.int32(no))


def excluded(gates, spot, bits):
    one, two = gates[spot + (bits,)], gates[spot + (bits + 1,)]
    first = where((one == bits) | (two == bits), bits, jnp.where(one == bits + 1, two, one))
    second = where((one == bits + 1) | (two == bits + 1), bits + 1, jnp.where(two == bits, one, two))
    return first, second


def place_targets(first, second, moved, maps, area, bits):
    for q in range(bits):
        maps[area, q] = jnp.int32(q)
    other = where(second == bits - 2, bits + 1, bits - 2)
    maps[area, jnp.where(moved[0] == 1, other, SPARE)] = first
    back = jnp.where((moved[0] == 1) & (second == bits - 2), first, second)
    last = jnp.where((moved[0] == 1) & (first == bits - 1), other, bits - 1)
    maps[area, jnp.where(moved[1] == 1, last, SPARE)] = back
    for j, qubit in enumerate((first, second)):
        maps[area, bits + j] = jnp.int32(bits - 2 + j)
        maps[area, qubit] = jnp.int32(bits - 2 + j)


def row_order(targets, maps, area, bits):
    for j, target in enumerate(targets):
        maps[INVERSE, maps[area, target]] = jnp.int32(1 << j)
    return [maps[INVERSE, b] for b in range(bits)]


IN, LANES, ROWS_A, ROWS_B, ROWS_C, PLACE, POS, INVERSE, HELD = range(9)
SPARE = 15


class Maps:
    def __init__(self, ref):
        self.ref = ref

    def __getitem__(self, at):
        return self.ref[at[0] * (SPARE + 1) + at[1]]

    def __setitem__(self, at, value):
        self.ref[at[0] * (SPARE + 1) + at[1]] = value


def start_maps(maps, bits):
    for area in (IN, LANES):
        for q in range(bits + 2):
            maps[area, q] = jnp.int32(q)


def first_plan(index, gates, maps, bits):
    plan = {}
    high = bits + 2
    spot = (0, index)
    first, second = excluded(gates, spot, bits)
    moved = [where(first != bits, 1, 0), where(second != bits + 1, 1, 0)]
    p0, p1 = (first, second) if index == 0 else (maps[IN, first], maps[IN, second])
    low0, low1 = p0 < SUB, p1 < SUB
    s0 = jnp.where(
        low0,
        jnp.where(low1 | (p1 != bits), p0, -1),
        jnp.where(low1 & (p0 != bits), p1, -1),
    )
    s1 = jnp.where(
        low0,
        jnp.where(low1, p1, jnp.where(p1 == bits, p0, -1)),
        jnp.where(low1 & (p0 == bits), p1, -1),
    )
    plan["stage"] = [s0, s1]
    for q in range(high if index == 0 else 0):
        maps[POS, q] = jnp.int32(q)
    for j, s in enumerate((s0, s1) if index == 0 else ()):
        maps[POS, jnp.where(s >= 0, s, SPARE)] = jnp.int32(bits + j)
        maps[POS, jnp.where(s >= 0, bits + j, SPARE)] = s
    for q in range(high if index > 0 else 0):
        p = maps[IN, q]
        p = jnp.where(p == s0, bits, jnp.where((p == bits) & (s0 >= 0), s0, p))
        p = jnp.where(p == s1, bits + 1, jnp.where((p == bits + 1) & (s1 >= 0), s1, p))
        maps[POS, q] = p
    e0, e1 = maps[POS, first], maps[POS, second]
    lower, upper = jnp.minimum(e0, e1) - SUB, jnp.maximum(e0, e1) - SUB
    plan["kept"] = []
    for j in range(TOP - 2):
        j = j + where(j >= lower, 1, 0)
        j = j + where(j >= upper, 1, 0)
        plan["kept"].append(jnp.left_shift(jnp.int32(1), j))
    plan["away"] = [jnp.left_shift(jnp.int32(1), e0 - SUB), jnp.left_shift(jnp.int32(1), e1 - SUB)]
    targets = [gates[spot + (j,)] for j in range(bits)]
    columns = [maps[POS, target] for target in targets]
    plan["columns0"] = [p - where(e0 < p, 1, 0) - where(e1 < p, 1, 0) for p in columns]
    place_targets(first, second, moved, maps, ROWS_A, bits)
    plan["order0"] = row_order(targets, maps, ROWS_A, bits)
    plan["moved0"] = moved
    return plan


def place_rows(first, second, moved, sent, wanted, maps, bits):
    place_targets(first, second, moved, maps, ROWS_B, bits)
    for q in range(bits):
        maps[HELD, maps[ROWS_B, q]] = jnp.int32(q)
    free = jnp.int32((1 << (bits - 2)) - (1 << SUB))
    free = free | where(moved[0] == 0, 1 << (bits - 2), 0) | where(moved[1] == 0, 1 << (bits - 1), 0)
    over = jnp.int32(-1)
    for q in sent:
        free = free & ~jnp.left_shift(jnp.int32(1), maps[ROWS_B, q])
    for j, q in enumerate(sent + wanted):
        if j == len(sent):
            for other in wanted:
                free = free & ~jnp.left_shift(jnp.int32(1), maps[ROWS_B, other])
        p = maps[ROWS_B, q]
        lowest = free & -free
        fits = (p < SUB) & (free != 0)
        place = jnp.int32(SUB)
        for b in range(SUB + 1, bits):
            place = place + (b - SUB) * ((lowest >> b) & 1)
        held = maps[HELD, place]
        maps[ROWS_B, jnp.where(fits, held, SPARE)] = p
        maps[ROWS_B, jnp.where(fits, q, SPARE)] = place
        if j < len(sent):
            over = jnp.where((p < SUB) & (free == 0), p, over)
        free = jnp.where(fits, free & ~lowest, free)
    return over


def later_plan(index, gates, swaps, count, maps, bits):
    plan = {}
    ends = index + 1 == gates.shape[1]
    sent = [swaps[index, j] for j in range(count)]
    wanted = [] if ends else [gates[0, index + 1, bits + j] for j in range(2)]
    for gate, lanes in ((1, LANES), (2, ROWS_A)):
        spot = (gate, index)
        first, second = excluded(gates, spot, bits)
        moved = [where(first != bits, 1, 0), where(second != bits + 1, 1, 0)]
        l0 = jnp.where(moved[0] == 1, maps[lanes, first], 0)
        l1 = jnp.where(moved[1] == 1, maps[lanes, second], 0)
        maps[lanes, bits] = l0
        maps[lanes, bits + 1] = l1
        plan[f"lanes{gate}"] = [l0, l1]
        targets = [gates[spot + (j,)] for j in range(bits)]
        plan[f"columns{gate}"] = [maps[lanes, target] for target in targets]
        plan[f"moved{gate}"] = moved
        if gate == 1:
            over = place_rows(first, second, moved, sent, wanted, maps, bits)
            rows = ROWS_B
            aside = (first, second)
        else:
            rows = ROWS_C
            for q in range(bits):
                maps[rows, q] = jnp.int32(q)
            maps[rows, bits] = first
            maps[rows, bits + 1] = second
            plan["back"] = [jnp.where(moved[0] == 1, first, 0), jnp.where(moved[1] == 1, second, 0)]
        plan[f"order{gate}"] = row_order(targets, maps, rows, bits)
    if ends:
        mask = jnp.int32(0)
        for s in sent:
            mask = mask | jnp.left_shift(jnp.int32(1), s)
        plan["post"] = [jnp.where((q < SUB) & ((mask >> q) & 1 == 0), q, -1) for q in aside]
    else:
        plan["post"] = [over, jnp.int32(-1)]
    plan["device"] = []
    rest = jnp.int32(2**TOP - 1)
    for s in sent:
        p = maps[ROWS_B, s]
        p = jnp.where(s >= bits, s, jnp.where(p == over, bits - 2, p))
        plan["device"].append(jnp.left_shift(jnp.int32(1), p - SUB))
        rest = rest & ~plan["device"][-1]
    plan["slot"] = []
    for _ in range(TOP - count):
        lowest = rest & -rest
        plan["slot"].append(lowest)
        rest = rest & ~lowest
    return plan


def end_places(plan, index, swaps, count, maps, bits):
    high = bits + 2
    sent = [swaps[index, j] for j in range(count)]
    post = plan["post"]
    for q in range(bits):
        p = maps[ROWS_B, q]
        p = jnp.where(p == post[0], bits - 2, jnp.where((p == bits - 2) & (post[0] >= 0), post[0], p))
        p = jnp.where(p == post[1], bits - 1, jnp.where((p == bits - 1) & (post[1] >= 0), post[1], p))
        maps[PLACE, q] = p
    maps[PLACE, bits] = jnp.int32(bits)
    maps[PLACE, bits + 1] = jnp.int32(bits + 1)
    places = [maps[PLACE, s] for s in sent]
    for q in range(high):
        p = maps[PLACE, q]
        for place in places:
            p = p - where(place < maps[PLACE, q], 1, 0)
        maps[IN, q] = p
    for j, s in enumerate(sent):
        maps[IN, s] = jnp.int32(high - count + j)
    for q in range(bits):
        maps[LANES, q] = jnp.int32(q)
    plan["last_stage"] = [jnp.where(s < SUB, s, -1) for s in sent]
    for q in range(SUB, high):
        p = maps[IN, q]
        for j, s in enumerate(plan["last_stage"]):
            p = jnp.where(p == s, high - count + j, p)
        maps[INVERSE, p - SUB] = jnp.int32(1 << (q - SUB))
    plan["last"] = [maps[INVERSE, j] for j in range(TOP)]


def make_plan(index, gates, swaps, count, maps, bits):
    plan = first_plan(index, gates, maps, bits)
    plan = plan | later_plan(index, gates, swaps, count, maps, bits)
    end_places(plan, index, swaps, count, maps, bits)
    return plan


KEYS = ("stage", "kept", "away", "moved0", "moved1", "moved2", "lanes1", "lanes2", "device", "slot")
KEYS = KEYS + ("back", "post", "last_stage", "last")


def plan_sizes(count, bits):
    sizes = (2, TOP - 2, 2, 2, 2, 2, 2, 2, count, TOP - count, 2, 2, count, TOP)
    return dict(zip(KEYS, sizes))


def write_plan(plan, ref):
    at = 0
    for key in KEYS:
        for value in plan[key]:
            ref[0, at] = value
            at += 1


def read_plan(ref, count, bits):
    plan, at = {}, 0
    for key, size in plan_sizes(count, bits).items():
        plan[key] = [ref[0, at + j] for j in range(size)]
        at += size
    return plan


def spread(position, sources, dests):
    total = jnp.zeros_like(position)
    for source, dest in zip(sources, dests):
        total = total | (((position >> source) & 1) << dest)
    return total


def split(value):
    top = value.astype(jnp.bfloat16)
    return top, (value - top.astype(jnp.float32)).astype(jnp.bfloat16)


def prepare_gate(plan, gate, real, imag, out):
    size = real.shape[0]
    bits = size.bit_length() - 1
    lane = lax.broadcasted_iota(jnp.int32, (8, size), 1)
    columns = spread(lane, plan[f"columns{gate}"], range(bits))
    columns = jnp.broadcast_to(columns[0:1, :], (size, size))
    weights = plan[f"order{gate}"]
    row = lax.broadcasted_iota(jnp.int32, (8, size), 0)
    for b in range(SUB):
        lane = lane - ((row >> b) & 1) * weights[b]
    chosen = [jnp.where(lane == first, 1.0, 0.0) for first in combos(weights[SUB:])]
    chosen = jnp.concatenate(chosen, axis=0).astype(jnp.bfloat16)
    parts = []
    for part in (real, imag):
        parts += split(jnp.take_along_axis(part, columns, axis=1))
    moved = jnp.dot(chosen, jnp.concatenate(parts, axis=1), preferred_element_type=jnp.float32)
    moved = moved.astype(jnp.bfloat16)
    re_hi, re_lo, im_hi, im_lo = (moved[:, j * size : (j + 1) * size] for j in range(4))
    for at, re, im in ((0, re_hi, im_hi), (2 * size, re_hi, im_hi), (4 * size, re_lo, im_lo)):
        out[gate, 0:size, at : at + size] = re
        out[gate, 0:size, at + size : at + 2 * size] = -im
        out[gate, size : 2 * size, at : at + size] = im
        out[gate, size : 2 * size, at + size : at + 2 * size] = re


def trade(v0, v1, low, keep0, keep1, index, axis):
    crossed = jnp.take_along_axis(jnp.where(low, v1, v0), index, axis=axis)
    return jnp.where(keep0, v0, crossed), jnp.where(keep1, v1, crossed)


def trade_masks(shape, axis, bit, moved, flip=0):
    position = lax.broadcasted_iota(jnp.int32, shape, axis)
    value = (position >> bit) & 1 ^ flip
    low = value == 0
    return low, (value & moved) == 0, ((1 - value) & moved) == 0, position ^ jnp.left_shift(jnp.int32(1), bit)


def trade_array(v, masks):
    for j, (a, b) in enumerate(((0, 1), (2, 3), (0, 2), (1, 3))):
        v[a], v[b] = trade(v[a], v[b], *masks[j // 2], 1)


def sublane_stage(state, vreg_bit, bit):
    @pl.when(bit >= 0)
    def _():
        masks = trade_masks(state.shape[2:], 0, jnp.maximum(bit, 0), 1)
        for part in range(state.shape[0]):
            for v in range(state.shape[1]):
                if (v >> vreg_bit) & 1 == 0:
                    w = v | 1 << vreg_bit
                    state[part, v], state[part, w] = trade(state[part, v], state[part, w], *masks, 0)


def block_rows(moved, size):
    a, b = 2 * size, size // 4
    d = []
    for i in range(2):
        d.append([[where(moved[i] == 1, f * a + h * b, h * a + f * b) << i for f in range(2)] for h in range(2)])
    return lambda h, f: d[0][h & 1][f & 1] + d[1][h >> 1][f >> 1]


def multiply(product, left, right, contract):
    size = left.shape[0] // 2
    out = lax.dot_general(left, right, (((1,), (contract,)), ((), ())), preferred_element_type=jnp.float32)
    for a in range(4):
        for part in range(2):
            at = a * 2 * size + part * size
            product[at : at + size, :] = out[part * size : (part + 1) * size, a * size : (a + 1) * size]


def run_round(plan, later, state, weights, by_row, by_lane, product):
    size = state.shape[-1]
    for j in range(2):
        sublane_stage(state, TOP - 2 + j, plan["stage"][j])
    away, kept = combos(plan["away"]), combos(plan["kept"])
    for part in range(2):
        for a in range(4):
            for m in range(len(kept) // 2):
                pair = [state[part, away[a] + kept[2 * m + j]] for j in range(2)]
                high, low = split(jnp.concatenate(pair, axis=0))
                at = part * size + 16 * m
                for row, value in ((at, high), (2 * size + at, low), (4 * size + at, high)):
                    by_row[row : row + 16, a * size : (a + 1) * size] = value
    plan = plan | later()
    multiply(product, weights[0], by_row[...], 0)
    rows = block_rows(plan["moved0"], size)
    for gate in (1, 2):
        masks = [
            trade_masks((16, size), 1, plan[f"lanes{gate}"][j], plan[f"moved{gate}"][j]) for j in range(2)
        ]
        for part in range(2):
            for f in range(4):
                for m in range(size // 64):
                    v = []
                    for h in range(4):
                        at = pl.multiple_of(rows(h, f) + (part * size + 16 * m), 16)
                        v.append(product[pl.ds(at, 16), :])
                    trade_array(v, masks)
                    for a in range(4):
                        high, low = split(v[a])
                        at = a * size + f * (size // 4) + 16 * m
                        for column, value in ((0, high), (2, low), (4, high)):
                            column = (column + part) * size
                            by_lane[at : at + 16, column : column + size] = value
        if gate == 1:
            multiply(product, weights[gate], by_lane[...], 1)
            rows = block_rows(plan["moved1"], size)
    out = lax.dot_general(
        by_lane[...], weights[2], (((1,), (1,)), ((), ())), preferred_element_type=jnp.float32
    )
    masks = [trade_masks((16, size), 1, plan["back"][j], plan["moved2"][j]) for j in range(2)]
    for part in range(2):
        for m in range(size // 16):
            v = [out[a * size + 16 * m : a * size + 16 * m + 16, part * size : (part + 1) * size] for a in range(4)]
            trade_array(v, masks)
            for h in range(4):
                at = h * (size // 8) + 2 * m
                state[part, at : at + 2] = v[h].reshape(2, 8, size)
    for j in range(2):
        sublane_stage(state, TOP - 4 + j, plan["post"][j])
    return plan


def turned(offset, turn):
    return offset ^ (3 * turn) if (offset ^ offset >> 1) & 1 else offset


def send_chunks(plan, state, me, turn, outs):
    slots = combos(plan["slot"])
    for offset, out in enumerate(outs):
        device = me ^ turned(offset, turn)
        base = jnp.int32(0)
        for j, weight in enumerate(plan["device"]):
            base = base + ((device >> j) & 1) * weight
        for part in range(2):
            for j, slot in enumerate(slots):
                at = (part * len(slots) + j) * 8
                out[at : at + 8, :] = state[part, base + slot]


def take_chunks(state, me, turn, order, chunks):
    slots = state.shape[1] // len(chunks)
    for offset, chunk in zip(order, chunks):
        device = me ^ turned(offset, turn)
        for part in range(2):
            block = chunk[part * slots * 8 : (part + 1) * slots * 8, :]
            state[part, pl.ds(device * slots, slots)] = block.reshape(slots, 8, state.shape[-1])


def first_kernel(axis, count, all_gates, all_swaps, amps, real, imag, *rest):
    devices = 2**count
    outs = rest[:devices]
    gates, swaps, maps, raw, re, im, weights, state, by_row, by_lane, product, sems = rest[devices:]
    piece = amps.shape[0] // 4
    moves = [(all_gates, gates), (all_swaps, swaps), (real.at[0, 0], re.at[0]), (imag.at[0, 0], im.at[0])]
    moves += [(amps.at[pl.ds(piece * j, piece)], raw.at[pl.ds(piece * j, piece)]) for j in range(4)]
    moves += [(real.at[0, pl.ds(1, 2)], re.at[pl.ds(1, 2)]), (imag.at[0, pl.ds(1, 2)], im.at[pl.ds(1, 2)])]
    copies = [pltpu.make_async_copy(source, dest, sems.at[j]) for j, (source, dest) in enumerate(moves)]
    for copy in copies:
        copy.start()
    bits = state.shape[-1].bit_length() - 1
    maps = Maps(maps)
    start_maps(maps, bits)
    for copy in copies[:2]:
        copy.wait()
    plan = first_plan(0, gates, maps, bits)
    for copy in copies[2:4]:
        copy.wait()
    prepare_gate(plan, 0, re[0], im[0], weights)
    for copy in copies[4:]:
        copy.wait()
    for part in range(2):
        for v in range(state.shape[1]):
            state[part, v] = raw[pl.ds(16 * v + part, 8, stride=2), :]

    def later():
        rest = later_plan(0, gates, swaps, count, maps, bits)
        for gate in (1, 2):
            prepare_gate(rest, gate, re[gate], im[gate], weights)
        return rest

    plan = run_round(plan, later, state, weights, by_row, by_lane, product)
    send_chunks(plan, state, lax.axis_index(axis), 0, outs)


def plan_kernel(counts, gates, swaps, real, imag, plan_out, weights, maps, re, im, kept, sems):
    copies = [
        pltpu.make_async_copy(source, dest, sems.at[j])
        for j, (source, dest) in enumerate(((real.at[1], re), (imag.at[1], im)))
    ]
    for copy in copies:
        copy.start()
    bits = re.shape[-1].bit_length() - 1
    maps = Maps(maps)
    start_maps(maps, bits)
    make_plan(0, gates, swaps, counts[0], maps, bits)
    plan = make_plan(1, gates, swaps, counts[1], maps, bits)
    write_plan(plan, kept)
    copies.append(pltpu.make_async_copy(kept, plan_out, sems.at[2]))
    copies[-1].start()
    for copy in copies:
        copy.wait()
    for gate in range(3):
        prepare_gate(plan, gate, re[gate], im[gate], weights)


def second_kernel(axes, counts, plan_ref, weights, *rest):
    chunks, rest = rest[: 2 ** counts[0]], rest[2 ** counts[0] :]
    outs, rest = rest[: 2 ** counts[1]], rest[2 ** counts[1] :]
    state, by_row, by_lane, product, kept, sem = rest
    copy = pltpu.make_async_copy(plan_ref, kept, sem)
    copy.start()
    take_chunks(state, lax.axis_index(axes[0]), 0, far_first(len(chunks)), chunks)
    copy.wait()
    plan = read_plan(kept, counts[1], state.shape[-1].bit_length() - 1)
    run_round(plan, dict, state, weights, by_row, by_lane, product)
    send_chunks(plan, state, lax.axis_index(axes[1]), lax.axis_index(axes[0]) & 1, outs)


def last_kernel(axes, count, plan_ref, *rest):
    chunks, (out, kept, sem) = rest[:-3], rest[-3:]
    copy = pltpu.make_async_copy(plan_ref, kept, sem)
    copy.start()
    devices, size = len(chunks), out.shape[-1]
    chunks = [chunks[near_first(devices).index(offset)] for offset in range(devices)]
    copy.wait()
    plan = read_plan(kept, count, size.bit_length() - 1)
    turn, me = lax.axis_index(axes[0]) & 1, lax.axis_index(axes[1])
    masks = []
    for j in range(count):
        bit, mine = plan["last_stage"][j], (me >> j) & 1
        if j < 2:
            bit = jnp.where(turn == 1, plan["last_stage"][1 - j], bit)
            mine = jnp.where(turn == 1, (me >> (1 - j)) & 1, mine)
        masks.append(trade_masks((8, size), 0, jnp.maximum(bit, 0), where(bit >= 0, 1, 0), mine))
    slots = combos(plan["last"][: TOP - count])
    bases = []
    for offset in range(devices):
        device = me ^ turned(offset, turn)
        base = jnp.int32(0)
        for j in range(count):
            base = base + ((device >> j) & 1) * plan["last"][TOP - count + j]
        bases.append(base)
    for part in range(2):
        for m, slot in enumerate(slots):
            at = (part * len(slots) + m) * 8
            v = [chunk[at : at + 8, :] for chunk in chunks]
            for j in range(count):
                for low in range(devices):
                    high = low | 1 << j
                    if low != high:
                        v[low], v[high] = trade(v[low], v[high], *masks[j], 0)
            for base, value in zip(bases, v):
                out[pl.ds(16 * (base + slot) + part, 8, stride=2), :] = value


def far_first(devices):
    return sorted(range(devices), key=lambda offset: (offset == 0, -(offset >> 1), offset))


def near_first(devices):
    return list(reversed(range(devices)))


def exchange(chunks, axis, order):
    devices = len(chunks)
    moved = []
    for offset in order:
        pairs = [(d, d ^ offset) for d in range(devices)]
        moved.append(lax.ppermute(chunks[offset], axis, pairs) if offset else chunks[0])
    return [pltpu.with_memory_space_constraint(chunk, pltpu.VMEM) for chunk in moved]


def exchange_turned(chunks, axes, others, order):
    devices = len(chunks)
    moved = []
    for offset in order:
        pairs = [
            (o * devices + d, o * devices + (d ^ turned(offset, o & 1))) for o in range(others) for d in range(devices)
        ]
        moved.append(lax.ppermute(chunks[offset], axes, pairs) if offset else chunks[0])
    return [pltpu.with_memory_space_constraint(chunk, pltpu.VMEM) for chunk in moved]


def fused(axes, counts, amplitudes, gate_real, gate_imag, gate_qubits, swap_qubits):
    size = gate_real.shape[-1]
    rows = amplitudes.shape[-1] // size
    amps = amplitudes.reshape(2, rows, size).transpose(1, 0, 2).reshape(2 * rows, size)
    f32, bf16, i32 = jnp.float32, jnp.bfloat16, jnp.int32
    smem = pl.BlockSpec(memory_space=pltpu.SMEM)
    vmem = pl.BlockSpec(memory_space=pltpu.VMEM)
    hbm = pl.BlockSpec(memory_space=pl.ANY)
    maps = pltpu.SMEM((9 * (SPARE + 1),), i32)
    gate_qubits = gate_qubits.transpose(1, 0, 2)
    gate = pltpu.VMEM(gate_real.shape[1:], f32)
    operators = (gate_real.shape[1], 2 * size, 6 * size)
    state = pltpu.VMEM((2, rows // 8, 8, size), f32)
    work = [
        state,
        pltpu.VMEM((6 * size, rows), bf16),
        pltpu.VMEM((rows, 6 * size), bf16),
        pltpu.VMEM((2 * rows, size), f32),
    ]
    chunk = [pltpu.VMEM((2 * rows >> count, size), f32) for count in counts]
    sent = pl.pallas_call(
        functools.partial(first_kernel, axes[0], counts[0]),
        out_shape=[chunk[0]] * 2 ** counts[0],
        in_specs=[hbm] * 5,
        out_specs=[vmem] * 2 ** counts[0],
        scratch_shapes=[pltpu.SMEM(gate_qubits.shape, i32), pltpu.SMEM(swap_qubits.shape, i32)]
        + [maps, pltpu.VMEM(amps.shape, f32), gate, gate, pltpu.VMEM(operators, bf16), *work]
        + [pltpu.SemaphoreType.DMA((10,))],
        name="first_round",
    )(gate_qubits, swap_qubits, amps, gate_real, gate_imag)
    plan, weights = pl.pallas_call(
        functools.partial(plan_kernel, counts),
        out_shape=[
            pltpu.VMEM((1, size), i32),
            pltpu.VMEM(operators, bf16),
        ],
        in_specs=[smem, smem, hbm, hbm],
        out_specs=[vmem, vmem],
        scratch_shapes=[maps, gate, gate, pltpu.SMEM((1, size), i32), pltpu.SemaphoreType.DMA((3,))],
        name="second_plan",
    )(gate_qubits, swap_qubits, gate_real, gate_imag)
    weights = pltpu.with_memory_space_constraint(weights, pltpu.VMEM)
    plan = pltpu.with_memory_space_constraint(plan, pltpu.VMEM)
    arrived = exchange(sent, axes[0], far_first(len(sent)))
    sent = pl.pallas_call(
        functools.partial(second_kernel, axes, counts),
        out_shape=[chunk[1]] * 2 ** counts[1],
        in_specs=[vmem] * (2 + len(arrived)),
        out_specs=[vmem] * 2 ** counts[1],
        scratch_shapes=work + [pltpu.SMEM((1, size), i32), pltpu.SemaphoreType.DMA],
        name="second_round",
    )(plan, weights, *arrived)
    arrived = exchange_turned(sent, axes, 2 ** counts[0], near_first(len(sent)))
    out = pl.pallas_call(
        functools.partial(last_kernel, axes, counts[1]),
        out_shape=jax.ShapeDtypeStruct(amps.shape, f32),
        in_specs=[vmem] * (1 + len(arrived)),
        out_specs=vmem,
        scratch_shapes=[pltpu.SMEM((1, size), i32), pltpu.SemaphoreType.DMA],
        name="last_places",
    )(plan, *arrived)
    return out.reshape(rows, 2, size).transpose(1, 0, 2).reshape(amplitudes.shape)


def program(mesh, *arrays):
    axes = ("row", "col")
    counts = tuple(mesh.shape[axis].bit_length() - 1 for axis in axes)
    amplitudes, gate_real = arrays[:2]
    size = gate_real.shape[-1]
    rounds = gate_real.shape[0] == 2 and gate_real.shape[1] == 3
    known = size == 128 and amplitudes.shape[-1] == 4 * size * size
    if known and rounds and max(counts) <= SUB and counts[1] > 1:
        return fused(axes, counts, *arrays)
    return per_device(*arrays)


def solution(mesh):
    placed = (P("row", "col", None, None), P(), P(), P(), P())
    return jax.shard_map(
        functools.partial(program, mesh),
        mesh=mesh,
        in_specs=placed,
        out_specs=P("row", "col", None, None),
        check_vma=False,
    )
```

```python
import functools

import jax
import jax.numpy as jnp
from jax import lax
from jax.experimental import pallas as pl
from jax.experimental.pallas import tpu as pltpu
from jax.sharding import PartitionSpec as P


def spread_bits(dest, total_bits):
    low_count = total_bits // 2
    high_count = total_bits - low_count

    def table(count, offset):
        position = jnp.arange(2**count, dtype=jnp.int32)
        result = jnp.zeros_like(position)
        for bit_index in range(count):
            result = result + jnp.left_shift(position >> bit_index & 1, dest[offset + bit_index])
        return result

    low_table = table(low_count, 0)
    high_table = table(high_count, low_count)
    return (high_table[:, None] + low_table[None, :]).reshape(-1)


def qubit_maps(chosen, top_count, total_bits):
    qubits = jnp.arange(total_bits, dtype=jnp.int32)
    picked = chosen[:top_count]
    matches = picked[:, None] == qubits[None, :]
    chosen_mask = jnp.any(matches, axis=0)
    slot_top = jnp.sum(
        jnp.where(matches, jnp.arange(top_count, dtype=jnp.int32)[:, None], 0), axis=0
    )
    unchosen = jnp.where(chosen_mask, 0, 1).astype(jnp.int32)
    rest_rank = jnp.cumsum(unchosen) - unchosen
    ordering = jnp.argsort(jnp.where(chosen_mask, total_bits + qubits, qubits))
    low_bits = total_bits - top_count
    forward_dest = jnp.concatenate([ordering[:low_bits], picked])
    backward_dest = jnp.where(chosen_mask, low_bits + slot_top, rest_rank)
    return (spread_bits(forward_dest, total_bits), spread_bits(backward_dest, total_bits))


def per_device(amplitudes, gate_real, gate_imag, gate_qubits, swap_qubits):
    local_size = amplitudes.shape[-1]
    total_bits = local_size.bit_length() - 1
    gate_size = gate_real.shape[-1]
    gate_bits = gate_size.bit_length() - 1
    high_bits = total_bits - gate_bits
    row_count = local_size // gate_size
    current = amplitudes.reshape(2, row_count, gate_size)
    for round_index in range(gate_real.shape[0]):
        for gate_index in range(gate_real.shape[1]):
            forward, backward = qubit_maps(
                gate_qubits[round_index, gate_index], gate_bits, high_bits
            )
            gathered = jnp.take(current, forward, axis=1, mode="clip").reshape(
                2 * gate_size, local_size // gate_size
            )
            real_part = gate_real[round_index, gate_index]
            imag_part = gate_imag[round_index, gate_index]
            operator = jnp.concatenate(
                [
                    jnp.concatenate([real_part, -imag_part], 1),
                    jnp.concatenate([imag_part, real_part], 1),
                ],
                0,
            )
            applied = jnp.dot(
                operator,
                gathered,
                precision=lax.Precision.HIGHEST,
                preferred_element_type=jnp.float32,
            ).reshape(2, row_count, gate_size)
            current = jnp.take(applied, backward, axis=1, mode="clip")
            current = (
                current.reshape(2, row_count // gate_size, gate_size, gate_size)
                .transpose(0, 1, 3, 2)
                .reshape(2, row_count, gate_size)
            )
        if round_index % 2 == 0:
            devices = lax.axis_size("row")
            forward, backward = qubit_maps(
                swap_qubits[round_index], devices.bit_length() - 1, high_bits
            )
            prepared = jnp.take(current, forward, axis=1, mode="clip").reshape(
                2, devices, local_size // devices
            )
            arrived = lax.all_to_all(prepared, "row", split_axis=1, concat_axis=1, tiled=True)
        else:
            devices = lax.axis_size("col")
            forward, backward = qubit_maps(
                swap_qubits[round_index], devices.bit_length() - 1, high_bits
            )
            prepared = jnp.take(current, forward, axis=1, mode="clip").reshape(
                2, devices, local_size // devices
            )
            arrived = lax.all_to_all(prepared, "col", split_axis=1, concat_axis=1, tiled=True)
        current = jnp.take(arrived.reshape(2, row_count, gate_size), backward, axis=1, mode="clip")
    return current.reshape(amplitudes.shape)


SUB = 3
TOP = 6


def combos(weights):
    sums = [jnp.int32(0)]
    for weight in weights:
        sums = sums + [total + weight for total in sums]
    return sums


def where(cond, yes, no):
    return jnp.where(cond, jnp.int32(yes), jnp.int32(no))


def excluded(gates, spot, bits):
    one, two = gates[spot + (bits,)], gates[spot + (bits + 1,)]
    first = where((one == bits) | (two == bits), bits, jnp.where(one == bits + 1, two, one))
    second = where((one == bits + 1) | (two == bits + 1), bits + 1, jnp.where(two == bits, one, two))
    return first, second


def place_targets(first, second, moved, maps, area, bits):
    for q in range(bits):
        maps[area, q] = jnp.int32(q)
    other = where(second == bits - 2, bits + 1, bits - 2)
    maps[area, jnp.where(moved[0] == 1, other, SPARE)] = first
    back = jnp.where((moved[0] == 1) & (second == bits - 2), first, second)
    last = jnp.where((moved[0] == 1) & (first == bits - 1), other, bits - 1)
    maps[area, jnp.where(moved[1] == 1, last, SPARE)] = back
    for j, qubit in enumerate((first, second)):
        maps[area, bits + j] = jnp.int32(bits - 2 + j)
        maps[area, qubit] = jnp.int32(bits - 2 + j)


def row_order(targets, maps, area, bits):
    for j, target in enumerate(targets):
        maps[INVERSE, maps[area, target]] = jnp.int32(1 << j)
    return [maps[INVERSE, b] for b in range(bits)]


IN, LANES, ROWS_A, ROWS_B, ROWS_C, PLACE, POS, INVERSE, HELD = range(9)
SPARE = 15


class Maps:
    def __init__(self, ref):
        self.ref = ref

    def __getitem__(self, at):
        return self.ref[at[0] * (SPARE + 1) + at[1]]

    def __setitem__(self, at, value):
        self.ref[at[0] * (SPARE + 1) + at[1]] = value


def start_maps(maps, bits):
    for area in (IN, LANES):
        for q in range(bits + 2):
            maps[area, q] = jnp.int32(q)


def first_plan(index, gates, maps, bits):
    plan = {}
    high = bits + 2
    spot = (0, index)
    first, second = excluded(gates, spot, bits)
    moved = [where(first != bits, 1, 0), where(second != bits + 1, 1, 0)]
    p0, p1 = (first, second) if index == 0 else (maps[IN, first], maps[IN, second])
    low0, low1 = p0 < SUB, p1 < SUB
    s0 = jnp.where(
        low0,
        jnp.where(low1 | (p1 != bits), p0, -1),
        jnp.where(low1 & (p0 != bits), p1, -1),
    )
    s1 = jnp.where(
        low0,
        jnp.where(low1, p1, jnp.where(p1 == bits, p0, -1)),
        jnp.where(low1 & (p0 == bits), p1, -1),
    )
    plan["stage"] = [s0, s1]
    for q in range(high if index == 0 else 0):
        maps[POS, q] = jnp.int32(q)
    for j, s in enumerate((s0, s1) if index == 0 else ()):
        maps[POS, jnp.where(s >= 0, s, SPARE)] = jnp.int32(bits + j)
        maps[POS, jnp.where(s >= 0, bits + j, SPARE)] = s
    for q in range(high if index > 0 else 0):
        p = maps[IN, q]
        p = jnp.where(p == s0, bits, jnp.where((p == bits) & (s0 >= 0), s0, p))
        p = jnp.where(p == s1, bits + 1, jnp.where((p == bits + 1) & (s1 >= 0), s1, p))
        maps[POS, q] = p
    e0, e1 = maps[POS, first], maps[POS, second]
    lower, upper = jnp.minimum(e0, e1) - SUB, jnp.maximum(e0, e1) - SUB
    plan["kept"] = []
    for j in range(TOP - 2):
        j = j + where(j >= lower, 1, 0)
        j = j + where(j >= upper, 1, 0)
        plan["kept"].append(jnp.left_shift(jnp.int32(1), j))
    plan["away"] = [jnp.left_shift(jnp.int32(1), e0 - SUB), jnp.left_shift(jnp.int32(1), e1 - SUB)]
    targets = [gates[spot + (j,)] for j in range(bits)]
    columns = [maps[POS, target] for target in targets]
    plan["columns0"] = [p - where(e0 < p, 1, 0) - where(e1 < p, 1, 0) for p in columns]
    place_targets(first, second, moved, maps, ROWS_A, bits)
    plan["order0"] = row_order(targets, maps, ROWS_A, bits)
    plan["moved0"] = moved
    return plan


def place_rows(first, second, moved, sent, wanted, maps, bits):
    place_targets(first, second, moved, maps, ROWS_B, bits)
    for q in range(bits):
        maps[HELD, maps[ROWS_B, q]] = jnp.int32(q)
    free = jnp.int32((1 << (bits - 2)) - (1 << SUB))
    free = free | where(moved[0] == 0, 1 << (bits - 2), 0) | where(moved[1] == 0, 1 << (bits - 1), 0)
    over = jnp.int32(-1)
    for q in sent:
        free = free & ~jnp.left_shift(jnp.int32(1), maps[ROWS_B, q])
    for j, q in enumerate(sent + wanted):
        if j == len(sent):
            for other in wanted:
                free = free & ~jnp.left_shift(jnp.int32(1), maps[ROWS_B, other])
        p = maps[ROWS_B, q]
        lowest = free & -free
        fits = (p < SUB) & (free != 0)
        place = jnp.int32(SUB)
        for b in range(SUB + 1, bits):
            place = place + (b - SUB) * ((lowest >> b) & 1)
        held = maps[HELD, place]
        maps[ROWS_B, jnp.where(fits, held, SPARE)] = p
        maps[ROWS_B, jnp.where(fits, q, SPARE)] = place
        if j < len(sent):
            over = jnp.where((p < SUB) & (free == 0), p, over)
        free = jnp.where(fits, free & ~lowest, free)
    return over


def later_plan(index, gates, swaps, count, maps, bits):
    plan = {}
    ends = index + 1 == gates.shape[1]
    sent = [swaps[index, j] for j in range(count)]
    wanted = [] if ends else [gates[0, index + 1, bits + j] for j in range(2)]
    for gate, lanes in ((1, LANES), (2, ROWS_A)):
        spot = (gate, index)
        first, second = excluded(gates, spot, bits)
        moved = [where(first != bits, 1, 0), where(second != bits + 1, 1, 0)]
        l0 = jnp.where(moved[0] == 1, maps[lanes, first], 0)
        l1 = jnp.where(moved[1] == 1, maps[lanes, second], 0)
        maps[lanes, bits] = l0
        maps[lanes, bits + 1] = l1
        plan[f"lanes{gate}"] = [l0, l1]
        targets = [gates[spot + (j,)] for j in range(bits)]
        plan[f"columns{gate}"] = [maps[lanes, target] for target in targets]
        plan[f"moved{gate}"] = moved
        if gate == 1:
            over = place_rows(first, second, moved, sent, wanted, maps, bits)
            rows = ROWS_B
            aside = (first, second)
        else:
            rows = ROWS_C
            for q in range(bits):
                maps[rows, q] = jnp.int32(q)
            maps[rows, bits] = first
            maps[rows, bits + 1] = second
            plan["back"] = [jnp.where(moved[0] == 1, first, 0), jnp.where(moved[1] == 1, second, 0)]
        plan[f"order{gate}"] = row_order(targets, maps, rows, bits)
    if ends:
        mask = jnp.int32(0)
        for s in sent:
            mask = mask | jnp.left_shift(jnp.int32(1), s)
        plan["post"] = [jnp.where((q < SUB) & ((mask >> q) & 1 == 0), q, -1) for q in aside]
    else:
        plan["post"] = [over, jnp.int32(-1)]
    plan["device"] = []
    rest = jnp.int32(2**TOP - 1)
    for s in sent:
        p = maps[ROWS_B, s]
        p = jnp.where(s >= bits, s, jnp.where(p == over, bits - 2, p))
        plan["device"].append(jnp.left_shift(jnp.int32(1), p - SUB))
        rest = rest & ~plan["device"][-1]
    plan["slot"] = []
    for _ in range(TOP - count):
        lowest = rest & -rest
        plan["slot"].append(lowest)
        rest = rest & ~lowest
    return plan


def end_places(plan, index, swaps, count, maps, bits):
    high = bits + 2
    sent = [swaps[index, j] for j in range(count)]
    post = plan["post"]
    for q in range(bits):
        p = maps[ROWS_B, q]
        p = jnp.where(p == post[0], bits - 2, jnp.where((p == bits - 2) & (post[0] >= 0), post[0], p))
        p = jnp.where(p == post[1], bits - 1, jnp.where((p == bits - 1) & (post[1] >= 0), post[1], p))
        maps[PLACE, q] = p
    maps[PLACE, bits] = jnp.int32(bits)
    maps[PLACE, bits + 1] = jnp.int32(bits + 1)
    places = [maps[PLACE, s] for s in sent]
    for q in range(high):
        p = maps[PLACE, q]
        for place in places:
            p = p - where(place < maps[PLACE, q], 1, 0)
        maps[IN, q] = p
    for j, s in enumerate(sent):
        maps[IN, s] = jnp.int32(high - count + j)
    for q in range(bits):
        maps[LANES, q] = jnp.int32(q)
    plan["last_stage"] = [jnp.where(s < SUB, s, -1) for s in sent]
    for q in range(SUB, high):
        p = maps[IN, q]
        for j, s in enumerate(plan["last_stage"]):
            p = jnp.where(p == s, high - count + j, p)
        maps[INVERSE, p - SUB] = jnp.int32(1 << (q - SUB))
    plan["last"] = [maps[INVERSE, j] for j in range(TOP)]


def make_plan(index, gates, swaps, count, maps, bits):
    plan = first_plan(index, gates, maps, bits)
    plan = plan | later_plan(index, gates, swaps, count, maps, bits)
    end_places(plan, index, swaps, count, maps, bits)
    return plan


KEYS = ("stage", "kept", "away", "moved0", "moved1", "moved2", "lanes1", "lanes2", "device", "slot")
KEYS = KEYS + ("back", "post", "last_stage", "last")


def plan_sizes(count, bits):
    sizes = (2, TOP - 2, 2, 2, 2, 2, 2, 2, count, TOP - count, 2, 2, count, TOP)
    return dict(zip(KEYS, sizes))


def write_plan(plan, ref):
    at = 0
    for key in KEYS:
        for value in plan[key]:
            ref[0, at] = value
            at += 1


def read_plan(ref, count, bits):
    plan, at = {}, 0
    for key, size in plan_sizes(count, bits).items():
        plan[key] = [ref[0, at + j] for j in range(size)]
        at += size
    return plan


def spread(position, sources, dests):
    total = jnp.zeros_like(position)
    for source, dest in zip(sources, dests):
        total = total | (((position >> source) & 1) << dest)
    return total


def split(value):
    top = value.astype(jnp.bfloat16)
    return top, (value - top.astype(jnp.float32)).astype(jnp.bfloat16)


def prepare_gate(plan, gate, real, imag, out):
    size = real.shape[0]
    bits = size.bit_length() - 1
    lane = lax.broadcasted_iota(jnp.int32, (8, size), 1)
    columns = spread(lane, plan[f"columns{gate}"], range(bits))
    columns = jnp.broadcast_to(columns[0:1, :], (size, size))
    weights = plan[f"order{gate}"]
    row = lax.broadcasted_iota(jnp.int32, (8, size), 0)
    for b in range(SUB):
        lane = lane - ((row >> b) & 1) * weights[b]
    chosen = [jnp.where(lane == first, 1.0, 0.0) for first in combos(weights[SUB:])]
    chosen = jnp.concatenate(chosen, axis=0).astype(jnp.bfloat16)
    parts = []
    for part in (real, imag):
        parts += split(jnp.take_along_axis(part, columns, axis=1))
    moved = jnp.dot(chosen, jnp.concatenate(parts, axis=1), preferred_element_type=jnp.float32)
    moved = moved.astype(jnp.bfloat16)
    re_hi, re_lo, im_hi, im_lo = (moved[:, j * size : (j + 1) * size] for j in range(4))
    for at, re, im in ((0, re_hi, im_hi), (2 * size, re_hi, im_hi), (4 * size, re_lo, im_lo)):
        out[gate, 0:size, at : at + size] = re
        out[gate, 0:size, at + size : at + 2 * size] = -im
        out[gate, size : 2 * size, at : at + size] = im
        out[gate, size : 2 * size, at + size : at + 2 * size] = re


def trade(v0, v1, low, keep0, keep1, index, axis):
    crossed = jnp.take_along_axis(jnp.where(low, v1, v0), index, axis=axis)
    return jnp.where(keep0, v0, crossed), jnp.where(keep1, v1, crossed)


def trade_masks(shape, axis, bit, moved, flip=0):
    position = lax.broadcasted_iota(jnp.int32, shape, axis)
    value = (position >> bit) & 1 ^ flip
    low = value == 0
    return low, (value & moved) == 0, ((1 - value) & moved) == 0, position ^ jnp.left_shift(jnp.int32(1), bit)


def trade_array(v, masks):
    for j, (a, b) in enumerate(((0, 1), (2, 3), (0, 2), (1, 3))):
        v[a], v[b] = trade(v[a], v[b], *masks[j // 2], 1)


def sublane_stage(state, vreg_bit, bit):
    @pl.when(bit >= 0)
    def _():
        masks = trade_masks(state.shape[2:], 0, jnp.maximum(bit, 0), 1)
        for part in range(state.shape[0]):
            for v in range(state.shape[1]):
                if (v >> vreg_bit) & 1 == 0:
                    w = v | 1 << vreg_bit
                    state[part, v], state[part, w] = trade(state[part, v], state[part, w], *masks, 0)


def block_rows(moved, size):
    a, b = 2 * size, size // 4
    d = []
    for i in range(2):
        d.append([[where(moved[i] == 1, f * a + h * b, h * a + f * b) << i for f in range(2)] for h in range(2)])
    return lambda h, f: d[0][h & 1][f & 1] + d[1][h >> 1][f >> 1]


def multiply(product, left, right, contract):
    size = left.shape[0] // 2
    out = lax.dot_general(left, right, (((1,), (contract,)), ((), ())), preferred_element_type=jnp.float32)
    for a in range(4):
        for part in range(2):
            at = a * 2 * size + part * size
            product[at : at + size, :] = out[part * size : (part + 1) * size, a * size : (a + 1) * size]


def run_round(plan, later, state, weights, by_row, by_lane, product):
    size = state.shape[-1]
    for j in range(2):
        sublane_stage(state, TOP - 2 + j, plan["stage"][j])
    away, kept = combos(plan["away"]), combos(plan["kept"])
    for part in range(2):
        for a in range(4):
            for m in range(len(kept) // 2):
                pair = [state[part, away[a] + kept[2 * m + j]] for j in range(2)]
                high, low = split(jnp.concatenate(pair, axis=0))
                at = part * size + 16 * m
                for row, value in ((at, high), (2 * size + at, low), (4 * size + at, high)):
                    by_row[row : row + 16, a * size : (a + 1) * size] = value
    plan = plan | later()
    multiply(product, weights[0], by_row[...], 0)
    rows = block_rows(plan["moved0"], size)
    for gate in (1, 2):
        masks = [
            trade_masks((16, size), 1, plan[f"lanes{gate}"][j], plan[f"moved{gate}"][j]) for j in range(2)
        ]
        for part in range(2):
            for f in range(4):
                for m in range(size // 64):
                    v = []
                    for h in range(4):
                        at = pl.multiple_of(rows(h, f) + (part * size + 16 * m), 16)
                        v.append(product[pl.ds(at, 16), :])
                    trade_array(v, masks)
                    for a in range(4):
                        high, low = split(v[a])
                        at = a * size + f * (size // 4) + 16 * m
                        for column, value in ((0, high), (2, low), (4, high)):
                            column = (column + part) * size
                            by_lane[at : at + 16, column : column + size] = value
        if gate == 1:
            multiply(product, weights[gate], by_lane[...], 1)
            rows = block_rows(plan["moved1"], size)
    out = lax.dot_general(
        by_lane[...], weights[2], (((1,), (1,)), ((), ())), preferred_element_type=jnp.float32
    )
    masks = [trade_masks((16, size), 1, plan["back"][j], plan["moved2"][j]) for j in range(2)]
    for part in range(2):
        for m in range(size // 16):
            v = [out[a * size + 16 * m : a * size + 16 * m + 16, part * size : (part + 1) * size] for a in range(4)]
            trade_array(v, masks)
            for h in range(4):
                at = h * (size // 8) + 2 * m
                state[part, at : at + 2] = v[h].reshape(2, 8, size)
    for j in range(2):
        sublane_stage(state, TOP - 4 + j, plan["post"][j])
    return plan


def turned(offset, turn):
    return offset ^ (3 * turn) if (offset ^ offset >> 1) & 1 else offset


def send_chunks(plan, state, me, turn, outs):
    slots = combos(plan["slot"])
    for offset, out in enumerate(outs):
        device = me ^ turned(offset, turn)
        base = jnp.int32(0)
        for j, weight in enumerate(plan["device"]):
            base = base + ((device >> j) & 1) * weight
        for part in range(2):
            for j, slot in enumerate(slots):
                at = (part * len(slots) + j) * 8
                out[at : at + 8, :] = state[part, base + slot]


def take_chunks(state, me, turn, order, chunks):
    slots = state.shape[1] // len(chunks)
    for offset, chunk in zip(order, chunks):
        device = me ^ turned(offset, turn)
        for part in range(2):
            block = chunk[part * slots * 8 : (part + 1) * slots * 8, :]
            state[part, pl.ds(device * slots, slots)] = block.reshape(slots, 8, state.shape[-1])


def first_kernel(axis, count, all_gates, all_swaps, amps, real, imag, *rest):
    devices = 2**count
    outs = rest[:devices]
    gates, swaps, maps, raw, re, im, weights, state, by_row, by_lane, product, sems = rest[devices:]
    piece = amps.shape[0] // 4
    moves = [(all_gates, gates), (all_swaps, swaps), (real.at[0, 0], re.at[0]), (imag.at[0, 0], im.at[0])]
    moves += [(amps.at[pl.ds(piece * j, piece)], raw.at[pl.ds(piece * j, piece)]) for j in range(4)]
    moves += [(real.at[0, pl.ds(1, 2)], re.at[pl.ds(1, 2)]), (imag.at[0, pl.ds(1, 2)], im.at[pl.ds(1, 2)])]
    copies = [pltpu.make_async_copy(source, dest, sems.at[j]) for j, (source, dest) in enumerate(moves)]
    for copy in copies:
        copy.start()
    bits = state.shape[-1].bit_length() - 1
    maps = Maps(maps)
    start_maps(maps, bits)
    for copy in copies[:2]:
        copy.wait()
    plan = first_plan(0, gates, maps, bits)
    for copy in copies[2:4]:
        copy.wait()
    prepare_gate(plan, 0, re[0], im[0], weights)
    for copy in copies[4:]:
        copy.wait()
    for part in range(2):
        for v in range(state.shape[1]):
            state[part, v] = raw[pl.ds(16 * v + part, 8, stride=2), :]

    def later():
        rest = later_plan(0, gates, swaps, count, maps, bits)
        for gate in (1, 2):
            prepare_gate(rest, gate, re[gate], im[gate], weights)
        return rest

    plan = run_round(plan, later, state, weights, by_row, by_lane, product)
    send_chunks(plan, state, lax.axis_index(axis), 0, outs)


def plan_kernel(counts, gates, swaps, real, imag, plan_out, weights, maps, re, im, kept, sems):
    copies = [
        pltpu.make_async_copy(source, dest, sems.at[j])
        for j, (source, dest) in enumerate(((real.at[1], re), (imag.at[1], im)))
    ]
    for copy in copies:
        copy.start()
    bits = re.shape[-1].bit_length() - 1
    maps = Maps(maps)
    start_maps(maps, bits)
    make_plan(0, gates, swaps, counts[0], maps, bits)
    plan = make_plan(1, gates, swaps, counts[1], maps, bits)
    write_plan(plan, kept)
    copies.append(pltpu.make_async_copy(kept, plan_out, sems.at[2]))
    copies[-1].start()
    for copy in copies:
        copy.wait()
    for gate in range(3):
        prepare_gate(plan, gate, re[gate], im[gate], weights)


def second_kernel(axes, counts, plan_ref, weights, *rest):
    chunks, rest = rest[: 2 ** counts[0]], rest[2 ** counts[0] :]
    outs, rest = rest[: 2 ** counts[1]], rest[2 ** counts[1] :]
    state, by_row, by_lane, product, kept, sem = rest
    copy = pltpu.make_async_copy(plan_ref, kept, sem)
    copy.start()
    take_chunks(state, lax.axis_index(axes[0]), 0, far_first(len(chunks)), chunks)
    copy.wait()
    plan = read_plan(kept, counts[1], state.shape[-1].bit_length() - 1)
    run_round(plan, dict, state, weights, by_row, by_lane, product)
    send_chunks(plan, state, lax.axis_index(axes[1]), lax.axis_index(axes[0]) & 1, outs)


def last_kernel(axes, count, plan_ref, *rest):
    chunks, (out, kept, sem) = rest[:-3], rest[-3:]
    copy = pltpu.make_async_copy(plan_ref, kept, sem)
    copy.start()
    devices, size = len(chunks), out.shape[-1]
    chunks = [chunks[near_first(devices).index(offset)] for offset in range(devices)]
    copy.wait()
    plan = read_plan(kept, count, size.bit_length() - 1)
    turn, me = lax.axis_index(axes[0]) & 1, lax.axis_index(axes[1])
    masks = []
    for j in range(count):
        bit, mine = plan["last_stage"][j], (me >> j) & 1
        if j < 2:
            bit = jnp.where(turn == 1, plan["last_stage"][1 - j], bit)
            mine = jnp.where(turn == 1, (me >> (1 - j)) & 1, mine)
        masks.append(trade_masks((8, size), 0, jnp.maximum(bit, 0), where(bit >= 0, 1, 0), mine))
    slots = combos(plan["last"][: TOP - count])
    bases = []
    for offset in range(devices):
        device = me ^ turned(offset, turn)
        base = jnp.int32(0)
        for j in range(count):
            base = base + ((device >> j) & 1) * plan["last"][TOP - count + j]
        bases.append(base)
    for part in range(2):
        for m, slot in enumerate(slots):
            at = (part * len(slots) + m) * 8
            v = [chunk[at : at + 8, :] for chunk in chunks]
            for j in range(count):
                for low in range(devices):
                    high = low | 1 << j
                    if low != high:
                        v[low], v[high] = trade(v[low], v[high], *masks[j], 0)
            for base, value in zip(bases, v):
                out[pl.ds(16 * (base + slot) + part, 8, stride=2), :] = value


def far_first(devices):
    def key(offset):
        chip = offset >> 1
        return (offset == 0, chip == 0, bin(chip).count("1"), -chip, offset)

    return sorted(range(devices), key=key)


def near_first(devices):
    return list(reversed(range(devices)))


def exchange(chunks, axis, order):
    devices = len(chunks)
    moved = []
    for offset in order:
        pairs = [(d, d ^ offset) for d in range(devices)]
        moved.append(lax.ppermute(chunks[offset], axis, pairs) if offset else chunks[0])
    return [pltpu.with_memory_space_constraint(chunk, pltpu.VMEM) for chunk in moved]


def exchange_turned(chunks, axes, others, order):
    devices = len(chunks)
    moved = []
    for offset in order:
        pairs = [
            (o * devices + d, o * devices + (d ^ turned(offset, o & 1))) for o in range(others) for d in range(devices)
        ]
        moved.append(lax.ppermute(chunks[offset], axes, pairs) if offset else chunks[0])
    return [pltpu.with_memory_space_constraint(chunk, pltpu.VMEM) for chunk in moved]


def fused(axes, counts, amplitudes, gate_real, gate_imag, gate_qubits, swap_qubits):
    size = gate_real.shape[-1]
    rows = amplitudes.shape[-1] // size
    amps = amplitudes.reshape(2, rows, size).transpose(1, 0, 2).reshape(2 * rows, size)
    f32, bf16, i32 = jnp.float32, jnp.bfloat16, jnp.int32
    smem = pl.BlockSpec(memory_space=pltpu.SMEM)
    vmem = pl.BlockSpec(memory_space=pltpu.VMEM)
    hbm = pl.BlockSpec(memory_space=pl.ANY)
    maps = pltpu.SMEM((9 * (SPARE + 1),), i32)
    gate_qubits = gate_qubits.transpose(1, 0, 2)
    gate = pltpu.VMEM(gate_real.shape[1:], f32)
    operators = (gate_real.shape[1], 2 * size, 6 * size)
    state = pltpu.VMEM((2, rows // 8, 8, size), f32)
    work = [
        state,
        pltpu.VMEM((6 * size, rows), bf16),
        pltpu.VMEM((rows, 6 * size), bf16),
        pltpu.VMEM((2 * rows, size), f32),
    ]
    chunk = [pltpu.VMEM((2 * rows >> count, size), f32) for count in counts]
    sent = pl.pallas_call(
        functools.partial(first_kernel, axes[0], counts[0]),
        out_shape=[chunk[0]] * 2 ** counts[0],
        in_specs=[hbm] * 5,
        out_specs=[vmem] * 2 ** counts[0],
        scratch_shapes=[pltpu.SMEM(gate_qubits.shape, i32), pltpu.SMEM(swap_qubits.shape, i32)]
        + [maps, pltpu.VMEM(amps.shape, f32), gate, gate, pltpu.VMEM(operators, bf16), *work]
        + [pltpu.SemaphoreType.DMA((10,))],
        name="first_round",
    )(gate_qubits, swap_qubits, amps, gate_real, gate_imag)
    plan, weights = pl.pallas_call(
        functools.partial(plan_kernel, counts),
        out_shape=[
            pltpu.VMEM((1, size), i32),
            pltpu.VMEM(operators, bf16),
        ],
        in_specs=[smem, smem, hbm, hbm],
        out_specs=[vmem, vmem],
        scratch_shapes=[maps, gate, gate, pltpu.SMEM((1, size), i32), pltpu.SemaphoreType.DMA((3,))],
        name="second_plan",
    )(gate_qubits, swap_qubits, gate_real, gate_imag)
    weights = pltpu.with_memory_space_constraint(weights, pltpu.VMEM)
    plan = pltpu.with_memory_space_constraint(plan, pltpu.VMEM)
    arrived = exchange(sent, axes[0], far_first(len(sent)))
    sent = pl.pallas_call(
        functools.partial(second_kernel, axes, counts),
        out_shape=[chunk[1]] * 2 ** counts[1],
        in_specs=[vmem] * (2 + len(arrived)),
        out_specs=[vmem] * 2 ** counts[1],
        scratch_shapes=work + [pltpu.SMEM((1, size), i32), pltpu.SemaphoreType.DMA],
        name="second_round",
    )(plan, weights, *arrived)
    arrived = exchange_turned(sent, axes, 2 ** counts[0], near_first(len(sent)))
    out = pl.pallas_call(
        functools.partial(last_kernel, axes, counts[1]),
        out_shape=jax.ShapeDtypeStruct(amps.shape, f32),
        in_specs=[vmem] * (1 + len(arrived)),
        out_specs=vmem,
        scratch_shapes=[pltpu.SMEM((1, size), i32), pltpu.SemaphoreType.DMA],
        name="last_places",
    )(plan, *arrived)
    return out.reshape(rows, 2, size).transpose(1, 0, 2).reshape(amplitudes.shape)


def program(mesh, *arrays):
    axes = ("row", "col")
    counts = tuple(mesh.shape[axis].bit_length() - 1 for axis in axes)
    amplitudes, gate_real = arrays[:2]
    size = gate_real.shape[-1]
    rounds = gate_real.shape[0] == 2 and gate_real.shape[1] == 3
    known = size == 128 and amplitudes.shape[-1] == 4 * size * size
    if known and rounds and max(counts) <= SUB and counts[1] > 1:
        return fused(axes, counts, *arrays)
    return per_device(*arrays)


def solution(mesh):
    placed = (P("row", "col", None, None), P(), P(), P(), P())
    return jax.shard_map(
        functools.partial(program, mesh),
        mesh=mesh,
        in_specs=placed,
        out_specs=P("row", "col", None, None),
        check_vma=False,
    )
```

```python
import functools

import jax
import jax.numpy as jnp
from jax import lax
from jax.experimental import pallas as pl
from jax.experimental.pallas import tpu as pltpu
from jax.sharding import PartitionSpec as P


def spread_bits(dest, total_bits):
    low_count = total_bits // 2
    high_count = total_bits - low_count

    def table(count, offset):
        position = jnp.arange(2**count, dtype=jnp.int32)
        result = jnp.zeros_like(position)
        for bit_index in range(count):
            result = result + jnp.left_shift(position >> bit_index & 1, dest[offset + bit_index])
        return result

    low_table = table(low_count, 0)
    high_table = table(high_count, low_count)
    return (high_table[:, None] + low_table[None, :]).reshape(-1)


def qubit_maps(chosen, top_count, total_bits):
    qubits = jnp.arange(total_bits, dtype=jnp.int32)
    picked = chosen[:top_count]
    matches = picked[:, None] == qubits[None, :]
    chosen_mask = jnp.any(matches, axis=0)
    slot_top = jnp.sum(
        jnp.where(matches, jnp.arange(top_count, dtype=jnp.int32)[:, None], 0), axis=0
    )
    unchosen = jnp.where(chosen_mask, 0, 1).astype(jnp.int32)
    rest_rank = jnp.cumsum(unchosen) - unchosen
    ordering = jnp.argsort(jnp.where(chosen_mask, total_bits + qubits, qubits))
    low_bits = total_bits - top_count
    forward_dest = jnp.concatenate([ordering[:low_bits], picked])
    backward_dest = jnp.where(chosen_mask, low_bits + slot_top, rest_rank)
    return (spread_bits(forward_dest, total_bits), spread_bits(backward_dest, total_bits))


def per_device(amplitudes, gate_real, gate_imag, gate_qubits, swap_qubits):
    local_size = amplitudes.shape[-1]
    total_bits = local_size.bit_length() - 1
    gate_size = gate_real.shape[-1]
    gate_bits = gate_size.bit_length() - 1
    high_bits = total_bits - gate_bits
    row_count = local_size // gate_size
    current = amplitudes.reshape(2, row_count, gate_size)
    for round_index in range(gate_real.shape[0]):
        for gate_index in range(gate_real.shape[1]):
            forward, backward = qubit_maps(
                gate_qubits[round_index, gate_index], gate_bits, high_bits
            )
            gathered = jnp.take(current, forward, axis=1, mode="clip").reshape(
                2 * gate_size, local_size // gate_size
            )
            real_part = gate_real[round_index, gate_index]
            imag_part = gate_imag[round_index, gate_index]
            operator = jnp.concatenate(
                [
                    jnp.concatenate([real_part, -imag_part], 1),
                    jnp.concatenate([imag_part, real_part], 1),
                ],
                0,
            )
            applied = jnp.dot(
                operator,
                gathered,
                precision=lax.Precision.HIGHEST,
                preferred_element_type=jnp.float32,
            ).reshape(2, row_count, gate_size)
            current = jnp.take(applied, backward, axis=1, mode="clip")
            current = (
                current.reshape(2, row_count // gate_size, gate_size, gate_size)
                .transpose(0, 1, 3, 2)
                .reshape(2, row_count, gate_size)
            )
        if round_index % 2 == 0:
            devices = lax.axis_size("row")
            forward, backward = qubit_maps(
                swap_qubits[round_index], devices.bit_length() - 1, high_bits
            )
            prepared = jnp.take(current, forward, axis=1, mode="clip").reshape(
                2, devices, local_size // devices
            )
            arrived = lax.all_to_all(prepared, "row", split_axis=1, concat_axis=1, tiled=True)
        else:
            devices = lax.axis_size("col")
            forward, backward = qubit_maps(
                swap_qubits[round_index], devices.bit_length() - 1, high_bits
            )
            prepared = jnp.take(current, forward, axis=1, mode="clip").reshape(
                2, devices, local_size // devices
            )
            arrived = lax.all_to_all(prepared, "col", split_axis=1, concat_axis=1, tiled=True)
        current = jnp.take(arrived.reshape(2, row_count, gate_size), backward, axis=1, mode="clip")
    return current.reshape(amplitudes.shape)


SUB = 3
TOP = 6


def combos(weights):
    sums = [jnp.int32(0)]
    for weight in weights:
        sums = sums + [total + weight for total in sums]
    return sums


def where(cond, yes, no):
    return jnp.where(cond, jnp.int32(yes), jnp.int32(no))


def excluded(gates, spot, bits):
    one, two = gates[spot + (bits,)], gates[spot + (bits + 1,)]
    first = where((one == bits) | (two == bits), bits, jnp.where(one == bits + 1, two, one))
    second = where((one == bits + 1) | (two == bits + 1), bits + 1, jnp.where(two == bits, one, two))
    return first, second


def place_targets(first, second, moved, maps, area, bits):
    for q in range(bits):
        maps[area, q] = jnp.int32(q)
    other = where(second == bits - 2, bits + 1, bits - 2)
    maps[area, jnp.where(moved[0] == 1, other, SPARE)] = first
    back = jnp.where((moved[0] == 1) & (second == bits - 2), first, second)
    last = jnp.where((moved[0] == 1) & (first == bits - 1), other, bits - 1)
    maps[area, jnp.where(moved[1] == 1, last, SPARE)] = back
    for j, qubit in enumerate((first, second)):
        maps[area, bits + j] = jnp.int32(bits - 2 + j)
        maps[area, qubit] = jnp.int32(bits - 2 + j)


def row_order(targets, maps, area, bits):
    for j, target in enumerate(targets):
        maps[INVERSE, maps[area, target]] = jnp.int32(1 << j)
    return [maps[INVERSE, b] for b in range(bits)]


IN, LANES, ROWS_A, ROWS_B, ROWS_C, PLACE, POS, INVERSE, HELD = range(9)
SPARE = 15


class Maps:
    def __init__(self, ref):
        self.ref = ref

    def __getitem__(self, at):
        return self.ref[at[0] * (SPARE + 1) + at[1]]

    def __setitem__(self, at, value):
        self.ref[at[0] * (SPARE + 1) + at[1]] = value


def start_maps(maps, bits):
    for area in (IN, LANES):
        for q in range(bits + 2):
            maps[area, q] = jnp.int32(q)


def first_plan(index, gates, maps, bits):
    plan = {}
    high = bits + 2
    spot = (0, index)
    first, second = excluded(gates, spot, bits)
    moved = [where(first != bits, 1, 0), where(second != bits + 1, 1, 0)]
    p0, p1 = (first, second) if index == 0 else (maps[IN, first], maps[IN, second])
    low0, low1 = p0 < SUB, p1 < SUB
    s0 = jnp.where(
        low0,
        jnp.where(low1 | (p1 != bits), p0, -1),
        jnp.where(low1 & (p0 != bits), p1, -1),
    )
    s1 = jnp.where(
        low0,
        jnp.where(low1, p1, jnp.where(p1 == bits, p0, -1)),
        jnp.where(low1 & (p0 == bits), p1, -1),
    )
    plan["stage"] = [s0, s1]
    for q in range(high if index == 0 else 0):
        maps[POS, q] = jnp.int32(q)
    for j, s in enumerate((s0, s1) if index == 0 else ()):
        maps[POS, jnp.where(s >= 0, s, SPARE)] = jnp.int32(bits + j)
        maps[POS, jnp.where(s >= 0, bits + j, SPARE)] = s
    for q in range(high if index > 0 else 0):
        p = maps[IN, q]
        p = jnp.where(p == s0, bits, jnp.where((p == bits) & (s0 >= 0), s0, p))
        p = jnp.where(p == s1, bits + 1, jnp.where((p == bits + 1) & (s1 >= 0), s1, p))
        maps[POS, q] = p
    e0, e1 = maps[POS, first], maps[POS, second]
    lower, upper = jnp.minimum(e0, e1) - SUB, jnp.maximum(e0, e1) - SUB
    plan["kept"] = []
    for j in range(TOP - 2):
        j = j + where(j >= lower, 1, 0)
        j = j + where(j >= upper, 1, 0)
        plan["kept"].append(jnp.left_shift(jnp.int32(1), j))
    plan["away"] = [jnp.left_shift(jnp.int32(1), e0 - SUB), jnp.left_shift(jnp.int32(1), e1 - SUB)]
    targets = [gates[spot + (j,)] for j in range(bits)]
    columns = [maps[POS, target] for target in targets]
    plan["columns0"] = [p - where(e0 < p, 1, 0) - where(e1 < p, 1, 0) for p in columns]
    place_targets(first, second, moved, maps, ROWS_A, bits)
    plan["order0"] = row_order(targets, maps, ROWS_A, bits)
    plan["moved0"] = moved
    return plan


def place_rows(first, second, moved, sent, wanted, maps, bits):
    place_targets(first, second, moved, maps, ROWS_B, bits)
    for q in range(bits):
        maps[HELD, maps[ROWS_B, q]] = jnp.int32(q)
    free = jnp.int32((1 << (bits - 2)) - (1 << SUB))
    free = free | where(moved[0] == 0, 1 << (bits - 2), 0) | where(moved[1] == 0, 1 << (bits - 1), 0)
    over = jnp.int32(-1)
    for q in sent:
        free = free & ~jnp.left_shift(jnp.int32(1), maps[ROWS_B, q])
    for j, q in enumerate(sent + wanted):
        if j == len(sent):
            for other in wanted:
                free = free & ~jnp.left_shift(jnp.int32(1), maps[ROWS_B, other])
        p = maps[ROWS_B, q]
        lowest = free & -free
        fits = (p < SUB) & (free != 0)
        place = jnp.int32(SUB)
        for b in range(SUB + 1, bits):
            place = place + (b - SUB) * ((lowest >> b) & 1)
        held = maps[HELD, place]
        maps[ROWS_B, jnp.where(fits, held, SPARE)] = p
        maps[ROWS_B, jnp.where(fits, q, SPARE)] = place
        if j < len(sent):
            over = jnp.where((p < SUB) & (free == 0), p, over)
        free = jnp.where(fits, free & ~lowest, free)
    return over


def later_plan(index, gates, swaps, count, maps, bits):
    plan = {}
    ends = index + 1 == gates.shape[1]
    sent = [swaps[index, j] for j in range(count)]
    wanted = [] if ends else [gates[0, index + 1, bits + j] for j in range(2)]
    for gate, lanes in ((1, LANES), (2, ROWS_A)):
        spot = (gate, index)
        first, second = excluded(gates, spot, bits)
        moved = [where(first != bits, 1, 0), where(second != bits + 1, 1, 0)]
        l0 = jnp.where(moved[0] == 1, maps[lanes, first], 0)
        l1 = jnp.where(moved[1] == 1, maps[lanes, second], 0)
        maps[lanes, bits] = l0
        maps[lanes, bits + 1] = l1
        plan[f"lanes{gate}"] = [l0, l1]
        targets = [gates[spot + (j,)] for j in range(bits)]
        plan[f"columns{gate}"] = [maps[lanes, target] for target in targets]
        plan[f"moved{gate}"] = moved
        if gate == 1:
            over = place_rows(first, second, moved, sent, wanted, maps, bits)
            rows = ROWS_B
            aside = (first, second)
        else:
            rows = ROWS_C
            for q in range(bits):
                maps[rows, q] = jnp.int32(q)
            maps[rows, bits] = first
            maps[rows, bits + 1] = second
            plan["back"] = [jnp.where(moved[0] == 1, first, 0), jnp.where(moved[1] == 1, second, 0)]
        plan[f"order{gate}"] = row_order(targets, maps, rows, bits)
    if ends:
        mask = jnp.int32(0)
        for s in sent:
            mask = mask | jnp.left_shift(jnp.int32(1), s)
        plan["post"] = [jnp.where((q < SUB) & ((mask >> q) & 1 == 0), q, -1) for q in aside]
    else:
        plan["post"] = [over, jnp.int32(-1)]
    plan["device"] = []
    rest = jnp.int32(2**TOP - 1)
    for s in sent:
        p = maps[ROWS_B, s]
        p = jnp.where(s >= bits, s, jnp.where(p == over, bits - 2, p))
        plan["device"].append(jnp.left_shift(jnp.int32(1), p - SUB))
        rest = rest & ~plan["device"][-1]
    plan["slot"] = []
    for _ in range(TOP - count):
        lowest = rest & -rest
        plan["slot"].append(lowest)
        rest = rest & ~lowest
    return plan


def end_places(plan, index, swaps, count, maps, bits):
    high = bits + 2
    sent = [swaps[index, j] for j in range(count)]
    post = plan["post"]
    for q in range(bits):
        p = maps[ROWS_B, q]
        p = jnp.where(p == post[0], bits - 2, jnp.where((p == bits - 2) & (post[0] >= 0), post[0], p))
        p = jnp.where(p == post[1], bits - 1, jnp.where((p == bits - 1) & (post[1] >= 0), post[1], p))
        maps[PLACE, q] = p
    maps[PLACE, bits] = jnp.int32(bits)
    maps[PLACE, bits + 1] = jnp.int32(bits + 1)
    places = [maps[PLACE, s] for s in sent]
    for q in range(high):
        p = maps[PLACE, q]
        for place in places:
            p = p - where(place < maps[PLACE, q], 1, 0)
        maps[IN, q] = p
    for j, s in enumerate(sent):
        maps[IN, s] = jnp.int32(high - count + j)
    for q in range(bits):
        maps[LANES, q] = jnp.int32(q)
    plan["last_stage"] = [jnp.where(s < SUB, s, -1) for s in sent]
    for q in range(SUB, high):
        p = maps[IN, q]
        for j, s in enumerate(plan["last_stage"]):
            p = jnp.where(p == s, high - count + j, p)
        maps[INVERSE, p - SUB] = jnp.int32(1 << (q - SUB))
    plan["last"] = [maps[INVERSE, j] for j in range(TOP)]


def make_plan(index, gates, swaps, count, maps, bits):
    plan = first_plan(index, gates, maps, bits)
    plan = plan | later_plan(index, gates, swaps, count, maps, bits)
    end_places(plan, index, swaps, count, maps, bits)
    return plan


KEYS = ("stage", "kept", "away", "moved0", "moved1", "moved2", "lanes1", "lanes2", "device", "slot")
KEYS = KEYS + ("back", "post", "last_stage", "last")


def plan_sizes(count, bits):
    sizes = (2, TOP - 2, 2, 2, 2, 2, 2, 2, count, TOP - count, 2, 2, count, TOP)
    return dict(zip(KEYS, sizes))


def write_plan(plan, ref):
    at = 0
    for key in KEYS:
        for value in plan[key]:
            ref[0, at] = value
            at += 1


def read_plan(ref, count, bits):
    plan, at = {}, 0
    for key, size in plan_sizes(count, bits).items():
        plan[key] = [ref[0, at + j] for j in range(size)]
        at += size
    return plan


def spread(position, sources, dests):
    total = jnp.zeros_like(position)
    for source, dest in zip(sources, dests):
        total = total | (((position >> source) & 1) << dest)
    return total


def split(value):
    top = value.astype(jnp.bfloat16)
    return top, (value - top.astype(jnp.float32)).astype(jnp.bfloat16)


def prepare_gate(plan, gate, real, imag, out):
    size = real.shape[0]
    bits = size.bit_length() - 1
    lane = lax.broadcasted_iota(jnp.int32, (8, size), 1)
    columns = spread(lane, plan[f"columns{gate}"], range(bits))
    columns = jnp.broadcast_to(columns[0:1, :], (size, size))
    weights = plan[f"order{gate}"]
    row = lax.broadcasted_iota(jnp.int32, (8, size), 0)
    for b in range(SUB):
        lane = lane - ((row >> b) & 1) * weights[b]
    chosen = [jnp.where(lane == first, 1.0, 0.0) for first in combos(weights[SUB:])]
    chosen = jnp.concatenate(chosen, axis=0).astype(jnp.bfloat16)
    parts = []
    for part in (real, imag):
        parts += split(jnp.take_along_axis(part, columns, axis=1))
    moved = jnp.dot(chosen, jnp.concatenate(parts, axis=1), preferred_element_type=jnp.float32)
    moved = moved.astype(jnp.bfloat16)
    re_hi, re_lo, im_hi, im_lo = (moved[:, j * size : (j + 1) * size] for j in range(4))
    for at, re, im in ((0, re_hi, im_hi), (2 * size, re_hi, im_hi), (4 * size, re_lo, im_lo)):
        out[gate, 0:size, at : at + size] = re
        out[gate, 0:size, at + size : at + 2 * size] = -im
        out[gate, size : 2 * size, at : at + size] = im
        out[gate, size : 2 * size, at + size : at + 2 * size] = re


def trade(v0, v1, low, keep0, keep1, index, axis):
    crossed = jnp.take_along_axis(jnp.where(low, v1, v0), index, axis=axis)
    return jnp.where(keep0, v0, crossed), jnp.where(keep1, v1, crossed)


def trade_masks(shape, axis, bit, moved, flip=0):
    position = lax.broadcasted_iota(jnp.int32, shape, axis)
    value = (position >> bit) & 1 ^ flip
    low = value == 0
    return low, (value & moved) == 0, ((1 - value) & moved) == 0, position ^ jnp.left_shift(jnp.int32(1), bit)


def trade_array(v, masks):
    for j, (a, b) in enumerate(((0, 1), (2, 3), (0, 2), (1, 3))):
        v[a], v[b] = trade(v[a], v[b], *masks[j // 2], 1)


def sublane_stage(state, vreg_bit, bit):
    @pl.when(bit >= 0)
    def _():
        masks = trade_masks(state.shape[2:], 0, jnp.maximum(bit, 0), 1)
        for part in range(state.shape[0]):
            for v in range(state.shape[1]):
                if (v >> vreg_bit) & 1 == 0:
                    w = v | 1 << vreg_bit
                    state[part, v], state[part, w] = trade(state[part, v], state[part, w], *masks, 0)


def block_rows(moved, size):
    a, b = 2 * size, size // 4
    d = []
    for i in range(2):
        d.append([[where(moved[i] == 1, f * a + h * b, h * a + f * b) << i for f in range(2)] for h in range(2)])
    return lambda h, f: d[0][h & 1][f & 1] + d[1][h >> 1][f >> 1]


def multiply(product, left, right, contract):
    size = left.shape[0] // 2
    out = lax.dot_general(left, right, (((1,), (contract,)), ((), ())), preferred_element_type=jnp.float32)
    for a in range(4):
        for part in range(2):
            at = a * 2 * size + part * size
            product[at : at + size, :] = out[part * size : (part + 1) * size, a * size : (a + 1) * size]


def run_round(plan, later, state, weights, by_row, by_lane, product):
    size = state.shape[-1]
    for j in range(2):
        sublane_stage(state, TOP - 2 + j, plan["stage"][j])
    away, kept = combos(plan["away"]), combos(plan["kept"])
    for part in range(2):
        for a in range(4):
            for m in range(len(kept) // 2):
                pair = [state[part, away[a] + kept[2 * m + j]] for j in range(2)]
                high, low = split(jnp.concatenate(pair, axis=0))
                at = part * size + 16 * m
                for row, value in ((at, high), (2 * size + at, low), (4 * size + at, high)):
                    by_row[row : row + 16, a * size : (a + 1) * size] = value
    plan = plan | later()
    multiply(product, weights[0], by_row[...], 0)
    rows = block_rows(plan["moved0"], size)
    for gate in (1, 2):
        masks = [
            trade_masks((16, size), 1, plan[f"lanes{gate}"][j], plan[f"moved{gate}"][j]) for j in range(2)
        ]
        for part in range(2):
            for f in range(4):
                for m in range(size // 64):
                    v = []
                    for h in range(4):
                        at = pl.multiple_of(rows(h, f) + (part * size + 16 * m), 16)
                        v.append(product[pl.ds(at, 16), :])
                    trade_array(v, masks)
                    for a in range(4):
                        high, low = split(v[a])
                        at = a * size + f * (size // 4) + 16 * m
                        for column, value in ((0, high), (2, low), (4, high)):
                            column = (column + part) * size
                            by_lane[at : at + 16, column : column + size] = value
        if gate == 1:
            multiply(product, weights[gate], by_lane[...], 1)
            rows = block_rows(plan["moved1"], size)
    out = lax.dot_general(
        by_lane[...], weights[2], (((1,), (1,)), ((), ())), preferred_element_type=jnp.float32
    )
    masks = [trade_masks((16, size), 1, plan["back"][j], plan["moved2"][j]) for j in range(2)]
    for part in range(2):
        for m in range(size // 16):
            v = [out[a * size + 16 * m : a * size + 16 * m + 16, part * size : (part + 1) * size] for a in range(4)]
            trade_array(v, masks)
            for h in range(4):
                at = h * (size // 8) + 2 * m
                state[part, at : at + 2] = v[h].reshape(2, 8, size)
    for j in range(2):
        sublane_stage(state, TOP - 4 + j, plan["post"][j])
    return plan


def turned(offset, turn):
    return offset ^ (3 * turn) if (offset ^ offset >> 1) & 1 else offset


def send_chunks(plan, state, me, turn, outs):
    slots = combos(plan["slot"])
    for offset, out in enumerate(outs):
        device = me ^ turned(offset, turn)
        base = jnp.int32(0)
        for j, weight in enumerate(plan["device"]):
            base = base + ((device >> j) & 1) * weight
        for part in range(2):
            for j, slot in enumerate(slots):
                at = (part * len(slots) + j) * 8
                out[at : at + 8, :] = state[part, base + slot]


def take_chunks(state, me, turn, order, chunks):
    slots = state.shape[1] // len(chunks)
    for offset, chunk in zip(order, chunks):
        device = me ^ turned(offset, turn)
        for part in range(2):
            block = chunk[part * slots * 8 : (part + 1) * slots * 8, :]
            state[part, pl.ds(device * slots, slots)] = block.reshape(slots, 8, state.shape[-1])


def first_kernel(axis, count, all_gates, all_swaps, amps, real, imag, *rest):
    devices = 2**count
    outs = rest[:devices]
    gates, swaps, maps, raw, re, im, weights, state, by_row, by_lane, product, sems = rest[devices:]
    piece = amps.shape[0] // 4
    moves = [(all_gates, gates), (all_swaps, swaps), (real.at[0, 0], re.at[0]), (imag.at[0, 0], im.at[0])]
    moves += [(amps.at[pl.ds(piece * j, piece)], raw.at[pl.ds(piece * j, piece)]) for j in range(4)]
    moves += [(real.at[0, pl.ds(1, 2)], re.at[pl.ds(1, 2)]), (imag.at[0, pl.ds(1, 2)], im.at[pl.ds(1, 2)])]
    copies = [pltpu.make_async_copy(source, dest, sems.at[j]) for j, (source, dest) in enumerate(moves)]
    for copy in copies:
        copy.start()
    bits = state.shape[-1].bit_length() - 1
    maps = Maps(maps)
    start_maps(maps, bits)
    for copy in copies[:2]:
        copy.wait()
    plan = first_plan(0, gates, maps, bits)
    for copy in copies[2:4]:
        copy.wait()
    prepare_gate(plan, 0, re[0], im[0], weights)
    for copy in copies[4:]:
        copy.wait()
    for part in range(2):
        for v in range(state.shape[1]):
            state[part, v] = raw[pl.ds(16 * v + part, 8, stride=2), :]

    def later():
        rest = later_plan(0, gates, swaps, count, maps, bits)
        for gate in (1, 2):
            prepare_gate(rest, gate, re[gate], im[gate], weights)
        return rest

    plan = run_round(plan, later, state, weights, by_row, by_lane, product)
    send_chunks(plan, state, lax.axis_index(axis), 0, outs)


def plan_kernel(counts, gates, swaps, real, imag, plan_out, weights, maps, re, im, kept, sems):
    copies = [
        pltpu.make_async_copy(source, dest, sems.at[j])
        for j, (source, dest) in enumerate(((real.at[1], re), (imag.at[1], im)))
    ]
    for copy in copies:
        copy.start()
    bits = re.shape[-1].bit_length() - 1
    maps = Maps(maps)
    start_maps(maps, bits)
    make_plan(0, gates, swaps, counts[0], maps, bits)
    plan = make_plan(1, gates, swaps, counts[1], maps, bits)
    write_plan(plan, kept)
    copies.append(pltpu.make_async_copy(kept, plan_out, sems.at[2]))
    copies[-1].start()
    for copy in copies:
        copy.wait()
    for gate in range(3):
        prepare_gate(plan, gate, re[gate], im[gate], weights)


def second_kernel(axes, counts, plan_ref, weights, *rest):
    chunks, rest = rest[: 2 ** counts[0]], rest[2 ** counts[0] :]
    outs, rest = rest[: 2 ** counts[1]], rest[2 ** counts[1] :]
    state, by_row, by_lane, product, kept, sem = rest
    copy = pltpu.make_async_copy(plan_ref, kept, sem)
    copy.start()
    take_chunks(state, lax.axis_index(axes[0]), 0, far_first(len(chunks)), chunks)
    copy.wait()
    plan = read_plan(kept, counts[1], state.shape[-1].bit_length() - 1)
    run_round(plan, dict, state, weights, by_row, by_lane, product)
    send_chunks(plan, state, lax.axis_index(axes[1]), lax.axis_index(axes[0]) & 1, outs)


def last_kernel(axes, count, plan_ref, *rest):
    chunks, (out, kept, sem) = rest[:-3], rest[-3:]
    copy = pltpu.make_async_copy(plan_ref, kept, sem)
    copy.start()
    devices, size = len(chunks), out.shape[-1]
    chunks = [chunks[near_first(devices).index(offset)] for offset in range(devices)]
    copy.wait()
    plan = read_plan(kept, count, size.bit_length() - 1)
    turn, me = lax.axis_index(axes[0]) & 1, lax.axis_index(axes[1])
    masks = []
    for j in range(count):
        bit, mine = plan["last_stage"][j], (me >> j) & 1
        if j < 2:
            bit = jnp.where(turn == 1, plan["last_stage"][1 - j], bit)
            mine = jnp.where(turn == 1, (me >> (1 - j)) & 1, mine)
        masks.append(trade_masks((8, size), 0, jnp.maximum(bit, 0), where(bit >= 0, 1, 0), mine))
    slots = combos(plan["last"][: TOP - count])
    bases = []
    for offset in range(devices):
        device = me ^ turned(offset, turn)
        base = jnp.int32(0)
        for j in range(count):
            base = base + ((device >> j) & 1) * plan["last"][TOP - count + j]
        bases.append(base)
    for part in range(2):
        for m, slot in enumerate(slots):
            at = (part * len(slots) + m) * 8
            v = [chunk[at : at + 8, :] for chunk in chunks]
            for j in range(count):
                for low in range(devices):
                    high = low | 1 << j
                    if low != high:
                        v[low], v[high] = trade(v[low], v[high], *masks[j], 0)
            for base, value in zip(bases, v):
                out[pl.ds(16 * (base + slot) + part, 8, stride=2), :] = value


def far_first(devices):
    def key(offset):
        chip = offset >> 1
        return (offset == 0, chip == 0, bin(chip).count("1"), offset & 1, -chip)

    return sorted(range(devices), key=key)


def near_first(devices):
    return list(reversed(range(devices)))


def exchange(chunks, axis, order):
    devices = len(chunks)
    moved = []
    for offset in order:
        pairs = [(d, d ^ offset) for d in range(devices)]
        moved.append(lax.ppermute(chunks[offset], axis, pairs) if offset else chunks[0])
    return [pltpu.with_memory_space_constraint(chunk, pltpu.VMEM) for chunk in moved]


def exchange_turned(chunks, axes, others, order):
    devices = len(chunks)
    moved = []
    for offset in order:
        pairs = [
            (o * devices + d, o * devices + (d ^ turned(offset, o & 1))) for o in range(others) for d in range(devices)
        ]
        moved.append(lax.ppermute(chunks[offset], axes, pairs) if offset else chunks[0])
    return [pltpu.with_memory_space_constraint(chunk, pltpu.VMEM) for chunk in moved]


def fused(axes, counts, amplitudes, gate_real, gate_imag, gate_qubits, swap_qubits):
    size = gate_real.shape[-1]
    rows = amplitudes.shape[-1] // size
    amps = amplitudes.reshape(2, rows, size).transpose(1, 0, 2).reshape(2 * rows, size)
    f32, bf16, i32 = jnp.float32, jnp.bfloat16, jnp.int32
    smem = pl.BlockSpec(memory_space=pltpu.SMEM)
    vmem = pl.BlockSpec(memory_space=pltpu.VMEM)
    hbm = pl.BlockSpec(memory_space=pl.ANY)
    maps = pltpu.SMEM((9 * (SPARE + 1),), i32)
    gate_qubits = gate_qubits.transpose(1, 0, 2)
    gate = pltpu.VMEM(gate_real.shape[1:], f32)
    operators = (gate_real.shape[1], 2 * size, 6 * size)
    state = pltpu.VMEM((2, rows // 8, 8, size), f32)
    work = [
        state,
        pltpu.VMEM((6 * size, rows), bf16),
        pltpu.VMEM((rows, 6 * size), bf16),
        pltpu.VMEM((2 * rows, size), f32),
    ]
    chunk = [pltpu.VMEM((2 * rows >> count, size), f32) for count in counts]
    sent = pl.pallas_call(
        functools.partial(first_kernel, axes[0], counts[0]),
        out_shape=[chunk[0]] * 2 ** counts[0],
        in_specs=[hbm] * 5,
        out_specs=[vmem] * 2 ** counts[0],
        scratch_shapes=[pltpu.SMEM(gate_qubits.shape, i32), pltpu.SMEM(swap_qubits.shape, i32)]
        + [maps, pltpu.VMEM(amps.shape, f32), gate, gate, pltpu.VMEM(operators, bf16), *work]
        + [pltpu.SemaphoreType.DMA((10,))],
        name="first_round",
    )(gate_qubits, swap_qubits, amps, gate_real, gate_imag)
    plan, weights = pl.pallas_call(
        functools.partial(plan_kernel, counts),
        out_shape=[
            pltpu.VMEM((1, size), i32),
            pltpu.VMEM(operators, bf16),
        ],
        in_specs=[smem, smem, hbm, hbm],
        out_specs=[vmem, vmem],
        scratch_shapes=[maps, gate, gate, pltpu.SMEM((1, size), i32), pltpu.SemaphoreType.DMA((3,))],
        name="second_plan",
    )(gate_qubits, swap_qubits, gate_real, gate_imag)
    weights = pltpu.with_memory_space_constraint(weights, pltpu.VMEM)
    plan = pltpu.with_memory_space_constraint(plan, pltpu.VMEM)
    arrived = exchange(sent, axes[0], far_first(len(sent)))
    sent = pl.pallas_call(
        functools.partial(second_kernel, axes, counts),
        out_shape=[chunk[1]] * 2 ** counts[1],
        in_specs=[vmem] * (2 + len(arrived)),
        out_specs=[vmem] * 2 ** counts[1],
        scratch_shapes=work + [pltpu.SMEM((1, size), i32), pltpu.SemaphoreType.DMA],
        name="second_round",
    )(plan, weights, *arrived)
    arrived = exchange_turned(sent, axes, 2 ** counts[0], near_first(len(sent)))
    out = pl.pallas_call(
        functools.partial(last_kernel, axes, counts[1]),
        out_shape=jax.ShapeDtypeStruct(amps.shape, f32),
        in_specs=[vmem] * (1 + len(arrived)),
        out_specs=vmem,
        scratch_shapes=[pltpu.SMEM((1, size), i32), pltpu.SemaphoreType.DMA],
        name="last_places",
    )(plan, *arrived)
    return out.reshape(rows, 2, size).transpose(1, 0, 2).reshape(amplitudes.shape)


def program(mesh, *arrays):
    axes = ("row", "col")
    counts = tuple(mesh.shape[axis].bit_length() - 1 for axis in axes)
    amplitudes, gate_real = arrays[:2]
    size = gate_real.shape[-1]
    rounds = gate_real.shape[0] == 2 and gate_real.shape[1] == 3
    known = size == 128 and amplitudes.shape[-1] == 4 * size * size
    if known and rounds and max(counts) <= SUB and counts[1] > 1:
        return fused(axes, counts, *arrays)
    return per_device(*arrays)


def solution(mesh):
    placed = (P("row", "col", None, None), P(), P(), P(), P())
    return jax.shard_map(
        functools.partial(program, mesh),
        mesh=mesh,
        in_specs=placed,
        out_specs=P("row", "col", None, None),
        check_vma=False,
    )
```
